32 devices in a mesh: dev: 32 (over z, y, x, core).
Axes of the slice: x: 2, y: 2, z: 4, core: 2. Of those that a mesh axis runs over, the one named last changes fastest.
Arguments:
- tokens_in: float32 [32768, 1024], P('dev'), may hold values from -6 to 6
- attn_gain: float32 [1024], P('dev'), may hold values from 0.25 to 1.75
- attn_bias: float32 [1024], P('dev'), may hold values from -3 to 3
- query_mat: float32 [1024, 1024], P('dev'), may hold values from -0.1875 to 0.1875
- query_bias: float32 [1024], P('dev'), may hold values from -3 to 3
- key_mat: float32 [1024, 1024], P('dev'), may hold values from -0.1875 to 0.1875
- value_mat: float32 [1024, 1024], P('dev'), may hold values from -0.1875 to 0.1875
- value_bias: float32 [1024], P('dev'), may hold values from -3 to 3
- output_mat: float32 [1024, 1024], P('dev'), may hold values from -4 to 4
- output_bias: float32 [1024], P('dev'), may hold values from -3 to 3
- mlp_gain: float32 [1024], P('dev'), may hold values from 0.25 to 1.75
- mlp_bias: float32 [1024], P('dev'), may hold values from -3 to 3
- expand_mat: float32 [1024, 4096], P('dev'), may hold values from -0.1875 to 0.1875
- expand_bias: float32 [4096], P('dev'), may hold values from -3 to 3
- reduce_mat: float32 [4096, 1024], P('dev'), may hold values from -0.09375 to 0.09375
- reduce_bias: float32 [1024], P('dev'), may hold values from -3 to 3
- image_ids: int32 [32768], P('dev'), may hold values from 0 to 74, never falling along the last dimension, each value on 1 to 577 neighbouring positions
- clip_flags: int32 [16], replicated, may hold values 0 or 1
- out_grad: float32 [32768, 1024], P('dev'), may hold values from -6 to 6
Outputs:
- block_out: float32 [32768, 1024], P('dev')
- tokens_grad: float32 [32768, 1024], P('dev')
- query_clipped: float32 [1024, 1024], P('dev')
- key_clipped: float32 [1024, 1024], P('dev')
- attn_gain_grad: float32 [1024], P('dev')
- attn_bias_grad: float32 [1024], P('dev')
- query_mat_grad: float32 [1024, 1024], P('dev')
- query_bias_grad: float32 [1024], P('dev')
- key_mat_grad: float32 [1024, 1024], P('dev')
- value_mat_grad: float32 [1024, 1024], P('dev')
- value_bias_grad: float32 [1024], P('dev')
- output_mat_grad: float32 [1024, 1024], P('dev')
- output_bias_grad: float32 [1024], P('dev')
- mlp_gain_grad: float32 [1024], P('dev')
- mlp_bias_grad: float32 [1024], P('dev')
- expand_mat_grad: float32 [1024, 4096], P('dev')
- expand_bias_grad: float32 [4096], P('dev')
- reduce_mat_grad: float32 [4096, 1024], P('dev')
- reduce_bias_grad: float32 [1024], P('dev')
The draws below stay inside these ranges and needn't reach their ends.
Inputs may be any that keep to these rules, and one draw needn't show every extreme that they name: `image_ids`: image numbers never fall along the tokens; every number occurs; each image has 1 to 577 tokens, and some image has exactly 577.
All inputs are finite; a program needn't handle non-finite values.
Results may differ from the reference program's by a relative error of at most 0.012.
The reference program's roundings to bfloat16 on the way count: a program that leaves them out, or rounds other values in their place, can miss the bound.
Values may be sent and summed in bfloat16 or wider, within the bound.
No kernel may reach another device: no remote copies, remote signals or barrier semaphores. Data moves between devices by JAX's collectives and lax.ppermute only.
A program may use at most 448 MiB of HBM per device.

```python
import math
from functools import partial
import jax
import jax.numpy as jnp
import numpy as np
from jax import lax

D = 1024
H = 16
HD = 64
FF = 4096
LEN = 577
QB = 512
TOKENS = 32768
IMAGES = 75


def touch_ends(array, own_key, low, top_value):
    extent = array.shape
    place = [jax.random.randint(jax.random.fold_in(own_key, axis), (), 0, extent[axis]) for axis in range(len(extent))]
    array = array.at[tuple(place)].set(low)
    longest = extent.index(max(extent))
    place[longest] = (place[longest] + 1) % extent[longest]
    return array.at[tuple(place)].set(top_value)


def block_scale(rng, shape, split, smallest, top_value):
    def one(dim, parts):
        steps = jax.random.uniform(jax.random.fold_in(jax.random.fold_in(rng, 6), dim), (parts,), jnp.float32, smallest / len(split), top_value / len(split))
        return jnp.repeat(jnp.exp(steps), shape[dim] // parts).reshape((-1,) + (1,) * (len(shape) - dim - 1))

    level = one(*split[0])
    for cut in split[1:]:
        level = level * one(*cut)
    return level


def profile(count, total, limit, lean):
    portions = [(1 << 20) // math.isqrt(rank ** lean) + 1 for rank in range(2, count + 1)]
    rest, counts = total - limit - (count - 1), [1] * (count - 1)
    while rest > 0:
        free = [i for i in range(count - 1) if counts[i] < limit]
        whole, remaining = sum([portions[i] for i in free]), rest
        for i in free:
            extra = min(limit - counts[i], max(1, remaining * portions[i] // whole), rest)
            counts[i] = counts[i] + extra
            rest = rest - extra
    return np.array([limit] + counts)


def ragged(rng, number_of, total, reach, skew):
    if number_of == 2:
        one = jax.random.randint(rng, (), max(1, total - reach), min(reach, total - 1) + 1)
        return jnp.stack([one, total - one])
    sizes = jnp.asarray(profile(number_of, total, reach, skew), jnp.int32)
    couples = (number_of - 1) // 2
    giver, taker = sizes[1:1 + 2 * couples:2], sizes[2:2 + 2 * couples:2]
    margin = jnp.minimum(giver - 1, reach - taker)
    passed = jax.random.randint(jax.random.fold_in(rng, 1), (couples,), 0, 1 << 20) % (margin + 1)
    sizes = sizes.at[1:1 + 2 * couples:2].set(giver - passed).at[2:2 + 2 * couples:2].set(taker + passed)
    return sizes[jax.random.permutation(jax.random.fold_in(rng, 2), number_of)]


def noise(stream_key, extent, deviation, bound, shards=(), kind=jnp.bfloat16):
    result = deviation * jax.random.normal(stream_key, extent, jnp.float32)
    if shards:
        result = result * block_scale(stream_key, extent, shards, -0.22, 0.18)
    return jnp.clip(result, -bound, bound).astype(kind)


def setup_inputs(seed: int = 0) -> dict:
    key_list = jax.random.split(jax.random.key(seed), 20)
    return {
        "tokens_in": noise(key_list[0], (TOKENS, D), 1.0, 6.0, ((0, 32),), jnp.float32),
        "attn_gain": jnp.clip(1.0 + 0.15 * jax.random.normal(key_list[1], (D,), jnp.float32), 0.25, 1.75),
        "attn_bias": noise(key_list[2], (D,), 0.5, 3.0, ((0, 32),), jnp.float32),
        "query_mat": noise(key_list[3], (D, D), D ** -0.5, 0.1875, ((0, 32),), jnp.float32),
        "query_bias": noise(key_list[4], (D,), 0.5, 3.0, ((0, 32),), jnp.float32),
        "key_mat": noise(key_list[5], (D, D), D ** -0.5, 0.1875, ((0, 32),), jnp.float32),
        "value_mat": noise(key_list[6], (D, D), D ** -0.5, 0.1875, ((0, 32),), jnp.float32),
        "value_bias": noise(key_list[7], (D,), 0.5, 3.0, ((0, 32),), jnp.float32),
        "output_mat": noise(key_list[8], (D, D), (max(1, 4 * D // (3 * LEN))) ** -0.5, 4.0, ((0, 32),), jnp.float32),
        "output_bias": noise(key_list[9], (D,), 0.5, 3.0, ((0, 32),), jnp.float32),
        "mlp_gain": jnp.clip(1.0 + 0.15 * jax.random.normal(key_list[10], (D,), jnp.float32), 0.25, 1.75),
        "mlp_bias": noise(key_list[11], (D,), 0.5, 3.0, ((0, 32),), jnp.float32),
        "expand_mat": noise(key_list[12], (D, FF), D ** -0.5, 0.1875, ((0, 32),), jnp.float32),
        "expand_bias": noise(key_list[13], (FF,), 0.5, 3.0, ((0, 32),), jnp.float32),
        "reduce_mat": noise(key_list[14], (FF, D), FF ** -0.5, 0.09375, ((0, 32),), jnp.float32),
        "reduce_bias": noise(key_list[15], (D,), 0.5, 3.0, ((0, 32),), jnp.float32),
        "image_ids": jnp.searchsorted(jnp.cumsum(ragged(key_list[16], IMAGES, TOKENS, LEN, 0)), jnp.arange(TOKENS), side="right").astype(jnp.int32),
        "clip_flags": touch_ends((jax.random.randint(key_list[17], (H,), 0, 2) < 1).astype(jnp.int32), jax.random.fold_in(key_list[17], 1), 0, 1),
        "out_grad": noise(key_list[18], (TOKENS, D), 1.0, 6.0, ((0, 32),), jnp.float32),
    }


NORM_EPS = 1e-05
CLIP_TAU = 3.0
GELU_COEF = 1.702
NEG_FILL = -1e+30

@jax.custom_vjp
def low(v):
    return lax.optimization_barrier(v.astype(jnp.bfloat16)).astype(jnp.float32)

@jax.custom_vjp
def low_back(v):
    return v

def low_keep(v):
    return (low(v), None)

def low_pass(kept, grad):
    return (grad,)

def back_keep(v):
    return (v, None)

def back_low(kept, grad):
    return (low(grad),)
low.defvjp(low_keep, low_pass)
low_back.defvjp(back_keep, back_low)

def precise_dot(lhs_mat, rhs_mat):
    return jnp.dot(lhs_mat, rhs_mat, precision=lax.Precision.HIGHEST, preferred_element_type=jnp.float32)

def layer_norm(values, gain, shift):
    centre = values - lax.optimization_barrier(jnp.mean(values, axis=1, keepdims=True))
    spread = lax.optimization_barrier(jnp.mean(centre * centre, axis=1, keepdims=True))
    return centre * lax.rsqrt(spread + NORM_EPS) * low(gain) + low(shift)

def forward(tokens_in, attn_gain, attn_bias, query_mat, query_bias, key_mat, value_mat, value_bias, output_mat, output_bias, mlp_gain, mlp_bias, expand_mat, expand_bias, reduce_mat, reduce_bias, image_ids=None):
    normed = low(layer_norm(tokens_in, attn_gain, attn_bias))
    queries = low_back(low(precise_dot(normed, low(query_mat)) + low(query_bias)))
    keys = low_back(low(precise_dot(normed, low(key_mat))))
    values = low_back(low(precise_dot(normed, low(value_mat)) + low(value_bias)))
    rim_rows = LEN - 1
    key_window = QB + 2 * rim_rows
    padded_keys = jnp.pad(keys, ((rim_rows, rim_rows), (0, 0)))
    padded_values = jnp.pad(values, ((rim_rows, rim_rows), (0, 0)))
    shifted_ids = (image_ids + 1).astype(jnp.int32)
    padded_ids = jnp.pad(shifted_ids, (rim_rows, rim_rows))
    score_scale = HD ** (-0.5)

    def attend(block_no):
        start = (block_no * QB).astype(jnp.int32)
        query_rows = lax.dynamic_slice_in_dim(queries, start, QB, 0).reshape(QB, H, HD)
        key_rows = lax.dynamic_slice_in_dim(padded_keys, start, key_window, 0).reshape(key_window, H, HD)
        value_rows = lax.dynamic_slice_in_dim(padded_values, start, key_window, 0).reshape(key_window, H, HD)
        own_ids = lax.dynamic_slice_in_dim(shifted_ids, start, QB, 0)
        near_ids = lax.dynamic_slice_in_dim(padded_ids, start, key_window, 0)
        allowed = (own_ids[:, None] == near_ids[None, :])[None]
        scores = low_back(jnp.einsum('qhd,khd->hqk', query_rows, key_rows, precision=lax.Precision.HIGHEST) * score_scale)
        masked = jnp.where(allowed, scores, NEG_FILL)
        row_top = lax.optimization_barrier(jnp.max(masked, axis=2, keepdims=True))
        weights = jnp.where(allowed, jnp.exp(masked - row_top), 0.0)
        prob_rows = low(weights / lax.optimization_barrier(jnp.sum(weights, axis=2, keepdims=True)))
        attn_mixed = jnp.einsum('hqk,khd->qhd', prob_rows, value_rows, precision=lax.Precision.HIGHEST)
        return (attn_mixed.reshape(QB, D), lax.optimization_barrier(jnp.max(row_top[:, :, 0], axis=1)))
    attn_mixed, block_top = lax.map(jax.checkpoint(attend), jnp.arange(TOKENS // QB, dtype=jnp.int32))
    mixed_low = low_back(low(attn_mixed.reshape(TOKENS, D)))
    attn_out = low_back(precise_dot(mixed_low, low(output_mat)) + low(output_bias))
    middle = tokens_in + attn_out
    normed_two = low(layer_norm(middle, mlp_gain, mlp_bias))
    hidden = low_back(precise_dot(normed_two, low(expand_mat)) + low(expand_bias))
    active = low(hidden * jax.nn.sigmoid(GELU_COEF * hidden))
    branch = low_back(precise_dot(active, low(reduce_mat)) + low(reduce_bias))
    return (middle + branch, lax.optimization_barrier(jnp.max(block_top, axis=0)))

def reference(tokens_in, attn_gain, attn_bias, query_mat, query_bias, key_mat, value_mat, value_bias, output_mat, output_bias, mlp_gain, mlp_bias, expand_mat, expand_bias, reduce_mat, reduce_bias, image_ids, clip_flags, out_grad):
    block_fn = partial(forward, image_ids=image_ids)
    block_out, pullback, head_top = jax.vjp(block_fn, tokens_in, attn_gain, attn_bias, query_mat, query_bias, key_mat, value_mat, value_bias, output_mat, output_bias, mlp_gain, mlp_bias, expand_mat, expand_bias, reduce_mat, reduce_bias, has_aux=True)
    grads = pullback(out_grad)
    ratio = CLIP_TAU / jnp.maximum(head_top, CLIP_TAU)
    factor = jnp.where(clip_flags == 1, jnp.sqrt(ratio), 1.0)
    columns = jnp.repeat(factor, HD)
    return (block_out, grads[0], query_mat * columns[None, :], key_mat * columns[None, :], grads[1], grads[2], grads[3], grads[4], grads[5], grads[6], grads[7], grads[8], grads[9], grads[10], grads[11], grads[12], grads[13], grads[14], grads[15])
```

```python
import functools

import jax
import jax.numpy as jnp
from jax import lax
from jax.experimental import pallas as pl
from jax.experimental.pallas import tpu as pltpu
from jax.sharding import PartitionSpec as P

H = 16
HD = 64
LEN = 577
RIM = LEN - 1
PAIR = 2 * HD
QB = 256
KB = 256

NORM_EPS = 1e-05
CLIP_TAU = 3.0
GELU_COEF = 1.702
NEG_FILL = -1e30
SCALE = HD ** (-0.5)

bf16 = jnp.bfloat16
f32 = jnp.float32
NN = (((1,), (0,)), ((), ()))
NT = (((1,), (1,)), ((), ()))
TN = (((0,), (0,)), ((), ()))


def dot(lhs, rhs, dims):
    return lax.dot_general(lhs, rhs, dims, preferred_element_type=f32)


def norm_stats(values):
    centre = values - jnp.mean(values, axis=1, keepdims=True)
    inv_std = lax.rsqrt(jnp.mean(centre * centre, axis=1, keepdims=True) + NORM_EPS)
    return centre * inv_std, inv_std


def norm_back(grad_out, gain, normal, inv_std):
    scaled = grad_out * gain
    return inv_std * (
        scaled
        - jnp.mean(scaled, axis=1, keepdims=True)
        - normal * jnp.mean(scaled * normal, axis=1, keepdims=True)
    )


def column_sums(values):
    return jnp.sum(values.astype(f32), axis=0)


def two_heads(block):
    lane = lax.broadcasted_iota(jnp.int32, block.shape, 1)
    zero = jnp.zeros_like(block)
    return jnp.concatenate(
        [jnp.where(lane < HD, block, zero), jnp.where(lane >= HD, block, zero)], axis=0
    )


def fill_bias(bias_ref, key_ids_ref, query_ids_ref, block, low, count):
    def one(c, carry):
        start = pl.multiple_of(low + c * KB, 128)
        keys = key_ids_ref[pl.ds(start, KB), :]
        same = keys == query_ids_ref[...]
        bias_ref[block, pl.ds(pl.multiple_of(c * KB, KB), KB), :] = jnp.where(same, 0.0, NEG_FILL)
        return carry

    lax.fori_loop(0, count, one, 0)


def attend_kernel(
    low_ref, count_ref, key_ids_ref, query_ids_ref, q_ref, k_ref, v_ref, o_ref, wide_ref, lse_ref, top_ref, bias_ref
):
    pair, block = pl.program_id(0), pl.program_id(1)
    low, count = low_ref[block], count_ref[block]

    @pl.when(pair == 0)
    def _():
        fill_bias(bias_ref, key_ids_ref, query_ids_ref, block, low, count)

    queries = two_heads(q_ref[...])
    width = queries.shape[0]

    def step(c, carry):
        top, total, acc = carry
        start = pl.multiple_of(low + c * KB, 128)
        bias = bias_ref[block, pl.ds(pl.multiple_of(c * KB, KB), KB), :]
        scores = dot(k_ref[pl.ds(start, KB), :], queries, NT) * SCALE
        scores = scores + jnp.concatenate([bias, bias], axis=1)
        new_top = jnp.maximum(top, jnp.max(scores, axis=0, keepdims=True))
        weights = jnp.exp(scores - new_top)
        fade = jnp.exp(top - new_top)
        total = total * fade + jnp.sum(weights, axis=0, keepdims=True)
        acc = acc * fade + dot(v_ref[pl.ds(start, KB), :], weights.astype(bf16), TN)
        return new_top, total, acc

    start_top = jnp.full((1, width), NEG_FILL, f32)
    top, total, acc = lax.fori_loop(
        0, count, step, (start_top, jnp.zeros((1, width), f32), jnp.zeros((PAIR, width), f32))
    )
    mixed = acc / total
    half = width // 2
    joined = jnp.concatenate([mixed[:HD, :half], mixed[HD:, half:]], axis=0)
    joined = joined.T
    wide_ref[...] = joined
    o_ref[...] = joined.astype(bf16)
    lse_ref[0] = top + jnp.log(total)

    @pl.when(block == 0)
    def _():
        top_ref[0] = top

    @pl.when(block != 0)
    def _():
        top_ref[0] = jnp.maximum(top_ref[0], top)


def attend_back_kernel(
    low_ref,
    count_ref,
    key_ids_ref,
    query_ids_ref,
    q_ref,
    k_ref,
    v_ref,
    do_ref,
    o_ref,
    lse_ref,
    dq_ref,
    dk_ref,
    dv_ref,
    bias_ref,
    dk_acc,
    dv_acc,
):
    pair, block = pl.program_id(0), pl.program_id(1)
    low, count = low_ref[block], count_ref[block]

    @pl.when(pair == 0)
    def _():
        fill_bias(bias_ref, key_ids_ref, query_ids_ref, block, low, count)

    @pl.when(block == 0)
    def _():
        dk_acc[...] = jnp.zeros_like(dk_acc)
        dv_acc[...] = jnp.zeros_like(dv_acc)

    queries = two_heads(q_ref[...])
    grads = two_heads(do_ref[...])
    mixed = jnp.concatenate([o_ref[...], o_ref[...]], axis=0)
    inner = lax.dot_general(
        jnp.ones((8, PAIR), f32),
        grads.astype(f32) * mixed,
        NT,
        precision=lax.Precision.HIGHEST,
        preferred_element_type=f32,
    )[0:1]
    log_sum = lse_ref[0]
    width = queries.shape[0]

    def step(c, acc):
        start = pl.multiple_of(low + c * KB, 128)
        keys = k_ref[pl.ds(start, KB), :]
        bias = bias_ref[block, pl.ds(pl.multiple_of(c * KB, KB), KB), :]
        scores = dot(keys, queries, NT) * SCALE + jnp.concatenate([bias, bias], axis=1)
        probs = jnp.exp(scores - log_sum)
        prob_grad = dot(v_ref[pl.ds(start, KB), :], grads, NT)
        score_grad = (probs * (prob_grad - inner)).astype(bf16)
        dv_acc[pl.ds(start, KB), :] += dot(probs.astype(bf16), grads, NN)
        dk_acc[pl.ds(start, KB), :] += dot(score_grad, queries, NN)
        return acc + dot(keys, score_grad, TN)

    acc = lax.fori_loop(0, count, step, jnp.zeros((PAIR, width), f32))
    half = width // 2
    joined = jnp.concatenate([acc[:HD, :half], acc[HD:, half:]], axis=0) * SCALE
    dq_ref[...] = joined.T.astype(bf16)

    @pl.when(block == pl.num_programs(1) - 1)
    def _():
        dk_ref[...] = (dk_acc[...] * SCALE).astype(bf16)
        dv_ref[...] = dv_acc[...].astype(bf16)


def key_ranges(own_ids, near_ids, blocks):
    rows, near = own_ids.shape[0], near_ids.shape[0]
    size = rows // blocks
    place = jnp.arange(near, dtype=jnp.int32)[None, :]
    first = own_ids[0::size][:, None]
    last = own_ids[size - 1 :: size][:, None]
    low = jnp.min(jnp.where(near_ids[None, :] == first, place, near), axis=1)
    high = jnp.max(jnp.where(near_ids[None, :] == last, place, -1), axis=1) + 1
    low = low // 128 * 128
    count = (high - low + KB - 1) // KB
    low = jnp.minimum(low, near - count * KB)
    return low.astype(jnp.int32), count.astype(jnp.int32)


def attention_specs(rows, near, blocks):
    pairs = H // 2
    most = -(-(QB + 2 * RIM + 127) // KB) * KB
    assert most <= near and rows % QB == 0 and near % 128 == 0
    own = pl.BlockSpec((QB, PAIR), lambda p, b, *_: (b, p))
    base = [
        pl.BlockSpec((near, 1), lambda p, b, *_: (0, 0)),
        pl.BlockSpec((1, QB), lambda p, b, *_: (0, b)),
        own,
        pl.BlockSpec((near, PAIR), lambda p, b, *_: (0, p)),
        pl.BlockSpec((near, PAIR), lambda p, b, *_: (0, p + pairs)),
    ]
    row = pl.BlockSpec((1, 1, 2 * QB), lambda p, b, *_: (p, 0, b))
    bias = pltpu.VMEM((blocks, most, QB), f32)
    return pairs, own, base, row, bias


def attend(ranges, key_ids, query_ids, queries, near_kv):
    rows, near = queries.shape[0], near_kv.shape[0]
    blocks = rows // QB
    pairs, own, base, row, bias = attention_specs(rows, near, blocks)
    top = pl.BlockSpec((1, 1, 2 * QB), lambda p, b, *_: (p, 0, 0))
    return pl.pallas_call(
        attend_kernel,
        grid_spec=pltpu.PrefetchScalarGridSpec(
            num_scalar_prefetch=2,
            grid=(pairs, blocks),
            in_specs=base,
            out_specs=[own, own, row, top],
            scratch_shapes=[bias],
        ),
        out_shape=[
            jax.ShapeDtypeStruct(queries.shape, bf16),
            jax.ShapeDtypeStruct(queries.shape, f32),
            jax.ShapeDtypeStruct((pairs, 1, 2 * rows), f32),
            jax.ShapeDtypeStruct((pairs, 1, 2 * QB), f32),
        ],
        compiler_params=pltpu.CompilerParams(vmem_limit_bytes=56 << 20),
        name="attend",
    )(*ranges, key_ids, query_ids, queries, near_kv, near_kv)


def attend_back(ranges, key_ids, query_ids, queries, near_kv, mixed_grad, mixed, log_sums):
    rows, near = queries.shape[0], near_kv.shape[0]
    blocks = rows // QB
    pairs, own, base, row, bias = attention_specs(rows, near, blocks)
    wide = pl.BlockSpec((near, PAIR), lambda p, b, *_: (0, p))
    return pl.pallas_call(
        attend_back_kernel,
        grid_spec=pltpu.PrefetchScalarGridSpec(
            num_scalar_prefetch=2,
            grid=(pairs, blocks),
            in_specs=base + [own, own, row],
            out_specs=[own, wide, wide],
            scratch_shapes=[bias, pltpu.VMEM((near, PAIR), f32), pltpu.VMEM((near, PAIR), f32)],
        ),
        out_shape=[
            jax.ShapeDtypeStruct(queries.shape, bf16),
            jax.ShapeDtypeStruct((near, queries.shape[1]), bf16),
            jax.ShapeDtypeStruct((near, queries.shape[1]), bf16),
        ],
        compiler_params=pltpu.CompilerParams(vmem_limit_bytes=56 << 20),
        name="attend_back",
    )(*ranges, key_ids, query_ids, queries, near_kv, near_kv, mixed_grad, mixed, log_sums)


def mlp_kernel(
    a_ref, dz_ref, x_ref, rb_ref, eb_ref, we_ref, wr_ref,
    y_ref, da_ref, ebg_ref, sum_ref,
    act_ref, du_ref, rg_ref, eg_ref, sems,
):
    j = pl.program_id(0)
    rows, width = a_ref.shape
    tile = 256

    def copies(step):
        d, r, _ = rg_ref.shape
        g, e, _ = eg_ref.shape
        fold = pl.num_programs(0)
        return (
            pltpu.make_async_copy(rg_ref, sum_ref.at[pl.ds(step * d, d), pl.ds(0, r), :], sems.at[0]),
            pltpu.make_async_copy(eg_ref, sum_ref.at[:, pl.ds(r + step * e, e), :], sems.at[1]),
        )

    @pl.when(j == 0)
    def _():
        y_ref[...] = x_ref[...] + rb_ref[...]
        da_ref[...] = jnp.zeros_like(da_ref)

    ebg_ref[...] = jnp.zeros_like(ebg_ref)

    def by_rows(r, carry):
        at = pl.ds(pl.multiple_of(r * tile, tile), tile)
        we = we_ref[...].reshape(width, width)
        wr = wr_ref[...].reshape(width, width)
        hidden = dot(a_ref[at, :], we, NN) + eb_ref[...]
        back = dot(dz_ref[at, :], wr, NT)
        sigma = jax.nn.sigmoid(GELU_COEF * hidden)
        act = (hidden * sigma).astype(bf16)
        act_ref[at, :] = act
        du = (back * (sigma + GELU_COEF * hidden * sigma * (1.0 - sigma))).astype(bf16)
        du_ref[at, :] = du
        ebg_ref[...] += jnp.sum(du.astype(f32), axis=0, keepdims=True)
        y_ref[at, :] += dot(act, wr, NN)
        da_ref[at, :] += dot(du, we, NT)
        return carry

    lax.fori_loop(0, rows // tile, by_rows, 0)

    @pl.when(j > 0)
    def _():
        for copy in copies(j - 1):
            copy.wait()

    def by_columns(t, carry):
        at = pl.ds(pl.multiple_of(t * tile, tile), tile)
        rg = dot(act_ref[:, at], dz_ref[...], TN).astype(bf16)
        n = tile // rg_ref.shape[1]
        rg_ref[pl.ds(t * n, n)] = rg.reshape(n, rg_ref.shape[1], width)
        eg = dot(a_ref[:, at], du_ref[...], TN).astype(bf16)
        n = tile // eg_ref.shape[1]
        eg_ref[pl.ds(t * n, n)] = eg.reshape(n, eg_ref.shape[1], width)
        return carry

    lax.fori_loop(0, width // tile, by_columns, 0)
    for copy in copies(j):
        copy.start()

    @pl.when(j == pl.num_programs(0) - 1)
    def _():
        for copy in copies(j):
            copy.wait()


def mlp(normed, branch_grad, middle, bias_reduce, bias_expand, packed, sum_rows):
    rows, width = normed.shape
    ff = bias_expand.shape[1]
    fold = ff // width
    groups = packed.shape[0]
    each = width // groups
    whole = lambda j: (0, 0)
    one = pl.Buffered(1)
    return pl.pallas_call(
        mlp_kernel,
        grid=(fold,),
        in_specs=[
            pl.BlockSpec((rows, width), whole, pipeline_mode=one),
            pl.BlockSpec((rows, width), whole, pipeline_mode=one),
            pl.BlockSpec((rows, width), whole, pipeline_mode=one),
            pl.BlockSpec((1, width), whole),
            pl.BlockSpec((1, width), lambda j: (0, j)),
            pl.BlockSpec((groups, each, width), lambda j: (0, fold + j, 0)),
            pl.BlockSpec((groups // fold, fold * each, width), lambda j: (j, 0, 0)),
        ],
        out_specs=[
            pl.BlockSpec((rows, width), whole),
            pl.BlockSpec((rows, width), whole),
            pl.BlockSpec((1, width), lambda j: (0, j)),
            pl.BlockSpec(memory_space=pl.ANY),
        ],
        out_shape=[
            jax.ShapeDtypeStruct((rows, width), f32),
            jax.ShapeDtypeStruct((rows, width), f32),
            jax.ShapeDtypeStruct((1, ff), f32),
            jax.ShapeDtypeStruct((groups, sum_rows, width), bf16),
        ],
        scratch_shapes=[
            pltpu.VMEM((rows, width), bf16),
            pltpu.VMEM((rows, width), bf16),
            pltpu.VMEM((groups // fold, fold * each, width), bf16),
            pltpu.VMEM((groups, each, width), bf16),
            pltpu.SemaphoreType.DMA((2,)),
        ],
        compiler_params=pltpu.CompilerParams(vmem_limit_bytes=58 << 20),
        name="mlp",
    )(normed, branch_grad, middle, bias_reduce, bias_expand, packed, packed)


def out_back_kernel(ag_ref, mixed_ref, wo_ref, sum_in_ref, mg_ref, sum_ref, og_ref, sem):
    rows, width = ag_ref.shape
    tile = 256
    groups, each, _ = og_ref.shape

    def by_columns(t, carry):
        at = pl.ds(pl.multiple_of(t * tile, tile), tile)
        og = dot(mixed_ref[:, at], ag_ref[...], TN).astype(bf16)
        n = tile // each
        og_ref[pl.ds(t * n, n)] = og.reshape(n, each, width)
        return carry

    lax.fori_loop(0, width // tile, by_columns, 0)
    copy = pltpu.make_async_copy(og_ref, sum_ref.at[:, pl.ds(sum_ref.shape[1] - each, each), :], sem)
    copy.start()

    def by_rows(t, carry):
        at = pl.ds(pl.multiple_of(t * tile, tile), tile)
        mg_ref[at, :] = dot(ag_ref[at, :], wo_ref[...].reshape(width, width), NT).astype(bf16)
        return carry

    lax.fori_loop(0, rows // tile, by_rows, 0)
    copy.wait()


def out_back(attn_grad, mixed, packed, sums):
    rows, width = attn_grad.shape
    groups = packed.shape[0]
    each = width // groups
    last = sums.shape[1] // each - 1
    whole = lambda i: (0, 0)
    return pl.pallas_call(
        out_back_kernel,
        grid=(1,),
        in_specs=[
            pl.BlockSpec((rows, width), whole),
            pl.BlockSpec((rows, width), whole),
            pl.BlockSpec((groups, each, width), lambda i: (0, last, 0)),
            pl.BlockSpec(memory_space=pl.ANY),
        ],
        out_specs=[pl.BlockSpec((rows, width), whole), pl.BlockSpec(memory_space=pl.ANY)],
        out_shape=[
            jax.ShapeDtypeStruct((rows, width), bf16),
            jax.ShapeDtypeStruct(sums.shape, bf16),
        ],
        scratch_shapes=[pltpu.VMEM((groups, each, width), bf16), pltpu.SemaphoreType.DMA(())],
        input_output_aliases={3: 1},
        compiler_params=pltpu.CompilerParams(vmem_limit_bytes=56 << 20),
        name="out_back",
    )(attn_grad, mixed, packed, sums)


def qkv_kernel(a_ref, w_ref, bias_ref, q_ref, kv_ref):
    j = pl.program_id(0)
    near, width = a_ref.shape
    rows = q_ref.shape[0]
    rim = (near - rows) // 2

    @pl.when(j == 0)
    def _():
        def step(t, carry):
            source = pl.ds(pl.multiple_of(rim + t * 256, 8), 256)
            w = w_ref[...].reshape(width, width)
            q_ref[pl.ds(pl.multiple_of(t * 256, 256), 256), :] = (
                dot(a_ref[source, :], w, NN) + bias_ref[...]
            ).astype(bf16)
            return carry

        lax.fori_loop(0, rows // 256, step, 0)

    @pl.when(j > 0)
    def _():
        size = near // 8

        def step(t, carry):
            at = pl.ds(pl.multiple_of(t * size, 16), size)
            w = w_ref[...].reshape(width, width)
            kv_ref[at, :] = (dot(a_ref[at, :], w, NN) + bias_ref[...]).astype(bf16)
            return carry

        lax.fori_loop(0, near // size, step, 0)


def project(normed_near, packed, biases, rows):
    near, width = normed_near.shape
    groups = packed.shape[0]
    each = width // groups
    return pl.pallas_call(
        qkv_kernel,
        grid=(3,),
        in_specs=[
            pl.BlockSpec((near, width), lambda j: (0, 0)),
            pl.BlockSpec((groups, each, width), lambda j: (0, j, 0)),
            pl.BlockSpec((1, width), lambda j: (0, j)),
        ],
        out_specs=[
            pl.BlockSpec((rows, width), lambda j: (0, 0)),
            pl.BlockSpec((near, width), lambda j: (0, jnp.maximum(j - 1, 0))),
        ],
        out_shape=[
            jax.ShapeDtypeStruct((rows, width), bf16),
            jax.ShapeDtypeStruct((near, 2 * width), bf16),
        ],
        compiler_params=pltpu.CompilerParams(vmem_limit_bytes=56 << 20),
        name="qkv",
    )(normed_near, packed, biases)


def qkv_grads_kernel(me_ref, a_ref, dq_ref, dk_ref, dv_ref, keep_ref, send_ref):
    j = pl.program_id(0)
    near, width = a_ref.shape
    rows = dq_ref.shape[0]
    rim = (near - rows) // 2
    tile = 256
    half, each, _ = keep_ref.shape
    n = tile // each

    def fill(grad_ref, source):
        def step(t, carry):
            at = pl.ds(pl.multiple_of(t * tile, tile), tile)
            out = dot(a_ref[source, at], grad_ref[...], TN).astype(bf16)
            for i in range(n):
                place = (t * n + i) ^ me_ref[0]
                spot, bit = 0, half
                while bit:
                    spot = spot + (place & 1) * bit
                    place, bit = place >> 1, bit >> 1
                block = out[i * each : (i + 1) * each]

                @pl.when(spot < half)
                def _():
                    keep_ref[spot] = block

                @pl.when(spot >= half)
                def _():
                    send_ref[spot - half] = block

            return carry

        lax.fori_loop(0, width // tile, step, 0)

    @pl.when(j == 0)
    def _():
        fill(dq_ref, slice(rim, rim + rows))

    @pl.when(j == 1)
    def _():
        fill(dk_ref, slice(0, near))

    @pl.when(j == 2)
    def _():
        fill(dv_ref, slice(0, near))


def qkv_grads(normed_near, query_grad, key_near, value_near, groups, place):
    near, width = normed_near.shape
    rows = query_grad.shape[0]
    each = width // groups
    whole = lambda j, *_: (0, 0)
    half = jax.ShapeDtypeStruct((groups // 2, 3 * each, width), bf16)
    out = pl.BlockSpec((groups // 2, each, width), lambda j, *_: (0, j, 0))
    return pl.pallas_call(
        qkv_grads_kernel,
        grid_spec=pltpu.PrefetchScalarGridSpec(
            num_scalar_prefetch=1,
            grid=(3,),
            in_specs=[
                pl.BlockSpec((near, width), whole),
                pl.BlockSpec((rows, width), whole),
                pl.BlockSpec((near, width), whole),
                pl.BlockSpec((near, width), whole),
            ],
            out_specs=[out, out],
        ),
        out_shape=[half, half],
        compiler_params=pltpu.CompilerParams(vmem_limit_bytes=56 << 20),
        name="qkv_grads",
    )(jnp.full((1,), place, jnp.int32), normed_near, query_grad, key_near, value_near)


def plus(a, b):
    return (a.astype(f32) + b.astype(f32)).astype(bf16)


def swap(value, bit):
    peers = lax.axis_size("dev")
    return lax.ppermute(value, "dev", [(i, i ^ bit) for i in range(peers)])


def halving(keep, send):
    _, rows, width = keep.shape
    half = rows // 2
    other = swap(send, 1).reshape(2, 2, 4, rows, width)
    keep = keep.reshape(2, 2, 4, rows, width)
    a, b = slice(0, half), slice(half, rows)
    from_x = swap(plus(keep[1, :, :, a], other[1, :, :, a]), 2)
    from_y = swap(plus(keep[:, 1, :, b], other[:, 1, :, b]), 4)
    keep_x = plus(keep[0, :, :, a], other[0, :, :, a])
    keep_y = plus(keep[:, 0, :, b], other[:, 0, :, b])
    second_y = swap(plus(keep_x[1], from_x[1]), 4)
    second_x = swap(plus(keep_y[1], from_y[1]), 2)
    keep_x = plus(keep_x[0], from_x[0])
    keep_y = plus(keep_y[0], from_y[0])
    send = jnp.concatenate([plus(keep_x[2:], second_y[2:]), plus(keep_y[2:], second_x[2:])], axis=1)
    low = swap(send, 8)
    keep = jnp.concatenate([plus(keep_x[:2], second_y[:2]), plus(keep_y[:2], second_x[:2])], axis=1)
    last = swap(plus(keep[1], low[1]), 16)
    return plus(keep[0], low[0]).astype(f32) + last.astype(f32)


def normed_grad_kernel(dq_ref, dkv_ref, w_ref, out_ref):
    j = pl.program_id(0)
    rows, width = out_ref.shape

    def step(t, carry):
        at = pl.ds(pl.multiple_of(t * 256, 256), 256)
        w = w_ref[...].reshape(width, width)

        @pl.when(j == 0)
        def _():
            out_ref[at, :] = dot(dq_ref[at, :], w, NT)

        @pl.when(j > 0)
        def _():
            out_ref[at, :] += dot(dkv_ref[at, :], w, NT)

        return carry

    lax.fori_loop(0, rows // 256, step, 0)


def project_back(query_grad, kv_grad, packed):
    rows, width = query_grad.shape
    groups = packed.shape[0]
    each = width // groups
    return pl.pallas_call(
        normed_grad_kernel,
        grid=(3,),
        in_specs=[
            pl.BlockSpec((rows, width), lambda j: (0, 0)),
            pl.BlockSpec((rows, width), lambda j: (0, jnp.maximum(j - 1, 0))),
            pl.BlockSpec((groups, each, width), lambda j: (0, j, 0)),
        ],
        out_specs=pl.BlockSpec((rows, width), lambda j: (0, 0)),
        out_shape=jax.ShapeDtypeStruct((rows, width), f32),
        compiler_params=pltpu.CompilerParams(vmem_limit_bytes=56 << 20),
        name="normed_grad",
    )(query_grad, kv_grad, packed)


def gather(value, segments, groups):
    peers = lax.axis_size("dev")
    rows, width = value.shape
    whole = lax.all_gather(value, "dev", axis=0, tiled=True)
    sub = peers // groups
    if sub == 1:
        return whole.reshape(groups, rows, width)
    whole = whole.reshape(groups, sub, rows, width)
    parts, at = [], 0
    for size in segments:
        parts.append(whole[:, :, at : at + size].reshape(groups, sub * size, width))
        at += size
    return jnp.concatenate(parts, axis=1)


def scatter(value, segments):
    peers = lax.axis_size("dev")
    groups, rows, width = value.shape
    sub = peers // groups
    if sub > 1:
        parts, at = [], 0
        for size in segments:
            cut = value[:, at : at + sub * size]
            parts.append(cut.reshape(groups, sub, size, width))
            at += sub * size
        value = jnp.concatenate(parts, axis=2)
    value = value.reshape(peers * sum(segments), width)
    return lax.psum_scatter(value, "dev", scatter_dimension=0, tiled=True)


def spread(vector, width):
    peers, me = lax.axis_size("dev"), lax.axis_index("dev")
    size = vector.shape[0]
    place = jnp.arange(peers * size, dtype=jnp.int32) // size
    full = jnp.where(place == me, jnp.tile(vector, peers), jnp.zeros((), vector.dtype))
    return full.reshape(-1, width)


def local(
    tokens_in,
    attn_gain,
    attn_bias,
    query_mat,
    query_bias,
    key_mat,
    value_mat,
    value_bias,
    output_mat,
    output_bias,
    mlp_gain,
    mlp_bias,
    expand_mat,
    expand_bias,
    reduce_mat,
    reduce_bias,
    image_ids,
    clip_flags,
    out_grad,
):
    peers, me = lax.axis_size("dev"), lax.axis_index("dev")
    rows, width = tokens_in.shape
    part = query_mat.shape[0]
    ff = expand_mat.shape[1]
    fold = ff // width
    groups = min(peers, 32)
    sub = peers // groups

    small = jnp.concatenate(
        [
            spread(v.astype(bf16), width)
            for v in (
                attn_gain,
                attn_bias,
                query_bias,
                value_bias,
                output_bias,
                mlp_gain,
                mlp_bias,
                reduce_bias,
            )
        ]
    )
    packed_one = jnp.concatenate([query_mat.astype(bf16), key_mat.astype(bf16), value_mat.astype(bf16), small])
    first = gather(packed_one, [part] * 3 + [8], groups)

    up = [(i, i + 1) for i in range(peers - 1)]
    down = [(i + 1, i) for i in range(peers - 1)]
    normal_one, inv_one = norm_stats(tokens_in)
    normal_low = normal_one.astype(bf16)
    before = lax.ppermute(normal_low[rows - RIM :], "dev", up)
    after = lax.ppermute(normal_low[:RIM], "dev", down)
    own_ids = image_ids + 1
    ids_before = lax.ppermute(own_ids[rows - RIM :], "dev", up)
    ids_after = lax.ppermute(own_ids[:RIM], "dev", down)
    near_ids = jnp.concatenate([ids_before, own_ids, ids_after])
    ranges = key_ranges(own_ids, near_ids, rows // QB)
    key_ids, query_ids = near_ids[:, None], own_ids[None, :]

    expand_low = expand_mat.astype(bf16)
    second = jnp.concatenate(
        [reduce_mat.astype(bf16)]
        + [expand_low[:, i * width : (i + 1) * width] for i in range(fold)]
        + [output_mat.astype(bf16), spread(expand_bias.astype(bf16), width), jnp.zeros((8 - fold, width), bf16)]
    )
    second, before, after = lax.optimization_barrier((second, before, after))
    second = gather(second, [fold * part] + [part] * (fold + 1) + [8], groups)

    vectors = jnp.sum(first[:, groups * 0 + 3 * part * sub :].reshape(groups * sub, 8, width).astype(f32), axis=0)
    (gain_one, bias_one, bias_query, bias_value, bias_output, gain_two, bias_two, bias_reduce) = [
        vectors[i : i + 1] for i in range(8)
    ]

    normed_near = jnp.concatenate(
        [(v.astype(f32) * gain_one + bias_one).astype(bf16) for v in (before, normal_one, after)], axis=0
    )
    bias_qkv = jnp.concatenate([bias_query, jnp.zeros_like(bias_value), bias_value], axis=1)
    queries, near_kv = project(normed_near, first, bias_qkv, rows)
    mixed, mixed_wide, log_sums, tops = attend(ranges, key_ids, query_ids, queries, near_kv)
    head_top = jnp.max(tops.reshape(H, QB), axis=1)

    tail = second[:, (2 * fold + 1) * part * sub :].reshape(groups * sub, 8, width)
    bias_expand = jnp.sum(tail.astype(f32), axis=0)[:fold].reshape(1, ff)
    w_output = second[:, 2 * fold * part * sub : (2 * fold + 1) * part * sub].reshape(width, width)
    middle = tokens_in + dot(mixed, w_output, NN) + bias_output
    normal_two, inv_two = norm_stats(middle)
    normed_two = (normal_two * gain_two + bias_two).astype(bf16)
    branch_grad = out_grad.astype(bf16)
    block_out, normed_two_grad, expand_bias_grad, sums = mlp(
        normed_two, branch_grad, middle, bias_reduce, bias_expand, second, (2 * fold + 1) * width // groups
    )
    reduce_bias_grad = column_sums(branch_grad)
    mlp_gain_grad = jnp.sum(normed_two_grad * normal_two, axis=0)
    mlp_bias_grad = jnp.sum(normed_two_grad, axis=0)
    middle_grad = out_grad + norm_back(normed_two_grad, gain_two, normal_two, inv_two)
    attn_grad = middle_grad.astype(bf16)
    output_bias_grad = column_sums(attn_grad)
    mixed_grad, sums = out_back(attn_grad, mixed, second, sums)
    first_sum = scatter(sums, [fold * part] + [part] * (fold + 1))

    query_grad, key_near, value_near = attend_back(
        ranges, key_ids, query_ids, queries, near_kv, mixed_grad, mixed_wide, log_sums
    )
    halves = qkv_grads(normed_near, query_grad, key_near, value_near, groups, me if peers == 32 else 0)
    if peers == 32:
        second_sum = halving(*halves)
    else:
        order = [int(f"{i:05b}"[::-1], 2) for i in range(groups)]
        joined = jnp.concatenate(halves, axis=0)
        second_sum = scatter(jnp.stack([joined[i] for i in order]), [part] * 3)
    outgoing = jnp.concatenate([key_near, value_near], axis=1)
    from_next = lax.ppermute(outgoing[:RIM], "dev", down)
    from_prev = lax.ppermute(outgoing[RIM + rows :], "dev", up)
    own = outgoing[RIM : RIM + rows].astype(f32)
    own = own + jnp.pad(from_prev.astype(f32), ((0, rows - RIM), (0, 0)))
    own = own + jnp.pad(from_next.astype(f32), ((rows - RIM, 0), (0, 0)))
    kv_grad = own.astype(bf16)
    query_bias_grad = column_sums(query_grad)
    value_bias_grad = column_sums(value_near)
    normed_grad = project_back(query_grad, kv_grad, first)
    attn_gain_grad = jnp.sum(normed_grad * normal_one, axis=0)
    attn_bias_grad = jnp.sum(normed_grad, axis=0)
    tokens_grad = middle_grad + norm_back(normed_grad, gain_one, normal_one, inv_one)

    totals = jnp.stack(
        [
            attn_gain_grad,
            attn_bias_grad,
            query_bias_grad,
            value_bias_grad,
            output_bias_grad,
            mlp_gain_grad,
            mlp_bias_grad,
            reduce_bias_grad,
        ]
    )
    totals = jnp.concatenate(
        [totals, expand_bias_grad.reshape(fold, width), jnp.pad(head_top, (0, width - H))[None]]
    )
    is_top = jnp.arange(totals.shape[0])[:, None] == totals.shape[0] - 1
    bit = 1
    while bit < peers:
        other = lax.ppermute(totals, "dev", [(i, i ^ bit) for i in range(peers)])
        totals = jnp.where(is_top, jnp.maximum(totals, other), totals + other)
        bit *= 2
    mine = lax.dynamic_slice_in_dim(totals[:8], me * part, part, 1)
    expand_mine = lax.dynamic_slice_in_dim(totals[8 : 8 + fold].reshape(-1), me * part * fold, part * fold, 0)
    global_top = totals[-1, :H]

    first_sum = first_sum.astype(f32)
    second_sum = second_sum.astype(f32)
    expand_out = jnp.concatenate(
        [first_sum[(fold + i) * part : (fold + i + 1) * part] for i in range(fold)], axis=1
    )
    ratio = CLIP_TAU / jnp.maximum(global_top, CLIP_TAU)
    factor = jnp.where(clip_flags == 1, jnp.sqrt(ratio), 1.0)
    by_column = jnp.repeat(factor, HD)
    return (
        block_out,
        tokens_grad,
        query_mat * by_column[None, :],
        key_mat * by_column[None, :],
        mine[0],
        mine[1],
        second_sum[:part],
        mine[2],
        second_sum[part : 2 * part],
        second_sum[2 * part : 3 * part],
        mine[3],
        first_sum[2 * fold * part :],
        mine[4],
        mine[5],
        mine[6],
        expand_out,
        expand_mine,
        first_sum[: fold * part],
        mine[7],
    )


def solution(mesh):
    split, both = P("dev"), P("dev", None)
    mat = both
    in_specs = (
        mat, split, split, mat, split, mat, mat, split, mat, split, split, split, mat, split, mat, split,
        split, P(), mat,
    )
    out_specs = (
        mat, mat, mat, mat, split, split, mat, split, mat, mat, split, mat, split, split, split, mat,
        split, mat, split,
    )
    return jax.shard_map(local, mesh=mesh, in_specs=in_specs, out_specs=out_specs, check_vma=False)
```

```python
import functools

import jax
import jax.numpy as jnp
from jax import lax
from jax.experimental import pallas as pl
from jax.experimental.pallas import tpu as pltpu
from jax.sharding import PartitionSpec as P

H = 16
HD = 64
LEN = 577
RIM = LEN - 1
HEADS = 4
QB = 256
KB = 256

NORM_EPS = 1e-05
CLIP_TAU = 3.0
GELU_COEF = 1.702
NEG_FILL = -1e30
SCALE = HD ** (-0.5)

bf16 = jnp.bfloat16
f32 = jnp.float32
NN = (((1,), (0,)), ((), ()))
NT = (((1,), (1,)), ((), ()))
TN = (((0,), (0,)), ((), ()))


def dot(lhs, rhs, dims):
    return lax.dot_general(lhs, rhs, dims, preferred_element_type=f32)


def norm_stats(values):
    centre = values - jnp.mean(values, axis=1, keepdims=True)
    inv_std = lax.rsqrt(jnp.mean(centre * centre, axis=1, keepdims=True) + NORM_EPS)
    return centre * inv_std, inv_std


def norm_back(grad_out, gain, normal, inv_std):
    scaled = grad_out * gain
    return inv_std * (
        scaled
        - jnp.mean(scaled, axis=1, keepdims=True)
        - normal * jnp.mean(scaled * normal, axis=1, keepdims=True)
    )


def column_sums(values):
    return jnp.sum(values.astype(f32), axis=0)


def cost(flops):
    return pl.CostEstimate(flops=flops, transcendentals=0, bytes_accessed=flops // 500)


def by_head(block):
    lane = lax.broadcasted_iota(jnp.int32, block.shape, 1) // HD
    zero = jnp.zeros_like(block)
    return jnp.concatenate([jnp.where(lane == i, block, zero) for i in range(HEADS)], axis=0)


def pair_slices(p):
    return slice(p * 2 * HD, (p + 1) * 2 * HD), slice(p * 2 * QB, (p + 1) * 2 * QB)


def untangle(parts):
    joined = []
    for part in parts:
        joined.append(jnp.concatenate([part[:HD, :QB], part[HD:, QB:]], axis=0).T)
    return jnp.concatenate(joined, axis=1)


def by_twos(count, step, start):
    two = lambda i, carry: step(2 * i + 1, step(2 * i, carry))
    return lax.fori_loop(count // 2 * 2, count, step, lax.fori_loop(0, count // 2, two, start))


def widen(bias):
    return jnp.concatenate([bias] * HEADS, axis=1)


def fill_bias(bias_ref, key_ids_ref, query_ids_ref, block, low, count):
    def one(c, carry):
        start = pl.multiple_of(low + c * KB, 128)
        keys = key_ids_ref[pl.ds(start, KB), :]
        same = keys == query_ids_ref[...]
        bias_ref[block, pl.ds(pl.multiple_of(c * KB, KB), KB), :] = jnp.where(same, 0.0, NEG_FILL)
        return carry

    lax.fori_loop(0, count, one, 0)


def attend_kernel(
    low_ref, count_ref, key_ids_ref, query_ids_ref, q_ref, k_ref, v_ref,
    o_ref, wide_ref, lse_ref, top_ref, bias_ref, score_ref,
):
    group, block = pl.program_id(0), pl.program_id(1)
    low, count = low_ref[block], count_ref[block]

    @pl.when(group == 0)
    def _():
        fill_bias(bias_ref, key_ids_ref, query_ids_ref, block, low, count)

    queries = by_head(q_ref[...] * jnp.asarray(SCALE, bf16))
    width = queries.shape[0]
    pairs = HEADS // 2

    def score(c):
        start = pl.multiple_of(low + c * KB, 128)
        return dot(k_ref[pl.ds(start, KB), :], queries, NT)

    def fold(op, tile):
        return op(tile.reshape(KB // 8, 8, width), axis=0)

    def first(c, top):
        at = pl.ds(pl.multiple_of(c * KB, KB), KB)
        scores = score(c) + widen(bias_ref[block, at, :])
        score_ref[at, :] = scores
        return jnp.maximum(top, fold(jnp.max, scores))

    top = by_twos(count, first, jnp.full((8, width), NEG_FILL, f32))
    top = jnp.max(top, axis=0, keepdims=True)

    def second(c, carry):
        total, accs = carry
        start = pl.multiple_of(low + c * KB, 128)
        weights = jnp.exp(score_ref[pl.ds(pl.multiple_of(c * KB, KB), KB), :] - top)
        total = total + fold(jnp.sum, weights)
        low_weights = weights.astype(bf16)
        values = v_ref[pl.ds(start, KB), :]
        new_accs = []
        for p, acc in enumerate(accs):
            lanes, place = pair_slices(p)
            new_accs.append(acc + dot(values[:, lanes], low_weights[:, place], TN))
        return total, tuple(new_accs)

    zeros = tuple(jnp.zeros((2 * HD, 2 * QB), f32) for _ in range(pairs))
    total, accs = by_twos(count, second, (jnp.zeros((8, width), f32), zeros))
    total = jnp.sum(total, axis=0, keepdims=True)
    mixed = untangle([acc / total[:, pair_slices(p)[1]] for p, acc in enumerate(accs)])
    wide_ref[...] = mixed
    o_ref[...] = mixed.astype(bf16)
    lse_ref[0] = top + jnp.log(total)

    @pl.when(block == 0)
    def _():
        top_ref[0] = top

    @pl.when(block != 0)
    def _():
        top_ref[0] = jnp.maximum(top_ref[0], top)


def attend_back_kernel(
    low_ref,
    count_ref,
    key_ids_ref,
    query_ids_ref,
    q_ref,
    k_ref,
    v_ref,
    do_ref,
    o_ref,
    lse_ref,
    dq_ref,
    dk_ref,
    dv_ref,
    bias_ref,
    dk_acc,
    dv_acc,
):
    pair, block = pl.program_id(0), pl.program_id(1)
    low, count = low_ref[block], count_ref[block]

    @pl.when(pair == 0)
    def _():
        fill_bias(bias_ref, key_ids_ref, query_ids_ref, block, low, count)

    @pl.when(block == 0)
    def _():
        dk_acc[...] = jnp.zeros_like(dk_acc)
        dv_acc[...] = jnp.zeros_like(dv_acc)

    queries = by_head(q_ref[...] * jnp.asarray(SCALE, bf16))
    grads = by_head(do_ref[...])
    product = (do_ref[...].astype(f32) * o_ref[...]).T
    inner = jnp.concatenate(
        [jnp.sum(product[i * HD : (i + 1) * HD], axis=0, keepdims=True) for i in range(HEADS)], axis=1
    )
    log_sum = lse_ref[0]
    pairs = HEADS // 2

    def step(c, accs):
        start = pl.multiple_of(low + c * KB, 128)
        keys = k_ref[pl.ds(start, KB), :]
        bias = bias_ref[block, pl.ds(pl.multiple_of(c * KB, KB), KB), :]
        scores = dot(keys, queries, NT) + widen(bias)
        probs = jnp.exp(scores - log_sum)
        prob_grad = dot(v_ref[pl.ds(start, KB), :], grads, NT)
        score_grad = (probs * (prob_grad - inner)).astype(bf16)
        dv_acc[pl.ds(start, KB), :] += dot(probs.astype(bf16), grads, NN)
        dk_acc[pl.ds(start, KB), :] += dot(score_grad, queries, NN)
        new_accs = []
        for p, acc in enumerate(accs):
            lanes, place = pair_slices(p)
            new_accs.append(acc + dot(keys[:, lanes], score_grad[:, place], TN))
        return tuple(new_accs)

    zeros = tuple(jnp.zeros((2 * HD, 2 * QB), f32) for _ in range(pairs))
    dq_ref[...] = (untangle(by_twos(count, step, zeros)) * SCALE).astype(bf16)

    @pl.when(block == pl.num_programs(1) - 1)
    def _():
        dk_ref[...] = dk_acc[...].astype(bf16)
        dv_ref[...] = dv_acc[...].astype(bf16)


def key_ranges(own_ids, near_ids, blocks):
    rows, near = own_ids.shape[0], near_ids.shape[0]
    size = rows // blocks
    place = jnp.arange(near, dtype=jnp.int32)[None, :]
    first = own_ids[0::size][:, None]
    last = own_ids[size - 1 :: size][:, None]
    low = jnp.min(jnp.where(near_ids[None, :] == first, place, near), axis=1)
    high = jnp.max(jnp.where(near_ids[None, :] == last, place, -1), axis=1) + 1
    low = low // 128 * 128
    count = (high - low + KB - 1) // KB
    low = jnp.minimum(low, near - count * KB)
    return low.astype(jnp.int32), count.astype(jnp.int32)


def attention_specs(rows, near, blocks):
    groups = H // HEADS
    span = HEADS * HD
    most = -(-(QB + 2 * RIM + 127) // KB) * KB
    assert most <= near and rows % QB == 0 and near % 128 == 0
    own = pl.BlockSpec((QB, span), lambda p, b, *_: (b, p))
    base = [
        pl.BlockSpec((near, 1), lambda p, b, *_: (0, 0)),
        pl.BlockSpec((1, QB), lambda p, b, *_: (0, b)),
        own,
        pl.BlockSpec((near, span), lambda p, b, *_: (0, p)),
        pl.BlockSpec((near, span), lambda p, b, *_: (0, p + groups)),
    ]
    row = pl.BlockSpec((1, 1, HEADS * QB), lambda p, b, *_: (p, 0, b))
    bias = pltpu.VMEM((blocks, most, QB), f32)
    return groups, own, base, row, bias


def attend(ranges, key_ids, query_ids, queries, near_kv):
    rows, near = queries.shape[0], near_kv.shape[0]
    blocks = rows // QB
    groups, own, base, row, bias = attention_specs(rows, near, blocks)
    top = pl.BlockSpec((1, 1, HEADS * QB), lambda p, b, *_: (p, 0, 0))
    return pl.pallas_call(
        attend_kernel,
        grid_spec=pltpu.PrefetchScalarGridSpec(
            num_scalar_prefetch=2,
            grid=(groups, blocks),
            in_specs=base,
            out_specs=[own, own, row, top],
            scratch_shapes=[bias, pltpu.VMEM((bias.shape[1], HEADS * QB), f32)],
        ),
        out_shape=[
            jax.ShapeDtypeStruct(queries.shape, bf16),
            jax.ShapeDtypeStruct(queries.shape, f32),
            jax.ShapeDtypeStruct((groups, 1, HEADS * rows), f32),
            jax.ShapeDtypeStruct((groups, 1, HEADS * QB), f32),
        ],
        compiler_params=pltpu.CompilerParams(vmem_limit_bytes=56 << 20),
        cost_estimate=cost(rows * H * HD * 850 * 16),
        name="attend",
    )(*ranges, key_ids, query_ids, queries, near_kv, near_kv)


def attend_back(ranges, key_ids, query_ids, queries, near_kv, mixed_grad, mixed, log_sums):
    rows, near = queries.shape[0], near_kv.shape[0]
    blocks = rows // QB
    groups, own, base, row, bias = attention_specs(rows, near, blocks)
    wide = pl.BlockSpec((near, HEADS * HD), lambda p, b, *_: (0, p))
    return pl.pallas_call(
        attend_back_kernel,
        grid_spec=pltpu.PrefetchScalarGridSpec(
            num_scalar_prefetch=2,
            grid=(groups, blocks),
            in_specs=base + [own, own, row],
            out_specs=[own, wide, wide],
            scratch_shapes=[bias, pltpu.VMEM((near, HEADS * HD), f32), pltpu.VMEM((near, HEADS * HD), f32)],
        ),
        out_shape=[
            jax.ShapeDtypeStruct(queries.shape, bf16),
            jax.ShapeDtypeStruct((near, queries.shape[1]), bf16),
            jax.ShapeDtypeStruct((near, queries.shape[1]), bf16),
        ],
        compiler_params=pltpu.CompilerParams(vmem_limit_bytes=56 << 20),
        cost_estimate=cost(rows * H * HD * 850 * 32),
        name="attend_back",
    )(*ranges, key_ids, query_ids, queries, near_kv, near_kv, mixed_grad, mixed, log_sums)


def spot_of(place, half):
    spot, bit = 0, half
    while bit:
        spot = spot + (place & 1) * bit
        place, bit = place >> 1, bit >> 1
    return spot


def mlp_kernel(
    a_ref, dz_ref, x_ref, rb_ref, eb_ref, we_ref, wr_ref,
    y_ref, da_ref, ebg_ref, sum_ref,
    act_ref, du_ref, rg_ref, eg_ref, sems,
):
    j = pl.program_id(0)
    rows, width = a_ref.shape
    tile = 256

    def copies(step):
        d, r, _ = rg_ref.shape
        g, e, _ = eg_ref.shape
        fold = pl.num_programs(0)
        return (
            pltpu.make_async_copy(rg_ref, sum_ref.at[pl.ds(step * d, d), pl.ds(0, r), :], sems.at[0]),
            pltpu.make_async_copy(eg_ref, sum_ref.at[:, pl.ds(r + step * e, e), :], sems.at[1]),
        )

    @pl.when(j == 0)
    def _():
        y_ref[...] = x_ref[...] + rb_ref[...]
        da_ref[...] = jnp.zeros_like(da_ref)

    ebg_ref[...] = jnp.zeros_like(ebg_ref)

    def by_rows(r, carry):
        at = pl.ds(pl.multiple_of(r * tile, tile), tile)
        we = we_ref[...].reshape(width, width)
        wr = wr_ref[...].reshape(width, width)
        hidden = dot(a_ref[at, :], we, NN) + eb_ref[...]
        back = dot(dz_ref[at, :], wr, NT)
        sigma = jax.nn.sigmoid(GELU_COEF * hidden)
        act = (hidden * sigma).astype(bf16)
        act_ref[at, :] = act
        du = (back * (sigma + GELU_COEF * hidden * sigma * (1.0 - sigma))).astype(bf16)
        du_ref[at, :] = du
        ebg_ref[...] += jnp.sum(du.astype(f32), axis=0, keepdims=True)
        y_ref[at, :] += dot(act, wr, NN)
        da_ref[at, :] += dot(du, we, NT)
        return carry

    lax.fori_loop(0, rows // tile, by_rows, 0)

    @pl.when(j > 0)
    def _():
        for copy in copies(j - 1):
            copy.wait()

    def by_columns(t, carry):
        at = pl.ds(pl.multiple_of(t * tile, tile), tile)
        rg = dot(act_ref[:, at], dz_ref[...], TN).astype(bf16)
        n = tile // rg_ref.shape[1]
        rg_ref[pl.ds(t * n, n)] = rg.reshape(n, rg_ref.shape[1], width)
        eg = dot(a_ref[:, at], du_ref[...], TN).astype(bf16)
        n = tile // eg_ref.shape[1]
        eg_ref[pl.ds(t * n, n)] = eg.reshape(n, eg_ref.shape[1], width)
        return carry

    lax.fori_loop(0, width // tile, by_columns, 0)
    for copy in copies(j):
        copy.start()

    @pl.when(j == pl.num_programs(0) - 1)
    def _():
        for copy in copies(j):
            copy.wait()


def mlp(normed, branch_grad, middle, bias_reduce, bias_expand, packed, sum_rows):
    rows, width = normed.shape
    ff = bias_expand.shape[1]
    fold = ff // width
    groups = packed.shape[0]
    each = width // groups
    whole = lambda j: (0, 0)
    one = pl.Buffered(1)
    return pl.pallas_call(
        mlp_kernel,
        grid=(fold,),
        in_specs=[
            pl.BlockSpec((rows, width), whole, pipeline_mode=one),
            pl.BlockSpec((rows, width), whole, pipeline_mode=one),
            pl.BlockSpec((rows, width), whole, pipeline_mode=one),
            pl.BlockSpec((1, width), whole),
            pl.BlockSpec((1, width), lambda j: (0, j)),
            pl.BlockSpec((groups, each, width), lambda j: (0, fold + j, 0)),
            pl.BlockSpec((groups // fold, fold * each, width), lambda j: (j, 0, 0)),
        ],
        out_specs=[
            pl.BlockSpec((rows, width), whole),
            pl.BlockSpec((rows, width), whole),
            pl.BlockSpec((1, width), lambda j: (0, j)),
            pl.BlockSpec(memory_space=pl.ANY),
        ],
        out_shape=[
            jax.ShapeDtypeStruct((rows, width), f32),
            jax.ShapeDtypeStruct((rows, width), f32),
            jax.ShapeDtypeStruct((1, ff), f32),
            jax.ShapeDtypeStruct((groups, sum_rows, width), bf16),
        ],
        scratch_shapes=[
            pltpu.VMEM((rows, width), bf16),
            pltpu.VMEM((rows, width), bf16),
            pltpu.VMEM((groups // fold, fold * each, width), bf16),
            pltpu.VMEM((groups, each, width), bf16),
            pltpu.SemaphoreType.DMA((2,)),
        ],
        compiler_params=pltpu.CompilerParams(vmem_limit_bytes=58 << 20),
        cost_estimate=cost(12 * rows * width * ff),
        name="mlp",
    )(normed, branch_grad, middle, bias_reduce, bias_expand, packed, packed)


def out_back_kernel(me_ref, ag_ref, mixed_ref, wo_ref, mg_ref, keep_ref, send_ref):
    rows, width = ag_ref.shape
    tile = 256
    half, each, _ = keep_ref.shape

    def by_columns(t, carry):
        at = pl.ds(pl.multiple_of(t * tile, tile), tile)
        og = dot(mixed_ref[:, at], ag_ref[...], TN).astype(bf16)
        n = tile // each
        for i in range(n):
            spot = spot_of((t * n + i) ^ me_ref[0], half)
            block = og[i * each : (i + 1) * each]

            @pl.when(spot < half)
            def _():
                keep_ref[spot] = block

            @pl.when(spot >= half)
            def _():
                send_ref[spot - half] = block

        return carry

    lax.fori_loop(0, width // tile, by_columns, 0)
    def by_rows(t, carry):
        at = pl.ds(pl.multiple_of(t * tile, tile), tile)
        mg_ref[at, :] = dot(ag_ref[at, :], wo_ref[...].reshape(width, width), NT).astype(bf16)
        return carry

    lax.fori_loop(0, rows // tile, by_rows, 0)


def out_back(attn_grad, mixed, packed, last, place):
    rows, width = attn_grad.shape
    groups = packed.shape[0]
    each = width // groups
    whole = lambda i, *_: (0, 0)
    side = pl.BlockSpec((groups // 2, each, width), lambda i, *_: (0, 0, 0))
    half = jax.ShapeDtypeStruct((groups // 2, each, width), bf16)
    return pl.pallas_call(
        out_back_kernel,
        grid_spec=pltpu.PrefetchScalarGridSpec(
            num_scalar_prefetch=1,
            grid=(1,),
            in_specs=[
                pl.BlockSpec((rows, width), whole),
                pl.BlockSpec((rows, width), whole),
                pl.BlockSpec((groups, each, width), lambda i, *_: (0, last, 0)),
            ],
            out_specs=[pl.BlockSpec((rows, width), whole), side, side],
        ),
        out_shape=[
            jax.ShapeDtypeStruct((rows, width), bf16),
            half,
            half,
        ],
        compiler_params=pltpu.CompilerParams(vmem_limit_bytes=56 << 20),
        cost_estimate=cost(4 * rows * width * width),
        name="out_back",
    )(place, attn_grad, mixed, packed)


def qkv_kernel(a_ref, w_ref, bias_ref, q_ref, kv_ref):
    j = pl.program_id(0)
    near, width = a_ref.shape
    rows = q_ref.shape[0]
    rim = (near - rows) // 2

    @pl.when(j == 0)
    def _():
        def step(t, carry):
            source = pl.ds(pl.multiple_of(rim + t * 256, 8), 256)
            w = w_ref[...].reshape(width, width)
            q_ref[pl.ds(pl.multiple_of(t * 256, 256), 256), :] = (
                dot(a_ref[source, :], w, NN) + bias_ref[...]
            ).astype(bf16)
            return carry

        lax.fori_loop(0, rows // 256, step, 0)

    @pl.when(j > 0)
    def _():
        size = near // 8

        def step(t, carry):
            at = pl.ds(pl.multiple_of(t * size, 16), size)
            w = w_ref[...].reshape(width, width)
            kv_ref[at, :] = (dot(a_ref[at, :], w, NN) + bias_ref[...]).astype(bf16)
            return carry

        lax.fori_loop(0, near // size, step, 0)


def project(normed_near, packed, biases, rows):
    near, width = normed_near.shape
    groups = packed.shape[0]
    each = width // groups
    return pl.pallas_call(
        qkv_kernel,
        grid=(3,),
        in_specs=[
            pl.BlockSpec((near, width), lambda j: (0, 0)),
            pl.BlockSpec((groups, each, width), lambda j: (0, j, 0)),
            pl.BlockSpec((1, width), lambda j: (0, j)),
        ],
        out_specs=[
            pl.BlockSpec((rows, width), lambda j: (0, 0)),
            pl.BlockSpec((near, width), lambda j: (0, jnp.maximum(j - 1, 0))),
        ],
        out_shape=[
            jax.ShapeDtypeStruct((rows, width), bf16),
            jax.ShapeDtypeStruct((near, 2 * width), bf16),
        ],
        compiler_params=pltpu.CompilerParams(vmem_limit_bytes=56 << 20),
        cost_estimate=cost(2 * width * width * (rows + 2 * near)),
        name="qkv",
    )(normed_near, packed, biases)


def qkv_grads_kernel(me_ref, a_ref, dq_ref, dk_ref, dv_ref, keep_ref, send_ref):
    j = pl.program_id(0)
    near, width = a_ref.shape
    rows = dq_ref.shape[0]
    rim = (near - rows) // 2
    tile = 256
    half, each, _ = keep_ref.shape
    n = tile // each

    def fill(grad_ref, source):
        def step(t, carry):
            at = pl.ds(pl.multiple_of(t * tile, tile), tile)
            out = dot(a_ref[source, at], grad_ref[...], TN).astype(bf16)
            for i in range(n):
                spot = spot_of((t * n + i) ^ me_ref[0], half)
                block = out[i * each : (i + 1) * each]

                @pl.when(spot < half)
                def _():
                    keep_ref[spot] = block

                @pl.when(spot >= half)
                def _():
                    send_ref[spot - half] = block

            return carry

        lax.fori_loop(0, width // tile, step, 0)

    @pl.when(j == 0)
    def _():
        fill(dq_ref, slice(rim, rim + rows))

    @pl.when(j == 1)
    def _():
        fill(dk_ref, slice(0, near))

    @pl.when(j == 2)
    def _():
        fill(dv_ref, slice(0, near))


def qkv_grads(normed_near, query_grad, key_near, value_near, groups, place):
    near, width = normed_near.shape
    rows = query_grad.shape[0]
    each = width // groups
    whole = lambda j, *_: (0, 0)
    half = jax.ShapeDtypeStruct((groups // 2, 3 * each, width), bf16)
    out = pl.BlockSpec((groups // 2, each, width), lambda j, *_: (0, j, 0))
    return pl.pallas_call(
        qkv_grads_kernel,
        grid_spec=pltpu.PrefetchScalarGridSpec(
            num_scalar_prefetch=1,
            grid=(3,),
            in_specs=[
                pl.BlockSpec((near, width), whole),
                pl.BlockSpec((rows, width), whole),
                pl.BlockSpec((near, width), whole),
                pl.BlockSpec((near, width), whole),
            ],
            out_specs=[out, out],
        ),
        out_shape=[half, half],
        compiler_params=pltpu.CompilerParams(vmem_limit_bytes=56 << 20),
        cost_estimate=cost(2 * width * width * (rows + 2 * near)),
        name="qkv_grads",
    )(place, normed_near, query_grad, key_near, value_near)


def plus(a, b):
    return (a.astype(f32) + b.astype(f32)).astype(bf16)


def swap(value, bit):
    peers = lax.axis_size("dev")
    return lax.ppermute(value, "dev", [(i, i ^ bit) for i in range(peers)])


def merge(totals, bit):
    other = swap(totals, bit)
    return jnp.concatenate([totals[:-1] + other[:-1], jnp.maximum(totals[-1:], other[-1:])], axis=0)


def halving(first, second, totals):
    def split(pair):
        keep, other = (v.reshape((2, 2, 4) + v.shape[1:]) for v in pair)
        return keep, other

    (keep, other), (keep_o, other_o) = split(first), split(second)
    half = (keep.shape[3] + keep_o.shape[3]) // 2

    def side_a(at):
        return plus(keep[at][..., :half, :], other[at][..., :half, :])

    def side_b(at):
        return jnp.concatenate(
            [plus(keep[at][..., half:, :], other[at][..., half:, :]), plus(keep_o[at], other_o[at])], axis=-2
        )

    to_x, to_y = side_a(1), side_b((slice(None), 1))
    to_x, to_y, totals = lax.optimization_barrier((to_x, to_y, totals))
    from_x, from_y = swap(to_x, 2), swap(to_y, 4)
    totals = merge(totals, 1)
    keep_x, keep_y = side_a(0), side_b((slice(None), 0))
    to_y, to_x = plus(keep_x[1], from_x[1]), plus(keep_y[1], from_y[1])
    to_x, to_y, totals = lax.optimization_barrier((to_x, to_y, totals))
    second_y, second_x = swap(to_y, 4), swap(to_x, 2)
    totals = merge(totals, 2)
    keep_x = plus(keep_x[0], from_x[0])
    keep_y = plus(keep_y[0], from_y[0])
    send = jnp.concatenate([plus(keep_x[2:], second_y[2:]), plus(keep_y[2:], second_x[2:])], axis=1)
    send, totals = lax.optimization_barrier((send, totals))
    low = swap(send, 8)
    totals = merge(totals, 4)
    keep = jnp.concatenate([plus(keep_x[:2], second_y[:2]), plus(keep_y[:2], second_x[:2])], axis=1)
    send, totals = lax.optimization_barrier((plus(keep[1], low[1]), totals))
    last = swap(send, 16)
    totals = merge(merge(totals, 8), 16)
    return plus(keep[0], low[0]).astype(f32) + last.astype(f32), totals


def plain(pairs, part):
    groups = 2 * pairs[0][0].shape[0]
    order = [int(f"{i:05b}"[::-1], 2) for i in range(groups)]
    joined = jnp.concatenate([jnp.concatenate(pair, axis=0) for pair in pairs], axis=1)
    joined = jnp.stack([joined[i] for i in order])
    return scatter(joined, [part] * (joined.shape[1] * groups // joined.shape[2])).astype(f32)


def normed_grad_kernel(
    dq_ref, dk_ref, dv_ref, w_ref, normal_ref, nb_ref, na_ref,
    own_ref, before_ref, after_ref, sums_ref, acc_b, acc_a,
):
    j = pl.program_id(0)
    rows, width = own_ref.shape
    rim = before_ref.shape[0]

    def by_rows(total, size, act):
        def step(t, carry):
            act(pl.multiple_of(t * size, size))
            return carry

        lax.fori_loop(0, total // size, step, 0)

    def near(grad_ref, first):
        def add(out_ref, base, size):
            def act(at):
                w = w_ref[...].reshape(width, width)
                part = dot(grad_ref[pl.ds(pl.multiple_of(base + at, 8), size), :], w, NT)
                spot = pl.ds(at, size)
                out_ref[spot, :] = part if first else out_ref[spot, :] + part

            return act

        by_rows(rim, rim // 2, add(acc_b, 0, rim // 2))
        by_rows(rim, rim // 2, add(acc_a, rim + rows, rim // 2))

        def act(at):
            w = w_ref[...].reshape(width, width)
            own_ref[pl.ds(at, 256), :] += dot(grad_ref[pl.ds(pl.multiple_of(rim + at, 8), 256), :], w, NT)

        by_rows(rows, 256, act)

    @pl.when(j == 0)
    def _():
        sums_ref[...] = jnp.zeros_like(sums_ref)

        def act(at):
            spot = pl.ds(at, 256)
            w = w_ref[...].reshape(width, width)
            grads = dq_ref[spot, :]
            own_ref[spot, :] = dot(grads, w, NT)

        by_rows(rows, 256, act)

    @pl.when(j == 1)
    def _():
        near(dk_ref, True)

    @pl.when(j == 2)
    def _():
        near(dv_ref, False)

        def finish(source, normal, out, carry):
            def step(t, carry):
                gain_sum, bias_sum = carry
                spot = pl.ds(pl.multiple_of(t * 16, 16), 16)
                value = source[spot, :]
                product = value * normal[spot, :].astype(f32)
                if out is not None:
                    out[spot, :] = value.astype(bf16)
                return gain_sum + product[:8] + product[8:], bias_sum + value[:8] + value[8:]

            return lax.fori_loop(0, source.shape[0] // 16, step, carry)

        carry = (jnp.zeros((8, width), f32), jnp.zeros((8, width), f32))
        carry = finish(acc_b, nb_ref, before_ref, carry)
        carry = finish(acc_a, na_ref, after_ref, carry)
        gain_sum, bias_sum = finish(own_ref, normal_ref, None, carry)
        sums_ref[0:1, :] = jnp.sum(gain_sum, axis=0, keepdims=True)
        sums_ref[1:2, :] = jnp.sum(bias_sum, axis=0, keepdims=True)
        sums_ref[2:3, :] = dot(jnp.ones((8, rows), bf16), dq_ref[...], NN)[0:1]
        sums_ref[3:4, :] = dot(jnp.ones((8, 2 * rim + rows), bf16), dv_ref[...], NN)[0:1]


def project_back(query_grad, key_near, value_near, packed, normal, before, after):
    rows, width = query_grad.shape
    near, rim = key_near.shape[0], before.shape[0]
    groups = packed.shape[0]
    each = width // groups
    whole = lambda j: (0, 0)
    one = pl.Buffered(1)
    own, wide, side = (pl.BlockSpec((n, width), whole, pipeline_mode=one) for n in (rows, near, rim))
    return pl.pallas_call(
        normed_grad_kernel,
        grid=(3,),
        in_specs=[own, wide, wide, pl.BlockSpec((groups, each, width), lambda j: (0, j, 0)), own, side, side],
        out_specs=[
            pl.BlockSpec((rows, width), whole),
            pl.BlockSpec((rim, width), whole),
            pl.BlockSpec((rim, width), whole),
            pl.BlockSpec((4, width), whole),
        ],
        out_shape=[
            jax.ShapeDtypeStruct((rows, width), f32),
            jax.ShapeDtypeStruct((rim, width), bf16),
            jax.ShapeDtypeStruct((rim, width), bf16),
            jax.ShapeDtypeStruct((4, width), f32),
        ],
        scratch_shapes=[pltpu.VMEM((rim, width), f32), pltpu.VMEM((rim, width), f32)],
        compiler_params=pltpu.CompilerParams(vmem_limit_bytes=58 << 20),
        cost_estimate=cost(2 * width * width * (rows + 2 * near)),
        name="normed_grad",
    )(query_grad, key_near, value_near, packed, normal, before, after)


def gather(value, segments, groups):
    peers = lax.axis_size("dev")
    rows, width = value.shape
    whole = lax.all_gather(value, "dev", axis=0, tiled=True)
    sub = peers // groups
    if sub == 1:
        return whole.reshape(groups, rows, width)
    whole = whole.reshape(groups, sub, rows, width)
    parts, at = [], 0
    for size in segments:
        parts.append(whole[:, :, at : at + size].reshape(groups, sub * size, width))
        at += size
    return jnp.concatenate(parts, axis=1)


def scatter(value, segments):
    peers = lax.axis_size("dev")
    groups, rows, width = value.shape
    sub = peers // groups
    if sub > 1:
        parts, at = [], 0
        for size in segments:
            cut = value[:, at : at + sub * size]
            parts.append(cut.reshape(groups, sub, size, width))
            at += sub * size
        value = jnp.concatenate(parts, axis=2)
    value = value.reshape(peers * sum(segments), width)
    return lax.psum_scatter(value, "dev", scatter_dimension=0, tiled=True)


def pack_kernel(me_ref, q_ref, k_ref, v_ref, small_ref, r_ref, e_ref, o_ref, eb_ref, one_ref, two_ref):
    part, width = q_ref.shape
    for i, ref in enumerate((q_ref, k_ref, v_ref)):
        one_ref[i * part : (i + 1) * part, :] = ref[...].astype(bf16)

    def place(value, size):
        index = lax.broadcasted_iota(jnp.int32, value.shape, 0) * width
        index = index + lax.broadcasted_iota(jnp.int32, value.shape, 1)
        return jnp.where(index // size == me_ref[0], value, jnp.zeros_like(value))

    lane = lax.broadcasted_iota(jnp.int32, (8, width), 1)
    one_ref[3 * part :, :] = jnp.where(lane // part == me_ref[0], small_ref[...], 0.0).astype(bf16)
    rows = r_ref.shape[0]
    fold = rows // part
    two_ref[:rows, :] = r_ref[...].astype(bf16)
    for i in range(fold):
        at = rows + i * part
        two_ref[at : at + part, :] = e_ref[:, i * width : (i + 1) * width].astype(bf16)
    at = rows + fold * part
    two_ref[at : at + part, :] = o_ref[...].astype(bf16)
    two_ref[at + part :, :] = place(jnp.broadcast_to(eb_ref[...], (8, width)), fold * part).astype(bf16)


def pack(me, mats, smalls, reduce_mat, expand_mat, output_mat, expand_bias):
    part, width = output_mat.shape
    tiled = jnp.stack([jnp.tile(v, width // part) for v in smalls])
    bias = jnp.tile(expand_bias, width // expand_bias.shape[0])[None]
    rows = reduce_mat.shape[0]
    return pl.pallas_call(
        pack_kernel,
        grid_spec=pltpu.PrefetchScalarGridSpec(
            num_scalar_prefetch=1,
            grid=(1,),
            in_specs=[
                pl.BlockSpec(v.shape, lambda i, *_: (0, 0))
                for v in (*mats, tiled, reduce_mat, expand_mat, output_mat, bias)
            ],
            out_specs=[
                pl.BlockSpec((3 * part + 8, width), lambda i, *_: (0, 0)),
                pl.BlockSpec((2 * rows + part + 8, width), lambda i, *_: (0, 0)),
            ],
        ),
        out_shape=[
            jax.ShapeDtypeStruct((3 * part + 8, width), bf16),
            jax.ShapeDtypeStruct((2 * rows + part + 8, width), bf16),
        ],
        name="pack",
    )(jnp.full((1,), me, jnp.int32), *mats, tiled, reduce_mat, expand_mat, output_mat, bias)


def place_kernel(me_ref, a_ref, ac_ref, b_ref, bc_ref, out_ref):
    half = out_ref.shape[2] // 2
    for core, (left, right) in enumerate(((a_ref, b_ref), (ac_ref, bc_ref))):
        for spot in range(16):
            high, low, z8, z16 = spot >> 3 & 1, spot >> 2 & 1, spot >> 1 & 1, spot & 1
            z = z8 * 8 + z16 * 16 + core
            out_ref[(z + high * 4 + low * 2) ^ me_ref[0], :, :half] = left[spot]
            out_ref[(z + high * 2 + low * 4) ^ me_ref[0], :, half:] = right[spot]


def doubling(value, me, beside):
    rows, width = value.shape
    half = width // 2
    grown = value[None]
    grown = jnp.concatenate([grown, swap(grown, 16)])
    other = swap(grown, 8)
    grown, other, *beside = lax.optimization_barrier((grown, other, *beside))
    a = jnp.concatenate([grown[..., :half], other[..., :half]])
    b = jnp.concatenate([grown[..., half:], other[..., half:]])
    from_x, from_y = swap(a, 2), swap(b, 4)
    a, b = jnp.concatenate([a, from_x]), jnp.concatenate([b, from_y])
    from_y, from_x = swap(a, 4), swap(b, 2)
    a, b = jnp.concatenate([a, from_y]), jnp.concatenate([b, from_x])
    block = pl.BlockSpec(a.shape, lambda i, *_: (0, 0, 0))
    placed = pl.pallas_call(
        place_kernel,
        grid_spec=pltpu.PrefetchScalarGridSpec(
            num_scalar_prefetch=1,
            grid=(1,),
            in_specs=[block] * 4,
            out_specs=pl.BlockSpec((32, rows, width), lambda i, *_: (0, 0, 0)),
        ),
        out_shape=jax.ShapeDtypeStruct((32, rows, width), bf16),
        compiler_params=pltpu.CompilerParams(vmem_limit_bytes=56 << 20),
        name="place",
    )(jnp.full((1,), me, jnp.int32), a, swap(a, 1), b, swap(b, 1))
    return placed, beside


def spread(vector, width):
    peers, me = lax.axis_size("dev"), lax.axis_index("dev")
    size = vector.shape[0]
    place = jnp.arange(peers * size, dtype=jnp.int32) // size
    full = jnp.where(place == me, jnp.tile(vector, peers), jnp.zeros((), vector.dtype))
    return full.reshape(-1, width)


def local(
    tokens_in,
    attn_gain,
    attn_bias,
    query_mat,
    query_bias,
    key_mat,
    value_mat,
    value_bias,
    output_mat,
    output_bias,
    mlp_gain,
    mlp_bias,
    expand_mat,
    expand_bias,
    reduce_mat,
    reduce_bias,
    image_ids,
    clip_flags,
    out_grad,
):
    peers, me = lax.axis_size("dev"), lax.axis_index("dev")
    rows, width = tokens_in.shape
    part = query_mat.shape[0]
    ff = expand_mat.shape[1]
    fold = ff // width
    groups = min(peers, 32)
    sub = peers // groups

    paired = peers == 32
    up = [(i, i + 1) for i in range(peers - 1)]
    down = [(i + 1, i) for i in range(peers - 1)]
    own_ids = image_ids + 1
    normal_one, inv_one = norm_stats(tokens_in)
    normal_low = normal_one.astype(bf16)

    def with_ids(at):
        ids = jnp.pad(own_ids[at], (0, width - RIM))
        return jnp.concatenate(
            [normal_low[at], (ids // 32).astype(bf16)[None], (ids % 32).astype(bf16)[None], jnp.zeros((6, width), bf16)]
        )

    before = lax.ppermute(with_ids(slice(rows - RIM, rows)), "dev", up)
    after = lax.ppermute(with_ids(slice(0, RIM)), "dev", down)
    smalls = (attn_gain, attn_bias, query_bias, value_bias, output_bias, mlp_gain, mlp_bias, reduce_bias)
    if paired:
        packed_one, packed_two = pack(
            me, (query_mat, key_mat, value_mat), smalls, reduce_mat, expand_mat, output_mat, expand_bias
        )
        first, (before, after, packed_two) = doubling(packed_one, me, (before, after, packed_two))
        second = gather(packed_two, (), groups)
    else:
        low = [v.astype(bf16) for v in (query_mat, key_mat, value_mat)]
        packed_one = jnp.concatenate(low + [spread(v.astype(bf16), width) for v in smalls])
        first = gather(packed_one, [part] * 3 + [8], groups)
        expand_low = expand_mat.astype(bf16)
        packed_two = jnp.concatenate(
            [reduce_mat.astype(bf16)]
            + [expand_low[:, i * width : (i + 1) * width] for i in range(fold)]
            + [output_mat.astype(bf16), spread(expand_bias.astype(bf16), width), jnp.zeros((8 - fold, width), bf16)]
        )
        second = gather(packed_two, [fold * part] + [part] * (fold + 1) + [8], groups)


    def ids_of(halo):
        return (halo[RIM, :RIM].astype(f32) * 32 + halo[RIM + 1, :RIM].astype(f32)).astype(jnp.int32)

    near_ids = jnp.concatenate([ids_of(before), own_ids, ids_of(after)])
    before, after = before[:RIM], after[:RIM]
    ranges = key_ranges(own_ids, near_ids, rows // QB)
    key_ids, query_ids = near_ids[:, None], own_ids[None, :]

    first, before, after, ranges, key_ids, query_ids, normal_one = lax.optimization_barrier(
        (first, before, after, ranges, key_ids, query_ids, normal_one)
    )
    vectors = jnp.sum(first[:, groups * 0 + 3 * part * sub :].reshape(groups * sub, 8, width).astype(f32), axis=0)
    (gain_one, bias_one, bias_query, bias_value, bias_output, gain_two, bias_two, bias_reduce) = [
        vectors[i : i + 1] for i in range(8)
    ]

    normed_near = jnp.concatenate(
        [(v.astype(f32) * gain_one + bias_one).astype(bf16) for v in (before, normal_one, after)], axis=0
    )
    bias_qkv = jnp.concatenate([bias_query, jnp.zeros_like(bias_value), bias_value], axis=1)
    queries, near_kv = project(normed_near, first, bias_qkv, rows)
    mixed, mixed_wide, log_sums, tops = attend(ranges, key_ids, query_ids, queries, near_kv)
    head_top = jnp.max(tops.reshape(H, QB), axis=1)

    tail = second[:, (2 * fold + 1) * part * sub :].reshape(groups * sub, 8, width)
    bias_expand = jnp.sum(tail.astype(f32), axis=0)[:fold].reshape(1, ff)
    w_output = second[:, 2 * fold * part * sub : (2 * fold + 1) * part * sub].reshape(width, width)
    middle = tokens_in + dot(mixed, w_output, NN) + bias_output
    normal_two, inv_two = norm_stats(middle)
    normed_two = (normal_two * gain_two + bias_two).astype(bf16)
    branch_grad = out_grad.astype(bf16)
    block_out, normed_two_grad, expand_bias_grad, sums = mlp(
        normed_two, branch_grad, middle, bias_reduce, bias_expand, second, 2 * fold * width // groups + 8
    )
    reduce_bias_grad = column_sums(branch_grad)
    mlp_gain_grad = jnp.sum(normed_two_grad * normal_two, axis=0)
    mlp_bias_grad = jnp.sum(normed_two_grad, axis=0)
    middle_grad = out_grad + norm_back(normed_two_grad, gain_two, normal_two, inv_two)
    attn_grad = middle_grad.astype(bf16)
    output_bias_grad = column_sums(attn_grad)
    first_sum = scatter(sums, [fold * part] + [part] * fold + [8 // sub])
    place = jnp.full((1,), me if peers == 32 else 0, jnp.int32)
    mixed_grad, *out_halves = out_back(attn_grad, mixed, second, 2 * fold, place)
    out_other = swap(out_halves[1], 1) if peers == 32 else None
    rest = jnp.concatenate(
        [
            output_bias_grad[None],
            mlp_gain_grad[None],
            mlp_bias_grad[None],
            reduce_bias_grad[None],
            expand_bias_grad.reshape(fold, width),
            jnp.pad(head_top, (0, width - H))[None],
        ]
    )
    mixed_grad, rest = lax.optimization_barrier((mixed_grad, rest))
    query_grad, key_near, value_near = attend_back(
        ranges, key_ids, query_ids, queries, near_kv, mixed_grad, mixed_wide, log_sums
    )
    halves = qkv_grads(normed_near, query_grad, key_near, value_near, groups, place)
    halves, query_grad, key_near, value_near = lax.optimization_barrier((halves, query_grad, key_near, value_near))
    received = swap(halves[1], 1) if peers == 32 else None
    normed_grad, to_prev, to_next, norm_sums = project_back(
        query_grad, key_near, value_near, first, normal_one, before, after
    )
    from_next = lax.ppermute(to_prev, "dev", down)
    from_prev = lax.ppermute(to_next, "dev", up)
    totals = jnp.concatenate([norm_sums, rest])
    if peers == 32:
        second_sum, totals = halving((halves[0], received), (out_halves[0], out_other), totals)
    else:
        second_sum = plain((halves, out_halves), part)
        bit = 1
        while bit < peers:
            totals = merge(totals, bit)
            bit *= 2
    normed_grad = normed_grad + jnp.pad(from_prev.astype(f32), ((0, rows - RIM), (0, 0)))
    normed_grad = normed_grad + jnp.pad(from_next.astype(f32), ((rows - RIM, 0), (0, 0)))
    tokens_grad = middle_grad + norm_back(normed_grad, gain_one, normal_one, inv_one)
    mine = lax.dynamic_slice_in_dim(totals[:8], me * part, part, 1)
    expand_mine = lax.dynamic_slice_in_dim(totals[8 : 8 + fold].reshape(-1), me * part * fold, part * fold, 0)
    global_top = totals[-1, :H]

    first_sum = first_sum.astype(f32)
    expand_out = jnp.concatenate(
        [first_sum[(fold + i) * part : (fold + i + 1) * part] for i in range(fold)], axis=1
    )
    ratio = CLIP_TAU / jnp.maximum(global_top, CLIP_TAU)
    factor = jnp.where(clip_flags == 1, jnp.sqrt(ratio), 1.0)
    by_column = jnp.repeat(factor, HD)
    return (
        block_out,
        tokens_grad,
        query_mat * by_column[None, :],
        key_mat * by_column[None, :],
        mine[0],
        mine[1],
        second_sum[:part],
        mine[2],
        second_sum[part : 2 * part],
        second_sum[2 * part : 3 * part],
        mine[3],
        second_sum[3 * part :],
        mine[4],
        mine[5],
        mine[6],
        expand_out,
        expand_mine,
        first_sum[: fold * part],
        mine[7],
    )


def solution(mesh):
    split, both = P("dev"), P("dev", None)
    mat = both
    in_specs = (
        mat, split, split, mat, split, mat, mat, split, mat, split, split, split, mat, split, mat, split,
        split, P(), mat,
    )
    out_specs = (
        mat, mat, mat, mat, split, split, mat, split, mat, mat, split, mat, split, split, split, mat,
        split, mat, split,
    )
    return jax.shard_map(local, mesh=mesh, in_specs=in_specs, out_specs=out_specs, check_vma=False)
```

```python
import functools

import jax
import jax.numpy as jnp
from jax import lax
from jax.experimental import pallas as pl
from jax.experimental.pallas import tpu as pltpu
from jax.sharding import PartitionSpec as P

H = 16
HD = 64
LEN = 577
RIM = LEN - 1
HEADS = 4
QB = 256
KB = 256

NORM_EPS = 1e-05
CLIP_TAU = 3.0
GELU_COEF = 1.702
NEG_FILL = -1e30
SCALE = HD ** (-0.5)

bf16 = jnp.bfloat16
f32 = jnp.float32
NN = (((1,), (0,)), ((), ()))
NT = (((1,), (1,)), ((), ()))
TN = (((0,), (0,)), ((), ()))


def dot(lhs, rhs, dims):
    return lax.dot_general(lhs, rhs, dims, preferred_element_type=f32)


def norm_stats(values):
    centre = values - jnp.mean(values, axis=1, keepdims=True)
    inv_std = lax.rsqrt(jnp.mean(centre * centre, axis=1, keepdims=True) + NORM_EPS)
    return centre * inv_std, inv_std


def norm_back(grad_out, gain, normal, inv_std):
    scaled = grad_out * gain
    return inv_std * (
        scaled
        - jnp.mean(scaled, axis=1, keepdims=True)
        - normal * jnp.mean(scaled * normal, axis=1, keepdims=True)
    )


def column_sums(values):
    return jnp.sum(values.astype(f32), axis=0)


def cost(flops):
    return pl.CostEstimate(flops=flops, transcendentals=0, bytes_accessed=flops // 500)


def by_head(block):
    lane = lax.broadcasted_iota(jnp.int32, block.shape, 1) // HD
    zero = jnp.zeros_like(block)
    return jnp.concatenate([jnp.where(lane == i, block, zero) for i in range(HEADS)], axis=0)


def pair_slices(p):
    return slice(p * 2 * HD, (p + 1) * 2 * HD), slice(p * 2 * QB, (p + 1) * 2 * QB)


def untangle(parts):
    joined = []
    for part in parts:
        joined.append(jnp.concatenate([part[:HD, :QB], part[HD:, QB:]], axis=0).T)
    return jnp.concatenate(joined, axis=1)


def by_twos(count, step, start):
    two = lambda i, carry: step(2 * i + 1, step(2 * i, carry))
    return lax.fori_loop(count // 2 * 2, count, step, lax.fori_loop(0, count // 2, two, start))


def widen(bias):
    return jnp.concatenate([bias] * HEADS, axis=1)


def fill_bias(bias_ref, key_ids_ref, query_ids_ref, block, low, count):
    def one(c, carry):
        start = pl.multiple_of(low + c * KB, 128)
        keys = key_ids_ref[pl.ds(start, KB), :]
        same = keys == query_ids_ref[...]
        bias_ref[block, pl.ds(pl.multiple_of(c * KB, KB), KB), :] = jnp.where(same, 0.0, NEG_FILL)
        return carry

    lax.fori_loop(0, count, one, 0)


def attend_kernel(
    low_ref, count_ref, key_ids_ref, query_ids_ref, q_ref, k_ref, v_ref,
    o_ref, wide_ref, lse_ref, top_ref, bias_ref, score_ref,
):
    group, block = pl.program_id(0), pl.program_id(1)
    low, count = low_ref[block], count_ref[block]

    @pl.when(group == 0)
    def _():
        fill_bias(bias_ref, key_ids_ref, query_ids_ref, block, low, count)

    queries = by_head(q_ref[...] * jnp.asarray(SCALE, bf16))
    width = queries.shape[0]
    pairs = HEADS // 2

    def score(c):
        start = pl.multiple_of(low + c * KB, 128)
        return dot(k_ref[pl.ds(start, KB), :], queries, NT)

    def fold(op, tile):
        return op(tile.reshape(KB // 8, 8, width), axis=0)

    def first(c, top):
        at = pl.ds(pl.multiple_of(c * KB, KB), KB)
        scores = score(c) + widen(bias_ref[block, at, :])
        score_ref[at, :] = scores
        return jnp.maximum(top, fold(jnp.max, scores))

    top = by_twos(count, first, jnp.full((8, width), NEG_FILL, f32))
    top = jnp.max(top, axis=0, keepdims=True)

    def second(c, carry):
        total, accs = carry
        start = pl.multiple_of(low + c * KB, 128)
        weights = jnp.exp(score_ref[pl.ds(pl.multiple_of(c * KB, KB), KB), :] - top)
        total = total + fold(jnp.sum, weights)
        low_weights = weights.astype(bf16)
        values = v_ref[pl.ds(start, KB), :]
        new_accs = []
        for p, acc in enumerate(accs):
            lanes, place = pair_slices(p)
            new_accs.append(acc + dot(values[:, lanes], low_weights[:, place], TN))
        return total, tuple(new_accs)

    zeros = tuple(jnp.zeros((2 * HD, 2 * QB), f32) for _ in range(pairs))
    total, accs = by_twos(count, second, (jnp.zeros((8, width), f32), zeros))
    total = jnp.sum(total, axis=0, keepdims=True)
    mixed = untangle([acc / total[:, pair_slices(p)[1]] for p, acc in enumerate(accs)])
    wide_ref[...] = mixed
    o_ref[...] = mixed.astype(bf16)
    lse_ref[0] = top + jnp.log(total)

    @pl.when(block == 0)
    def _():
        top_ref[0] = top

    @pl.when(block != 0)
    def _():
        top_ref[0] = jnp.maximum(top_ref[0], top)


def attend_back_kernel(
    low_ref,
    count_ref,
    key_ids_ref,
    query_ids_ref,
    q_ref,
    k_ref,
    v_ref,
    do_ref,
    o_ref,
    lse_ref,
    dq_ref,
    dk_ref,
    dv_ref,
    sums_ref,
    bias_ref,
    dk_acc,
    dv_acc,
):
    pair, block = pl.program_id(0), pl.program_id(1)
    low, count = low_ref[block], count_ref[block]

    @pl.when(pair == 0)
    def _():
        fill_bias(bias_ref, key_ids_ref, query_ids_ref, block, low, count)

    @pl.when(block == 0)
    def _():
        dk_acc[...] = jnp.zeros_like(dk_acc)
        dv_acc[...] = jnp.zeros_like(dv_acc)

    queries = by_head(q_ref[...] * jnp.asarray(SCALE, bf16))
    grads = by_head(do_ref[...])
    product = (do_ref[...].astype(f32) * o_ref[...]).T
    inner = jnp.concatenate(
        [jnp.sum(product[i * HD : (i + 1) * HD], axis=0, keepdims=True) for i in range(HEADS)], axis=1
    )
    log_sum = lse_ref[0]
    pairs = HEADS // 2

    def step(c, accs):
        start = pl.multiple_of(low + c * KB, 128)
        keys = k_ref[pl.ds(start, KB), :]
        bias = bias_ref[block, pl.ds(pl.multiple_of(c * KB, KB), KB), :]
        scores = dot(keys, queries, NT) + widen(bias)
        probs = jnp.exp(scores - log_sum)
        prob_grad = dot(v_ref[pl.ds(start, KB), :], grads, NT)
        score_grad = (probs * (prob_grad - inner)).astype(bf16)
        dv_acc[pl.ds(start, KB), :] += dot(probs.astype(bf16), grads, NN)
        dk_acc[pl.ds(start, KB), :] += dot(score_grad, queries, NN)
        new_accs = []
        for p, acc in enumerate(accs):
            lanes, place = pair_slices(p)
            new_accs.append(acc + dot(keys[:, lanes], score_grad[:, place], TN))
        return tuple(new_accs)

    zeros = tuple(jnp.zeros((2 * HD, 2 * QB), f32) for _ in range(pairs))
    dq = (untangle(by_twos(count, step, zeros)) * SCALE).astype(bf16)
    dq_ref[...] = dq
    dq_sum = jnp.sum(dq.astype(f32), axis=0, keepdims=True)

    @pl.when(block == 0)
    def _():
        sums_ref[0:1, :] = dq_sum

    @pl.when(block != 0)
    def _():
        sums_ref[0:1, :] += dq_sum

    @pl.when(block == pl.num_programs(1) - 1)
    def _():
        dk_ref[...] = dk_acc[...].astype(bf16)
        dv = dv_acc[...].astype(bf16)
        dv_ref[...] = dv
        sums_ref[1:2, :] = jnp.sum(dv.astype(f32), axis=0, keepdims=True)


def key_ranges(own_ids, near_ids, blocks):
    rows, near = own_ids.shape[0], near_ids.shape[0]
    size = rows // blocks
    place = jnp.arange(near, dtype=jnp.int32)[None, :]
    first = own_ids[0::size][:, None]
    last = own_ids[size - 1 :: size][:, None]
    low = jnp.min(jnp.where(near_ids[None, :] == first, place, near), axis=1)
    high = jnp.max(jnp.where(near_ids[None, :] == last, place, -1), axis=1) + 1
    low = low // 128 * 128
    count = (high - low + KB - 1) // KB
    low = jnp.minimum(low, near - count * KB)
    return low.astype(jnp.int32), count.astype(jnp.int32)


def attention_specs(rows, near, blocks):
    groups = H // HEADS
    span = HEADS * HD
    most = -(-(QB + 2 * RIM + 127) // KB) * KB
    assert most <= near and rows % QB == 0 and near % 128 == 0
    own = pl.BlockSpec((QB, span), lambda p, b, *_: (b, p))
    base = [
        pl.BlockSpec((near, 1), lambda p, b, *_: (0, 0)),
        pl.BlockSpec((1, QB), lambda p, b, *_: (0, b)),
        own,
        pl.BlockSpec((near, span), lambda p, b, *_: (0, p)),
        pl.BlockSpec((near, span), lambda p, b, *_: (0, p + groups)),
    ]
    row = pl.BlockSpec((1, 1, HEADS * QB), lambda p, b, *_: (p, 0, b))
    bias = pltpu.VMEM((blocks, most, QB), f32)
    return groups, own, base, row, bias


def attend(ranges, key_ids, query_ids, queries, near_kv):
    rows, near = queries.shape[0], near_kv.shape[0]
    blocks = rows // QB
    groups, own, base, row, bias = attention_specs(rows, near, blocks)
    top = pl.BlockSpec((1, 1, HEADS * QB), lambda p, b, *_: (p, 0, 0))
    return pl.pallas_call(
        attend_kernel,
        grid_spec=pltpu.PrefetchScalarGridSpec(
            num_scalar_prefetch=2,
            grid=(groups, blocks),
            in_specs=base,
            out_specs=[own, own, row, top],
            scratch_shapes=[bias, pltpu.VMEM((bias.shape[1], HEADS * QB), f32)],
        ),
        out_shape=[
            jax.ShapeDtypeStruct(queries.shape, bf16),
            jax.ShapeDtypeStruct(queries.shape, f32),
            jax.ShapeDtypeStruct((groups, 1, HEADS * rows), f32),
            jax.ShapeDtypeStruct((groups, 1, HEADS * QB), f32),
        ],
        compiler_params=pltpu.CompilerParams(vmem_limit_bytes=56 << 20),
        cost_estimate=cost(rows * H * HD * 850 * 16),
        name="attend",
    )(*ranges, key_ids, query_ids, queries, near_kv, near_kv)


def attend_back(ranges, key_ids, query_ids, queries, near_kv, mixed_grad, mixed, log_sums):
    rows, near = queries.shape[0], near_kv.shape[0]
    blocks = rows // QB
    groups, own, base, row, bias = attention_specs(rows, near, blocks)
    wide = pl.BlockSpec((near, HEADS * HD), lambda p, b, *_: (0, p))
    return pl.pallas_call(
        attend_back_kernel,
        grid_spec=pltpu.PrefetchScalarGridSpec(
            num_scalar_prefetch=2,
            grid=(groups, blocks),
            in_specs=base + [own, own, row],
            out_specs=[own, wide, wide, pl.BlockSpec((2, HEADS * HD), lambda p, b, *_: (0, p))],
            scratch_shapes=[bias, pltpu.VMEM((near, HEADS * HD), f32), pltpu.VMEM((near, HEADS * HD), f32)],
        ),
        out_shape=[
            jax.ShapeDtypeStruct(queries.shape, bf16),
            jax.ShapeDtypeStruct((near, queries.shape[1]), bf16),
            jax.ShapeDtypeStruct((near, queries.shape[1]), bf16),
            jax.ShapeDtypeStruct((2, queries.shape[1]), f32),
        ],
        compiler_params=pltpu.CompilerParams(vmem_limit_bytes=56 << 20),
        cost_estimate=cost(rows * H * HD * 850 * 32),
        name="attend_back",
    )(*ranges, key_ids, query_ids, queries, near_kv, near_kv, mixed_grad, mixed, log_sums)


def spot_of(place, half):
    spot, bit = 0, half
    while bit:
        spot = spot + (place & 1) * bit
        place, bit = place >> 1, bit >> 1
    return spot


def mlp_kernel(
    a_ref, dz_ref, x_ref, rb_ref, eb_ref, we_ref, wr_ref,
    y_ref, da_ref, ebg_ref, sum_ref,
    act_ref, du_ref, rg_ref, eg_ref, sems,
):
    j = pl.program_id(0)
    rows, width = a_ref.shape
    tile = 256

    def copies(step):
        d, r, _ = rg_ref.shape
        g, e, _ = eg_ref.shape
        fold = pl.num_programs(0)
        return (
            pltpu.make_async_copy(rg_ref, sum_ref.at[pl.ds(step * d, d), pl.ds(0, r), :], sems.at[0]),
            pltpu.make_async_copy(eg_ref, sum_ref.at[:, pl.ds(r + step * e, e), :], sems.at[1]),
        )

    @pl.when(j == 0)
    def _():
        y_ref[...] = x_ref[...] + rb_ref[...]
        da_ref[...] = jnp.zeros_like(da_ref)

    ebg_ref[...] = jnp.zeros_like(ebg_ref)

    def by_rows(r, carry):
        at = pl.ds(pl.multiple_of(r * tile, tile), tile)
        we = we_ref[...].reshape(width, width)
        wr = wr_ref[...].reshape(width, width)
        hidden = dot(a_ref[at, :], we, NN) + eb_ref[...]
        back = dot(dz_ref[at, :], wr, NT)
        sigma = jax.nn.sigmoid(GELU_COEF * hidden)
        act = (hidden * sigma).astype(bf16)
        act_ref[at, :] = act
        du = (back * (sigma + GELU_COEF * hidden * sigma * (1.0 - sigma))).astype(bf16)
        du_ref[at, :] = du
        ebg_ref[...] += jnp.sum(du.astype(f32), axis=0, keepdims=True)
        y_ref[at, :] += dot(act, wr, NN)
        da_ref[at, :] += dot(du, we, NT)
        return carry

    lax.fori_loop(0, rows // tile, by_rows, 0)

    @pl.when(j > 0)
    def _():
        for copy in copies(j - 1):
            copy.wait()

    def by_columns(t, carry):
        at = pl.ds(pl.multiple_of(t * tile, tile), tile)
        rg = dot(act_ref[:, at], dz_ref[...], TN).astype(bf16)
        n = tile // rg_ref.shape[1]
        rg_ref[pl.ds(t * n, n)] = rg.reshape(n, rg_ref.shape[1], width)
        eg = dot(a_ref[:, at], du_ref[...], TN).astype(bf16)
        n = tile // eg_ref.shape[1]
        eg_ref[pl.ds(t * n, n)] = eg.reshape(n, eg_ref.shape[1], width)
        return carry

    lax.fori_loop(0, width // tile, by_columns, 0)
    for copy in copies(j):
        copy.start()

    @pl.when(j == pl.num_programs(0) - 1)
    def _():
        for copy in copies(j):
            copy.wait()


def mlp(normed, branch_grad, middle, bias_reduce, bias_expand, packed, sum_rows):
    rows, width = normed.shape
    ff = bias_expand.shape[1]
    fold = ff // width
    groups = packed.shape[0]
    each = width // groups
    whole = lambda j: (0, 0)
    one = pl.Buffered(1)
    return pl.pallas_call(
        mlp_kernel,
        grid=(fold,),
        in_specs=[
            pl.BlockSpec((rows, width), whole, pipeline_mode=one),
            pl.BlockSpec((rows, width), whole, pipeline_mode=one),
            pl.BlockSpec((rows, width), whole, pipeline_mode=one),
            pl.BlockSpec((1, width), whole),
            pl.BlockSpec((1, width), lambda j: (0, j)),
            pl.BlockSpec((groups, each, width), lambda j: (0, fold + j, 0)),
            pl.BlockSpec((groups // fold, fold * each, width), lambda j: (j, 0, 0)),
        ],
        out_specs=[
            pl.BlockSpec((rows, width), whole),
            pl.BlockSpec((rows, width), whole),
            pl.BlockSpec((1, width), lambda j: (0, j)),
            pl.BlockSpec(memory_space=pl.ANY),
        ],
        out_shape=[
            jax.ShapeDtypeStruct((rows, width), f32),
            jax.ShapeDtypeStruct((rows, width), f32),
            jax.ShapeDtypeStruct((1, ff), f32),
            jax.ShapeDtypeStruct((groups, sum_rows, width), bf16),
        ],
        scratch_shapes=[
            pltpu.VMEM((rows, width), bf16),
            pltpu.VMEM((rows, width), bf16),
            pltpu.VMEM((groups // fold, fold * each, width), bf16),
            pltpu.VMEM((groups, each, width), bf16),
            pltpu.SemaphoreType.DMA((2,)),
        ],
        compiler_params=pltpu.CompilerParams(vmem_limit_bytes=58 << 20),
        cost_estimate=cost(12 * rows * width * ff),
        name="mlp",
    )(normed, branch_grad, middle, bias_reduce, bias_expand, packed, packed)


def middle_back_kernel(
    me_ref, da_ref, x_ref, og_ref, gain_ref, mixed_ref, wo_ref,
    grad_ref, mg_ref, keep_ref, send_ref, sums_ref, ag_ref,
):
    i = pl.program_id(0)
    tile, width = da_ref.shape
    steps = pl.num_programs(0) // 2
    half, each, _ = keep_ref.shape

    @pl.when(i == 0)
    def _():
        sums_ref[...] = jnp.zeros_like(sums_ref)

    @pl.when(i < steps)
    def _():
        normal, inv_std = norm_stats(x_ref[...])
        da = da_ref[...]
        grad = og_ref[...] + norm_back(da, gain_ref[...], normal, inv_std)
        grad_ref[...] = grad
        low = grad.astype(bf16)
        ag_ref[pl.ds(pl.multiple_of(i * tile, tile), tile), :] = low
        mg_ref[...] = dot(low, wo_ref[...].reshape(width, width), NT).astype(bf16)
        sums_ref[0:1, :] += jnp.sum(low.astype(f32), axis=0, keepdims=True)
        sums_ref[1:2, :] += jnp.sum(da * normal, axis=0, keepdims=True)
        sums_ref[2:3, :] += jnp.sum(da, axis=0, keepdims=True)

    @pl.when(i >= steps)
    def _():
        t = i - steps
        size = width // steps
        at = pl.ds(pl.multiple_of(t * size, size), size)
        out = dot(mixed_ref[:, at], ag_ref[...], TN).astype(bf16)
        n = size // each
        for k in range(n):
            spot = spot_of((t * n + k) ^ me_ref[0], half)
            block = out[k * each : (k + 1) * each]

            @pl.when(spot < half)
            def _():
                keep_ref[spot] = block

            @pl.when(spot >= half)
            def _():
                send_ref[spot - half] = block


def middle_back(normed_grad, middle, out_grad, gain, mixed, packed, last, place):
    rows, width = middle.shape
    groups = packed.shape[0]
    each = width // groups
    tile = rows // 4
    whole = lambda i, *_: (0, 0)
    by_rows = pl.BlockSpec((tile, width), lambda i, *_: (jnp.minimum(i, 3), 0))
    side = pl.BlockSpec((groups // 2, each, width), lambda i, *_: (0, 0, 0))
    half = jax.ShapeDtypeStruct((groups // 2, each, width), bf16)
    return pl.pallas_call(
        middle_back_kernel,
        grid_spec=pltpu.PrefetchScalarGridSpec(
            num_scalar_prefetch=1,
            grid=(8,),
            in_specs=[
                by_rows,
                by_rows,
                by_rows,
                pl.BlockSpec((1, width), whole),
                pl.BlockSpec((rows, width), whole),
                pl.BlockSpec((groups, each, width), lambda i, *_: (0, last, 0)),
            ],
            out_specs=[by_rows, by_rows, side, side, pl.BlockSpec((3, width), whole)],
            scratch_shapes=[pltpu.VMEM((rows, width), bf16)],
        ),
        out_shape=[
            jax.ShapeDtypeStruct((rows, width), f32),
            jax.ShapeDtypeStruct((rows, width), bf16),
            half,
            half,
            jax.ShapeDtypeStruct((3, width), f32),
        ],
        compiler_params=pltpu.CompilerParams(vmem_limit_bytes=56 << 20),
        cost_estimate=cost(4 * rows * width * width),
        name="middle_back",
    )(place, normed_grad, middle, out_grad, gain, mixed, packed)


def middle_kernel(mixed_ref, wo_ref, x_ref, bo_ref, gain_ref, bias_ref, out_ref, low_ref):
    width = x_ref.shape[1]
    middle = x_ref[...] + dot(mixed_ref[...], wo_ref[...].reshape(width, width), NN) + bo_ref[...]
    out_ref[...] = middle
    low_ref[...] = (norm_stats(middle)[0] * gain_ref[...] + bias_ref[...]).astype(bf16)


def middle_forward(mixed, packed, tokens, bias_output, gain, bias, last):
    rows, width = tokens.shape
    groups = packed.shape[0]
    by_rows = pl.BlockSpec((rows // 4, width), lambda i: (i, 0))
    vector = pl.BlockSpec((1, width), lambda i: (0, 0))
    return pl.pallas_call(
        middle_kernel,
        grid=(4,),
        in_specs=[
            by_rows,
            pl.BlockSpec((groups, width // groups, width), lambda i: (0, last, 0)),
            by_rows,
            vector,
            vector,
            vector,
        ],
        out_specs=[by_rows, by_rows],
        out_shape=[jax.ShapeDtypeStruct((rows, width), f32), jax.ShapeDtypeStruct((rows, width), bf16)],
        compiler_params=pltpu.CompilerParams(vmem_limit_bytes=56 << 20),
        cost_estimate=cost(2 * rows * width * width),
        name="middle",
    )(mixed, packed, tokens, bias_output, gain, bias)


def assemble(me, parts, w_ref):
    each, half = parts[0].shape[1:]
    for core, (left, right) in enumerate(((parts[0], parts[2]), (parts[1], parts[3]))):
        for spot in range(16):
            high, low, z8, z16 = spot >> 3 & 1, spot >> 2 & 1, spot >> 1 & 1, spot & 1
            z = z8 * 8 + z16 * 16 + core
            for ref, owner, lanes in (
                (left, z + high * 4 + low * 2, slice(0, half)),
                (right, z + high * 2 + low * 4, slice(half, 2 * half)),
            ):
                w_ref[pl.ds(pl.multiple_of((owner ^ me) * each, each), each), lanes] = ref[spot]


def part_specs(width):
    each = width // 32
    return [pl.BlockSpec((16, each, width // 2), lambda j, *_: (0, j, 0)) for _ in range(4)]


def qkv_kernel(me_ref, a_ref, p0, p1, p2, p3, bias_ref, q_ref, kv_ref, w_ref):
    j = pl.program_id(0)
    assemble(me_ref[0], (p0, p1, p2, p3), w_ref)
    near, width = a_ref.shape
    rows = q_ref.shape[0]
    rim = (near - rows) // 2

    @pl.when(j == 0)
    def _():
        def step(t, carry):
            source = pl.ds(pl.multiple_of(rim + t * 256, 8), 256)
            w = w_ref[...]
            q_ref[pl.ds(pl.multiple_of(t * 256, 256), 256), :] = (
                dot(a_ref[source, :], w, NN) + bias_ref[...]
            ).astype(bf16)
            return carry

        lax.fori_loop(0, rows // 256, step, 0)

    @pl.when(j > 0)
    def _():
        size = near // 8

        def step(t, carry):
            at = pl.ds(pl.multiple_of(t * size, 16), size)
            w = w_ref[...]
            kv_ref[at, :] = (dot(a_ref[at, :], w, NN) + bias_ref[...]).astype(bf16)
            return carry

        lax.fori_loop(0, near // size, step, 0)


def project(normed_near, parts, biases, rows, place):
    near, width = normed_near.shape
    return pl.pallas_call(
        qkv_kernel,
        grid_spec=pltpu.PrefetchScalarGridSpec(
            num_scalar_prefetch=1,
            grid=(3,),
            in_specs=[pl.BlockSpec((near, width), lambda j, *_: (0, 0))]
            + part_specs(width)
            + [pl.BlockSpec((1, width), lambda j, *_: (0, j))],
            out_specs=[
                pl.BlockSpec((rows, width), lambda j, *_: (0, 0)),
                pl.BlockSpec((near, width), lambda j, *_: (0, jnp.maximum(j - 1, 0))),
            ],
            scratch_shapes=[pltpu.VMEM((width, width), bf16)],
        ),
        out_shape=[
            jax.ShapeDtypeStruct((rows, width), bf16),
            jax.ShapeDtypeStruct((near, 2 * width), bf16),
        ],
        compiler_params=pltpu.CompilerParams(vmem_limit_bytes=56 << 20),
        cost_estimate=cost(2 * width * width * (rows + 2 * near)),
        name="qkv",
    )(place, normed_near, *parts, biases)


def qkv_grads_kernel(me_ref, a_ref, dq_ref, dk_hbm, dv_hbm, keep_ref, send_ref, dk_ref, dv_ref, sems):
    j = pl.program_id(0)
    near, width = a_ref.shape
    rows = dq_ref.shape[0]
    rim = (near - rows) // 2
    tile = 256
    half, each, _ = keep_ref.shape
    n = tile // each

    def fill(grad_ref, source):
        def step(t, carry):
            at = pl.ds(pl.multiple_of(t * tile, tile), tile)
            out = dot(a_ref[source, at], grad_ref[...], TN).astype(bf16)
            for i in range(n):
                spot = spot_of((t * n + i) ^ me_ref[0], half)
                block = out[i * each : (i + 1) * each]

                @pl.when(spot < half)
                def _():
                    keep_ref[spot] = block

                @pl.when(spot >= half)
                def _():
                    send_ref[spot - half] = block

            return carry

        lax.fori_loop(0, width // tile, step, 0)

    keys = pltpu.make_async_copy(dk_hbm, dk_ref, sems.at[0])
    values = pltpu.make_async_copy(dv_hbm, dv_ref, sems.at[1])

    @pl.when(j == 0)
    def _():
        keys.start()
        values.start()
        fill(dq_ref, slice(rim, rim + rows))

    @pl.when(j == 1)
    def _():
        keys.wait()
        fill(dk_ref, slice(0, near))

    @pl.when(j == 2)
    def _():
        values.wait()
        fill(dv_ref, slice(0, near))


def qkv_grads(normed_near, query_grad, key_near, value_near, groups, place):
    near, width = normed_near.shape
    rows = query_grad.shape[0]
    each = width // groups
    whole = lambda j, *_: (0, 0)
    half = jax.ShapeDtypeStruct((groups // 2, 3 * each, width), bf16)
    out = pl.BlockSpec((groups // 2, each, width), lambda j, *_: (0, j, 0))
    return pl.pallas_call(
        qkv_grads_kernel,
        grid_spec=pltpu.PrefetchScalarGridSpec(
            num_scalar_prefetch=1,
            grid=(3,),
            in_specs=[
                pl.BlockSpec((near, width), whole),
                pl.BlockSpec((rows, width), whole),
                pl.BlockSpec(memory_space=pl.ANY),
                pl.BlockSpec(memory_space=pl.ANY),
            ],
            out_specs=[out, out],
            scratch_shapes=[
                pltpu.VMEM((near, width), bf16),
                pltpu.VMEM((near, width), bf16),
                pltpu.SemaphoreType.DMA((2,)),
            ],
        ),
        out_shape=[half, half],
        compiler_params=pltpu.CompilerParams(vmem_limit_bytes=56 << 20),
        cost_estimate=cost(2 * width * width * (rows + 2 * near)),
        name="qkv_grads",
    )(place, normed_near, query_grad, key_near, value_near)


def plus(a, b):
    return (a.astype(f32) + b.astype(f32)).astype(bf16)


def swap(value, bit):
    peers = lax.axis_size("dev")
    return lax.ppermute(value, "dev", [(i, i ^ bit) for i in range(peers)])


def merge(totals, bits, *beside):
    others = [swap(totals, bit) for bit in bits]
    out = lax.optimization_barrier((*beside, *others))
    beside, others = out[: len(beside)], out[len(beside) :]
    for other in others:
        totals = jnp.concatenate([totals[:-1] + other[:-1], jnp.maximum(totals[-1:], other[-1:])], axis=0)
    return totals, *beside


class Halving:
    def __init__(self, first, second):
        def split(pair):
            return [v.reshape((2, 2, 4) + v.shape[1:]) for v in pair]

        (keep, other), (keep_o, other_o) = split(first), split(second)
        half = (keep.shape[3] + keep_o.shape[3]) // 2

        def side_a(at):
            return plus(keep[at][..., :half, :], other[at][..., :half, :])

        def side_b(at):
            return jnp.concatenate(
                [plus(keep[at][..., half:, :], other[at][..., half:, :]), plus(keep_o[at], other_o[at])], axis=-2
            )

        self.sides = side_a(1), side_b((slice(None), 1))
        self.keeps = lambda: (side_a(0), side_b((slice(None), 0)))

    def start(self, *after):
        to_x, to_y, *after = lax.optimization_barrier((*self.sides, *after))
        self.others = swap(to_x, 2), swap(to_y, 4)
        return after

    def finish(self, totals, *beside):
        (from_x, from_y), (keep_x, keep_y) = self.others, self.keeps()
        to_y, to_x = plus(keep_x[1], from_x[1]), plus(keep_y[1], from_y[1])
        to_x, to_y, totals = lax.optimization_barrier((to_x, to_y, totals))
        second_y, second_x = swap(to_y, 4), swap(to_x, 2)
        totals, second_y, second_x = merge(totals, (1, 2, 3), second_y, second_x)
        keep_x = plus(keep_x[0], from_x[0])
        keep_y = plus(keep_y[0], from_y[0])
        send = jnp.concatenate([plus(keep_x[2:], second_y[2:]), plus(keep_y[2:], second_x[2:])], axis=1)
        send, totals = lax.optimization_barrier((send, totals))
        low = swap(send, 8)
        totals, low, *beside = merge(totals, (4, 8, 12), low, *beside)
        keep = jnp.concatenate([plus(keep_x[:2], second_y[:2]), plus(keep_y[:2], second_x[:2])], axis=1)
        send, totals = lax.optimization_barrier((plus(keep[1], low[1]), totals))
        last = swap(send, 16)
        totals, last = merge(totals, (16,), last)
        return plus(keep[0], low[0]).astype(f32) + last.astype(f32), totals, *beside


def plain(pairs, part):
    groups = 2 * pairs[0][0].shape[0]
    order = [int(f"{i:05b}"[::-1], 2) for i in range(groups)]
    joined = jnp.concatenate([jnp.concatenate(pair, axis=0) for pair in pairs], axis=1)
    joined = jnp.stack([joined[i] for i in order])
    return scatter(joined, [part] * (joined.shape[1] * groups // joined.shape[2])).astype(f32)


def normed_grad_kernel(
    me_ref, dq_ref, dk_hbm, dv_hbm, p0, p1, p2, p3, normal_hbm, nb_hbm, na_hbm,
    own_ref, before_ref, after_ref, sums_ref,
    acc_b, acc_a, dk_ref, dv_ref, normal_ref, nb_ref, na_ref, sems, w_ref,
):
    j = pl.program_id(0)
    assemble(me_ref[0], (p0, p1, p2, p3), w_ref)
    rows, width = own_ref.shape
    rim = before_ref.shape[0]

    pairs = ((dk_hbm, dk_ref), (dv_hbm, dv_ref), (normal_hbm, normal_ref), (nb_hbm.at[pl.ds(0, rim)], nb_ref), (na_hbm.at[pl.ds(0, rim)], na_ref))
    loads = [pltpu.make_async_copy(source, target, sems.at[i]) for i, (source, target) in enumerate(pairs)]

    def by_rows(total, size, act):
        def step(t, carry):
            act(pl.multiple_of(t * size, size))
            return carry

        lax.fori_loop(0, total // size, step, 0)

    def near(grad_ref, first):
        def add(out_ref, base, size):
            def act(at):
                w = w_ref[...]
                part = dot(grad_ref[pl.ds(pl.multiple_of(base + at, 8), size), :], w, NT)
                spot = pl.ds(at, size)
                out_ref[spot, :] = part if first else out_ref[spot, :] + part

            return act

        by_rows(rim, rim // 2, add(acc_b, 0, rim // 2))
        by_rows(rim, rim // 2, add(acc_a, rim + rows, rim // 2))

        def act(at):
            w = w_ref[...]
            own_ref[pl.ds(at, 256), :] += dot(grad_ref[pl.ds(pl.multiple_of(rim + at, 8), 256), :], w, NT)

        by_rows(rows, 256, act)

    @pl.when(j == 0)
    def _():
        for load in loads:
            load.start()

        def act(at):
            spot = pl.ds(at, 256)
            w = w_ref[...]
            grads = dq_ref[spot, :]
            own_ref[spot, :] = dot(grads, w, NT)

        by_rows(rows, 256, act)

    @pl.when(j == 1)
    def _():
        loads[0].wait()
        near(dk_ref, True)

    @pl.when(j == 2)
    def _():
        for load in loads[1:]:
            load.wait()
        near(dv_ref, False)

        def finish(source, normal, out, carry):
            def step(t, carry):
                gain_sum, bias_sum = carry
                spot = pl.ds(pl.multiple_of(t * 16, 16), 16)
                value = source[spot, :]
                product = value * normal[spot, :].astype(f32)
                if out is not None:
                    out[spot, :] = value.astype(bf16)
                return gain_sum + product[:8] + product[8:], bias_sum + value[:8] + value[8:]

            return lax.fori_loop(0, source.shape[0] // 16, step, carry)

        carry = (jnp.zeros((8, width), f32), jnp.zeros((8, width), f32))
        carry = finish(acc_b, nb_ref, before_ref, carry)
        carry = finish(acc_a, na_ref, after_ref, carry)
        gain_sum, bias_sum = finish(own_ref, normal_ref, None, carry)
        sums_ref[0:1, :] = jnp.sum(gain_sum, axis=0, keepdims=True)
        sums_ref[1:2, :] = jnp.sum(bias_sum, axis=0, keepdims=True)


def project_back(query_grad, key_near, value_near, parts, normal, before, after, place):
    rows, width = query_grad.shape
    near = key_near.shape[0]
    rim = (near - rows) // 2
    whole = lambda j, *_: (0, 0)
    anywhere = pl.BlockSpec(memory_space=pl.ANY)
    return pl.pallas_call(
        normed_grad_kernel,
        grid_spec=pltpu.PrefetchScalarGridSpec(
            num_scalar_prefetch=1,
            grid=(3,),
            in_specs=[pl.BlockSpec((rows, width), whole, pipeline_mode=pl.Buffered(1)), anywhere, anywhere]
            + part_specs(width)
            + [anywhere, anywhere, anywhere],
            out_specs=[
                pl.BlockSpec((rows, width), whole),
                pl.BlockSpec((rim, width), whole),
                pl.BlockSpec((rim, width), whole),
                pl.BlockSpec((2, width), whole),
            ],
            scratch_shapes=[
                pltpu.VMEM((rim, width), f32),
                pltpu.VMEM((rim, width), f32),
                pltpu.VMEM((near, width), bf16),
                pltpu.VMEM((near, width), bf16),
                pltpu.VMEM((rows, width), f32),
                pltpu.VMEM((rim, width), bf16),
                pltpu.VMEM((rim, width), bf16),
                pltpu.SemaphoreType.DMA((5,)),
                pltpu.VMEM((width, width), bf16),
            ],
        ),
        out_shape=[
            jax.ShapeDtypeStruct((rows, width), f32),
            jax.ShapeDtypeStruct((rim, width), bf16),
            jax.ShapeDtypeStruct((rim, width), bf16),
            jax.ShapeDtypeStruct((2, width), f32),
        ],
        compiler_params=pltpu.CompilerParams(vmem_limit_bytes=58 << 20),
        cost_estimate=cost(2 * width * width * (rows + 2 * near)),
        name="normed_grad",
    )(place, query_grad, key_near, value_near, *parts, normal, before, after)


def gather(value, segments, groups):
    peers = lax.axis_size("dev")
    rows, width = value.shape
    whole = lax.all_gather(value, "dev", axis=0, tiled=True)
    sub = peers // groups
    if sub == 1:
        return whole.reshape(groups, rows, width)
    whole = whole.reshape(groups, sub, rows, width)
    parts, at = [], 0
    for size in segments:
        parts.append(whole[:, :, at : at + size].reshape(groups, sub * size, width))
        at += size
    return jnp.concatenate(parts, axis=1)


def scatter(value, segments):
    peers = lax.axis_size("dev")
    groups, rows, width = value.shape
    sub = peers // groups
    if sub > 1:
        parts, at = [], 0
        for size in segments:
            cut = value[:, at : at + sub * size]
            parts.append(cut.reshape(groups, sub, size, width))
            at += sub * size
        value = jnp.concatenate(parts, axis=2)
    value = value.reshape(peers * sum(segments), width)
    return lax.psum_scatter(value, "dev", scatter_dimension=0, tiled=True)


def pack_kernel(me_ref, q_ref, k_ref, v_ref, small_ref, r_ref, e_ref, o_ref, eb_ref, one_ref, two_ref):
    part, width = q_ref.shape
    for i, ref in enumerate((q_ref, k_ref, v_ref)):
        one_ref[i * part : (i + 1) * part, :] = ref[...].astype(bf16)

    def place(value, size):
        index = lax.broadcasted_iota(jnp.int32, value.shape, 0) * width
        index = index + lax.broadcasted_iota(jnp.int32, value.shape, 1)
        return jnp.where(index // size == me_ref[0], value, jnp.zeros_like(value))

    row = lax.broadcasted_iota(jnp.int32, (part, width), 0)
    column = lax.broadcasted_iota(jnp.int32, (part, width), 1)
    pick = jnp.where(column - me_ref[0] * part == row, 1.0, 0.0).astype(bf16)
    one_ref[3 * part :, :] = dot(small_ref[...].astype(bf16), pick, NN).astype(bf16)
    rows = r_ref.shape[0]
    fold = rows // part
    two_ref[:rows, :] = r_ref[...].astype(bf16)
    for i in range(fold):
        at = rows + i * part
        two_ref[at : at + part, :] = e_ref[:, i * width : (i + 1) * width].astype(bf16)
    at = rows + fold * part
    two_ref[at : at + part, :] = o_ref[...].astype(bf16)
    bias = jnp.concatenate([eb_ref[...]] * (width // eb_ref.shape[1]), axis=1)
    two_ref[at + part :, :] = place(jnp.broadcast_to(bias, (8, width)), fold * part).astype(bf16)


def pack(me, mats, smalls, reduce_mat, expand_mat, output_mat, expand_bias):
    part, width = output_mat.shape
    tiled = jnp.stack(smalls)
    bias = expand_bias[None]
    rows = reduce_mat.shape[0]
    return pl.pallas_call(
        pack_kernel,
        grid_spec=pltpu.PrefetchScalarGridSpec(
            num_scalar_prefetch=1,
            grid=(1,),
            in_specs=[
                pl.BlockSpec(v.shape, lambda i, *_: (0, 0))
                for v in (*mats, tiled, reduce_mat, expand_mat, output_mat, bias)
            ],
            out_specs=[
                pl.BlockSpec((3 * part + 8, width), lambda i, *_: (0, 0)),
                pl.BlockSpec((2 * rows + part + 8, width), lambda i, *_: (0, 0)),
            ],
        ),
        out_shape=[
            jax.ShapeDtypeStruct((3 * part + 8, width), bf16),
            jax.ShapeDtypeStruct((2 * rows + part + 8, width), bf16),
        ],
        name="pack",
    )(jnp.full((1,), me, jnp.int32), *mats, tiled, reduce_mat, expand_mat, output_mat, bias)


def doubling(value, tokens, packed, exchange, prepare):
    rows, width = value.shape
    half = width // 2
    grown = value[None]
    grown = jnp.concatenate([grown, swap(grown, 16)])
    grown, tokens = lax.optimization_barrier((grown, tokens))
    other = swap(grown, 8)
    near = exchange(tokens)
    grown, other, packed, *near = lax.optimization_barrier((grown, other, packed, *near))
    a = jnp.concatenate([grown[..., :half], other[..., :half]])
    b = jnp.concatenate([grown[..., half:], other[..., half:]])
    from_x, from_y = swap(a, 2), swap(b, 4)
    a, b = jnp.concatenate([a, from_x]), jnp.concatenate([b, from_y])
    from_y, from_x = swap(a, 4), swap(b, 2)
    prepared = prepare(*near)
    a, b = jnp.concatenate([a, from_y]), jnp.concatenate([b, from_x])
    a, b, *prepared = lax.optimization_barrier((a, b, *prepared))
    return (a, swap(a, 1), b, swap(b, 1)), prepared, packed


def fold_smalls(natural, sub):
    at = natural.shape[1] - 8 * sub
    tail = natural[:, at:].reshape(natural.shape[0], sub, 8, natural.shape[2])
    tail = jnp.sum(tail.astype(f32), axis=1).astype(natural.dtype)
    return jnp.concatenate([natural[:, :at], tail], axis=1)


def as_doubled(natural):
    half = natural.shape[2] // 2
    out = []
    for cut, orders in ((slice(0, half), (4, 2)), (slice(half, None), (2, 4))):
        for core in (0, 1):
            picks = []
            for spot in range(16):
                high, low, z8, z16 = spot >> 3 & 1, spot >> 2 & 1, spot >> 1 & 1, spot & 1
                picks.append(natural[z8 * 8 + z16 * 16 + core + high * orders[0] + low * orders[1], :, cut])
            out.append(jnp.stack(picks))
    return tuple(out)


def spread(vector, width):
    peers, me = lax.axis_size("dev"), lax.axis_index("dev")
    size = vector.shape[0]
    place = jnp.arange(peers * size, dtype=jnp.int32) // size
    full = jnp.where(place == me, jnp.tile(vector, peers), jnp.zeros((), vector.dtype))
    return full.reshape(-1, width)


def local(
    tokens_in,
    attn_gain,
    attn_bias,
    query_mat,
    query_bias,
    key_mat,
    value_mat,
    value_bias,
    output_mat,
    output_bias,
    mlp_gain,
    mlp_bias,
    expand_mat,
    expand_bias,
    reduce_mat,
    reduce_bias,
    image_ids,
    clip_flags,
    out_grad,
):
    peers, me = lax.axis_size("dev"), lax.axis_index("dev")
    rows, width = tokens_in.shape
    part = query_mat.shape[0]
    ff = expand_mat.shape[1]
    fold = ff // width
    groups = min(peers, 32)
    sub = peers // groups

    paired = peers == 32
    up = [(i, i + 1) for i in range(peers - 1)]
    down = [(i + 1, i) for i in range(peers - 1)]
    own_ids = image_ids + 1
    smalls = (attn_gain, attn_bias, query_bias, value_bias, output_bias, mlp_gain, mlp_bias, reduce_bias)

    def ids_of(halo):
        return (halo[RIM, :RIM].astype(f32) * 32 + halo[RIM + 1, :RIM].astype(f32)).astype(jnp.int32)

    def exchange(tokens):
        normal_one, inv_one = norm_stats(tokens)
        normal_low = normal_one.astype(bf16)

        def with_ids(at):
            ids = jnp.pad(own_ids[at], (0, width - RIM))
            ids = [(ids // 32).astype(bf16)[None], (ids % 32).astype(bf16)[None]]
            return jnp.concatenate([normal_low[at], *ids, jnp.zeros((6, width), bf16)])

        before = lax.ppermute(with_ids(slice(rows - RIM, rows)), "dev", up)
        after = lax.ppermute(with_ids(slice(0, RIM)), "dev", down)
        return before, after, normal_one, inv_one

    def prepare(before, after, normal_one, inv_one):
        near_ids = jnp.concatenate([ids_of(before), own_ids, ids_of(after)])
        ranges = key_ranges(own_ids, near_ids, rows // QB)
        return before, after, near_ids, near_ids[:, None], own_ids[None, :], *ranges, normal_one, inv_one

    if paired:
        packed_one, packed_two = pack(
            me, (query_mat, key_mat, value_mat), smalls, reduce_mat, expand_mat, output_mat, expand_bias
        )
        first, prepared, packed_two = doubling(packed_one, tokens_in, packed_two, exchange, prepare)
        second = gather(packed_two, (), groups)
    else:
        low = [v.astype(bf16) for v in (query_mat, key_mat, value_mat)]
        packed_one = jnp.concatenate(low + [spread(v.astype(bf16), width) for v in smalls])
        first = as_doubled(fold_smalls(gather(packed_one, [part] * 3 + [8], groups), sub))
        prepared = prepare(*exchange(tokens_in))
        expand_low = expand_mat.astype(bf16)
        packed_two = jnp.concatenate(
            [reduce_mat.astype(bf16)]
            + [expand_low[:, i * width : (i + 1) * width] for i in range(fold)]
            + [output_mat.astype(bf16), spread(expand_bias.astype(bf16), width), jnp.zeros((8 - fold, width), bf16)]
        )
        second = gather(packed_two, [fold * part] + [part] * (fold + 1) + [8], groups)

    before, after, near_ids, key_ids, query_ids, *ranges, normal_one, inv_one = prepared
    vectors = jnp.concatenate(
        [
            sum(jnp.sum(v[:, 3 * width // groups :].astype(f32), axis=0) for v in first[i : i + 2])
            for i in (0, 2)
        ],
        axis=1,
    )
    (gain_one, bias_one, bias_query, bias_value, bias_output, gain_two, bias_two, bias_reduce) = [
        vectors[i : i + 1] for i in range(8)
    ]

    normed_near = jnp.concatenate(
        [(v.astype(f32) * gain_one + bias_one).astype(bf16) for v in (before[:RIM], normal_one, after[:RIM])],
        axis=0,
    )
    bias_qkv = jnp.concatenate([bias_query, jnp.zeros_like(bias_value), bias_value], axis=1)
    place = jnp.full((1,), me if paired else 0, jnp.int32)
    queries, near_kv = project(normed_near, first, bias_qkv, rows, place)
    mixed, mixed_wide, log_sums, tops = attend(ranges, key_ids, query_ids, queries, near_kv)
    head_top = jnp.max(tops.reshape(H, QB), axis=1)

    tail = second[:, (2 * fold + 1) * part * sub :].reshape(groups * sub, 8, width)
    bias_expand = jnp.sum(tail.astype(f32), axis=0)[:fold].reshape(1, ff)
    middle, normed_two = middle_forward(mixed, second, tokens_in, bias_output, gain_two, bias_two, 2 * fold)
    branch_grad = out_grad.astype(bf16)
    block_out, normed_two_grad, expand_bias_grad, sums = mlp(
        normed_two, branch_grad, middle, bias_reduce, bias_expand, second, 2 * fold * width // groups + 8
    )
    reduce_bias_grad = column_sums(branch_grad)
    first_sum = scatter(sums, [fold * part] + [part] * fold + [8 // sub])
    middle_grad, mixed_grad, *out_halves, middle_sums = middle_back(
        normed_two_grad, middle, out_grad, gain_two, mixed, second, 2 * fold, place
    )
    out_other = swap(out_halves[1], 1) if peers == 32 else None
    rest = jnp.concatenate(
        [
            middle_sums,
            reduce_bias_grad[None],
            expand_bias_grad.reshape(fold, width),
            jnp.pad(head_top, (0, width - H))[None],
        ]
    )
    mixed_grad, rest = lax.optimization_barrier((mixed_grad, rest))
    query_grad, key_near, value_near, bias_sums = attend_back(
        ranges, key_ids, query_ids, queries, near_kv, mixed_grad, mixed_wide, log_sums
    )
    halves = qkv_grads(normed_near, query_grad, key_near, value_near, groups, place)
    if paired:
        late = Halving((halves[0], swap(halves[1], 1)), (out_halves[0], out_other))
        query_grad, key_near, value_near = late.start(query_grad, key_near, value_near)
    normed_grad, to_prev, to_next, norm_sums = project_back(
        query_grad, key_near, value_near, first, normal_one, before, after, place
    )
    from_next = lax.ppermute(to_prev, "dev", down)
    from_prev = lax.ppermute(to_next, "dev", up)
    totals = jnp.concatenate([norm_sums, bias_sums, rest])
    if paired:
        second_sum, totals, from_next, from_prev = late.finish(totals, from_next, from_prev)
    else:
        second_sum = plain((halves, out_halves), part)
        bit = 1
        while bit < peers:
            (totals,) = merge(totals, (bit,))
            bit *= 2
    normed_grad = normed_grad + jnp.pad(from_prev.astype(f32), ((0, rows - RIM), (0, 0)))
    normed_grad = normed_grad + jnp.pad(from_next.astype(f32), ((rows - RIM, 0), (0, 0)))
    tokens_grad = middle_grad + norm_back(normed_grad, gain_one, normal_one, inv_one)
    mine = lax.dynamic_slice_in_dim(totals[:8], me * part, part, 1)
    expand_mine = lax.dynamic_slice_in_dim(totals[8 : 8 + fold].reshape(-1), me * part * fold, part * fold, 0)
    global_top = totals[-1, :H]

    first_sum = first_sum.astype(f32)
    expand_out = jnp.concatenate(
        [first_sum[(fold + i) * part : (fold + i + 1) * part] for i in range(fold)], axis=1
    )
    ratio = CLIP_TAU / jnp.maximum(global_top, CLIP_TAU)
    factor = jnp.where(clip_flags == 1, jnp.sqrt(ratio), 1.0)
    by_column = jnp.repeat(factor, HD)
    return (
        block_out,
        tokens_grad,
        query_mat * by_column[None, :],
        key_mat * by_column[None, :],
        mine[0],
        mine[1],
        second_sum[:part],
        mine[2],
        second_sum[part : 2 * part],
        second_sum[2 * part : 3 * part],
        mine[3],
        second_sum[3 * part :],
        mine[4],
        mine[5],
        mine[6],
        expand_out,
        expand_mine,
        first_sum[: fold * part],
        mine[7],
    )


def solution(mesh):
    split, both = P("dev"), P("dev", None)
    mat = both
    in_specs = (
        mat, split, split, mat, split, mat, mat, split, mat, split, split, split, mat, split, mat, split,
        split, P(), mat,
    )
    out_specs = (
        mat, mat, mat, mat, split, split, mat, split, mat, mat, split, mat, split, split, split, mat,
        split, mat, split,
    )
    return jax.shard_map(local, mesh=mesh, in_specs=in_specs, out_specs=out_specs, check_vma=False)
```

```python
import functools

import jax
import jax.numpy as jnp
from jax import lax
from jax.experimental import pallas as pl
from jax.experimental.pallas import tpu as pltpu
from jax.sharding import PartitionSpec as P

H = 16
HD = 64
LEN = 577
RIM = LEN - 1
HEADS = 4
QB = 256
KB = 256

NORM_EPS = 1e-05
CLIP_TAU = 3.0
GELU_COEF = 1.702
NEG_FILL = -1e30
SCALE = HD ** (-0.5)

bf16 = jnp.bfloat16
f32 = jnp.float32
NN = (((1,), (0,)), ((), ()))
NT = (((1,), (1,)), ((), ()))
TN = (((0,), (0,)), ((), ()))


def dot(lhs, rhs, dims):
    return lax.dot_general(lhs, rhs, dims, preferred_element_type=f32)


def norm_stats(values):
    centre = values - jnp.mean(values, axis=1, keepdims=True)
    inv_std = lax.rsqrt(jnp.mean(centre * centre, axis=1, keepdims=True) + NORM_EPS)
    return centre * inv_std, inv_std


def norm_back(grad_out, gain, normal, inv_std):
    scaled = grad_out * gain
    return inv_std * (
        scaled
        - jnp.mean(scaled, axis=1, keepdims=True)
        - normal * jnp.mean(scaled * normal, axis=1, keepdims=True)
    )


def column_sums(values):
    return jnp.sum(values.astype(f32), axis=0)


def cost(flops):
    return pl.CostEstimate(flops=flops, transcendentals=0, bytes_accessed=flops // 500)


def by_head(block):
    lane = lax.broadcasted_iota(jnp.int32, block.shape, 1) // HD
    zero = jnp.zeros_like(block)
    return jnp.concatenate([jnp.where(lane == i, block, zero) for i in range(HEADS)], axis=0)


def pair_slices(p):
    return slice(p * 2 * HD, (p + 1) * 2 * HD), slice(p * 2 * QB, (p + 1) * 2 * QB)


def untangle(parts):
    joined = []
    for part in parts:
        joined.append(jnp.concatenate([part[:HD, :QB], part[HD:, QB:]], axis=0).T)
    return jnp.concatenate(joined, axis=1)


def by_twos(count, step, start):
    two = lambda i, carry: step(2 * i + 1, step(2 * i, carry))
    return lax.fori_loop(count // 2 * 2, count, step, lax.fori_loop(0, count // 2, two, start))


def widen(bias):
    return jnp.concatenate([bias] * HEADS, axis=1)


def fill_bias(bias_ref, key_ids_ref, query_ids_ref, block, low, count):
    def one(c, carry):
        start = pl.multiple_of(low + c * KB, 128)
        keys = key_ids_ref[pl.ds(start, KB), :]
        same = keys == query_ids_ref[...]
        bias_ref[block, pl.ds(pl.multiple_of(c * KB, KB), KB), :] = jnp.where(same, 0.0, NEG_FILL)
        return carry

    lax.fori_loop(0, count, one, 0)


def attend_kernel(
    low_ref, count_ref, key_ids_ref, query_ids_ref, q_ref, k_ref, v_ref,
    o_ref, wide_ref, lse_ref, top_ref, bias_ref, score_ref,
):
    group, block = pl.program_id(0), pl.program_id(1)
    low, count = low_ref[block], count_ref[block]

    @pl.when(group == 0)
    def _():
        fill_bias(bias_ref, key_ids_ref, query_ids_ref, block, low, count)

    queries = by_head(q_ref[...] * jnp.asarray(SCALE, bf16))
    width = queries.shape[0]
    pairs = HEADS // 2

    def score(c):
        start = pl.multiple_of(low + c * KB, 128)
        return dot(k_ref[pl.ds(start, KB), :], queries, NT)

    def fold(op, tile):
        return op(tile.reshape(KB // 8, 8, width), axis=0)

    def first(c, top):
        at = pl.ds(pl.multiple_of(c * KB, KB), KB)
        scores = score(c) + widen(bias_ref[block, at, :])
        score_ref[at, :] = scores
        return jnp.maximum(top, fold(jnp.max, scores))

    top = by_twos(count, first, jnp.full((8, width), NEG_FILL, f32))
    top = jnp.max(top, axis=0, keepdims=True)

    def second(c, carry):
        total, accs = carry
        start = pl.multiple_of(low + c * KB, 128)
        weights = jnp.exp(score_ref[pl.ds(pl.multiple_of(c * KB, KB), KB), :] - top)
        total = total + fold(jnp.sum, weights)
        low_weights = weights.astype(bf16)
        values = v_ref[pl.ds(start, KB), :]
        new_accs = []
        for p, acc in enumerate(accs):
            lanes, place = pair_slices(p)
            new_accs.append(acc + dot(values[:, lanes], low_weights[:, place], TN))
        return total, tuple(new_accs)

    zeros = tuple(jnp.zeros((2 * HD, 2 * QB), f32) for _ in range(pairs))
    total, accs = by_twos(count, second, (jnp.zeros((8, width), f32), zeros))
    total = jnp.sum(total, axis=0, keepdims=True)
    mixed = untangle([acc / total[:, pair_slices(p)[1]] for p, acc in enumerate(accs)])
    wide_ref[...] = mixed
    o_ref[...] = mixed.astype(bf16)
    lse_ref[0] = top + jnp.log(total)

    @pl.when(block == 0)
    def _():
        top_ref[0] = top

    @pl.when(block != 0)
    def _():
        top_ref[0] = jnp.maximum(top_ref[0], top)


def attend_back_kernel(
    low_ref,
    count_ref,
    key_ids_ref,
    query_ids_ref,
    q_ref,
    k_ref,
    v_ref,
    do_ref,
    o_ref,
    lse_ref,
    dq_ref,
    dk_ref,
    dv_ref,
    sums_ref,
    bias_ref,
    dk_acc,
    dv_acc,
):
    pair, block = pl.program_id(0), pl.program_id(1)
    low, count = low_ref[block], count_ref[block]

    @pl.when(pair == 0)
    def _():
        fill_bias(bias_ref, key_ids_ref, query_ids_ref, block, low, count)

    @pl.when(block == 0)
    def _():
        dk_acc[...] = jnp.zeros_like(dk_acc)
        dv_acc[...] = jnp.zeros_like(dv_acc)

    queries = by_head(q_ref[...] * jnp.asarray(SCALE, bf16))
    grads = by_head(do_ref[...])
    product = (do_ref[...].astype(f32) * o_ref[...]).T
    inner = jnp.concatenate(
        [jnp.sum(product[i * HD : (i + 1) * HD], axis=0, keepdims=True) for i in range(HEADS)], axis=1
    )
    log_sum = lse_ref[0]
    pairs = HEADS // 2

    def step(c, accs):
        start = pl.multiple_of(low + c * KB, 128)
        keys = k_ref[pl.ds(start, KB), :]
        bias = bias_ref[block, pl.ds(pl.multiple_of(c * KB, KB), KB), :]
        scores = dot(keys, queries, NT) + widen(bias)
        probs = jnp.exp(scores - log_sum)
        prob_grad = dot(v_ref[pl.ds(start, KB), :], grads, NT)
        score_grad = (probs * (prob_grad - inner)).astype(bf16)
        dv_acc[pl.ds(start, KB), :] += dot(probs.astype(bf16), grads, NN)
        dk_acc[pl.ds(start, KB), :] += dot(score_grad, queries, NN)
        new_accs = []
        for p, acc in enumerate(accs):
            lanes, place = pair_slices(p)
            new_accs.append(acc + dot(keys[:, lanes], score_grad[:, place], TN))
        return tuple(new_accs)

    zeros = tuple(jnp.zeros((2 * HD, 2 * QB), f32) for _ in range(pairs))
    dq = (untangle(by_twos(count, step, zeros)) * SCALE).astype(bf16)
    dq_ref[...] = dq
    dq_sum = jnp.sum(dq.astype(f32), axis=0, keepdims=True)

    @pl.when(block == 0)
    def _():
        sums_ref[0:1, :] = dq_sum

    @pl.when(block != 0)
    def _():
        sums_ref[0:1, :] += dq_sum

    @pl.when(block == pl.num_programs(1) - 1)
    def _():
        dk_ref[...] = dk_acc[...].astype(bf16)
        dv = dv_acc[...].astype(bf16)
        dv_ref[...] = dv
        sums_ref[1:2, :] = jnp.sum(dv.astype(f32), axis=0, keepdims=True)


def key_ranges(own_ids, near_ids, blocks):
    rows, near = own_ids.shape[0], near_ids.shape[0]
    size = rows // blocks
    place = jnp.arange(near, dtype=jnp.int32)[None, :]
    first = own_ids[0::size][:, None]
    last = own_ids[size - 1 :: size][:, None]
    low = jnp.min(jnp.where(near_ids[None, :] == first, place, near), axis=1)
    high = jnp.max(jnp.where(near_ids[None, :] == last, place, -1), axis=1) + 1
    low = low // 128 * 128
    count = (high - low + KB - 1) // KB
    low = jnp.minimum(low, near - count * KB)
    return low.astype(jnp.int32), count.astype(jnp.int32)


def attention_specs(rows, near, blocks):
    groups = H // HEADS
    span = HEADS * HD
    most = -(-(QB + 2 * RIM + 127) // KB) * KB
    assert most <= near and rows % QB == 0 and near % 128 == 0
    own = pl.BlockSpec((QB, span), lambda p, b, *_: (b, p))
    base = [
        pl.BlockSpec((near, 1), lambda p, b, *_: (0, 0)),
        pl.BlockSpec((1, QB), lambda p, b, *_: (0, b)),
        own,
        pl.BlockSpec((near, span), lambda p, b, *_: (0, p)),
        pl.BlockSpec((near, span), lambda p, b, *_: (0, p + groups)),
    ]
    row = pl.BlockSpec((1, 1, HEADS * QB), lambda p, b, *_: (p, 0, b))
    bias = pltpu.VMEM((blocks, most, QB), f32)
    return groups, own, base, row, bias


def attend(ranges, key_ids, query_ids, queries, near_kv):
    rows, near = queries.shape[0], near_kv.shape[0]
    blocks = rows // QB
    groups, own, base, row, bias = attention_specs(rows, near, blocks)
    top = pl.BlockSpec((1, 1, HEADS * QB), lambda p, b, *_: (p, 0, 0))
    return pl.pallas_call(
        attend_kernel,
        grid_spec=pltpu.PrefetchScalarGridSpec(
            num_scalar_prefetch=2,
            grid=(groups, blocks),
            in_specs=base,
            out_specs=[own, own, row, top],
            scratch_shapes=[bias, pltpu.VMEM((bias.shape[1], HEADS * QB), f32)],
        ),
        out_shape=[
            jax.ShapeDtypeStruct(queries.shape, bf16),
            jax.ShapeDtypeStruct(queries.shape, f32),
            jax.ShapeDtypeStruct((groups, 1, HEADS * rows), f32),
            jax.ShapeDtypeStruct((groups, 1, HEADS * QB), f32),
        ],
        compiler_params=pltpu.CompilerParams(vmem_limit_bytes=56 << 20),
        cost_estimate=cost(rows * H * HD * 850 * 16),
        name="attend",
    )(*ranges, key_ids, query_ids, queries, near_kv, near_kv)


def attend_back(ranges, key_ids, query_ids, queries, near_kv, mixed_grad, mixed, log_sums):
    rows, near = queries.shape[0], near_kv.shape[0]
    blocks = rows // QB
    groups, own, base, row, bias = attention_specs(rows, near, blocks)
    wide = pl.BlockSpec((near, HEADS * HD), lambda p, b, *_: (0, p))
    return pl.pallas_call(
        attend_back_kernel,
        grid_spec=pltpu.PrefetchScalarGridSpec(
            num_scalar_prefetch=2,
            grid=(groups, blocks),
            in_specs=base + [own, own, row],
            out_specs=[own, wide, wide, pl.BlockSpec((2, HEADS * HD), lambda p, b, *_: (0, p))],
            scratch_shapes=[bias, pltpu.VMEM((near, HEADS * HD), f32), pltpu.VMEM((near, HEADS * HD), f32)],
        ),
        out_shape=[
            jax.ShapeDtypeStruct(queries.shape, bf16),
            jax.ShapeDtypeStruct((near, queries.shape[1]), bf16),
            jax.ShapeDtypeStruct((near, queries.shape[1]), bf16),
            jax.ShapeDtypeStruct((2, queries.shape[1]), f32),
        ],
        compiler_params=pltpu.CompilerParams(vmem_limit_bytes=56 << 20),
        cost_estimate=cost(rows * H * HD * 850 * 32),
        name="attend_back",
    )(*ranges, key_ids, query_ids, queries, near_kv, near_kv, mixed_grad, mixed, log_sums)


def spot_of(place, half):
    spot, bit = 0, half
    while bit:
        spot = spot + (place & 1) * bit
        place, bit = place >> 1, bit >> 1
    return spot


def mlp_kernel(
    a_ref, dz_ref, x_ref, rb_ref, eb_ref, we_ref, wr_ref,
    y_ref, da_ref, ebg_ref, sum_ref,
    act_ref, du_ref, rg_ref, eg_ref, sems,
):
    j = pl.program_id(0)
    rows, width = a_ref.shape
    tile = 256

    def copies(step):
        d, r, _ = rg_ref.shape
        g, e, _ = eg_ref.shape
        fold = pl.num_programs(0)
        return (
            pltpu.make_async_copy(rg_ref, sum_ref.at[pl.ds(step * d, d), pl.ds(0, r), :], sems.at[0]),
            pltpu.make_async_copy(eg_ref, sum_ref.at[:, pl.ds(r + step * e, e), :], sems.at[1]),
        )

    @pl.when(j == 0)
    def _():
        y_ref[...] = x_ref[...] + rb_ref[...]
        da_ref[...] = jnp.zeros_like(da_ref)

    ebg_ref[...] = jnp.zeros_like(ebg_ref)

    def by_rows(r, carry):
        at = pl.ds(pl.multiple_of(r * tile, tile), tile)
        we = we_ref[...].reshape(width, width)
        wr = wr_ref[...].reshape(width, width)
        hidden = dot(a_ref[at, :], we, NN) + eb_ref[...]
        back = dot(dz_ref[at, :], wr, NT)
        sigma = jax.nn.sigmoid(GELU_COEF * hidden)
        act = (hidden * sigma).astype(bf16)
        act_ref[at, :] = act
        du = (back * (sigma + GELU_COEF * hidden * sigma * (1.0 - sigma))).astype(bf16)
        du_ref[at, :] = du
        ebg_ref[...] += jnp.sum(du.astype(f32), axis=0, keepdims=True)
        y_ref[at, :] += dot(act, wr, NN)
        da_ref[at, :] += dot(du, we, NT)
        return carry

    lax.fori_loop(0, rows // tile, by_rows, 0)

    @pl.when(j > 0)
    def _():
        for copy in copies(j - 1):
            copy.wait()

    def by_columns(t, carry):
        at = pl.ds(pl.multiple_of(t * tile, tile), tile)
        rg = dot(act_ref[:, at], dz_ref[...], TN).astype(bf16)
        n = tile // rg_ref.shape[1]
        rg_ref[pl.ds(t * n, n)] = rg.reshape(n, rg_ref.shape[1], width)
        eg = dot(a_ref[:, at], du_ref[...], TN).astype(bf16)
        n = tile // eg_ref.shape[1]
        eg_ref[pl.ds(t * n, n)] = eg.reshape(n, eg_ref.shape[1], width)
        return carry

    lax.fori_loop(0, width // tile, by_columns, 0)
    for copy in copies(j):
        copy.start()

    @pl.when(j == pl.num_programs(0) - 1)
    def _():
        for copy in copies(j):
            copy.wait()


def mlp(normed, branch_grad, middle, bias_reduce, bias_expand, packed, sum_rows):
    rows, width = normed.shape
    ff = bias_expand.shape[1]
    fold = ff // width
    groups = packed.shape[0]
    each = width // groups
    whole = lambda j: (0, 0)
    one = pl.Buffered(1)
    return pl.pallas_call(
        mlp_kernel,
        grid=(fold,),
        in_specs=[
            pl.BlockSpec((rows, width), whole, pipeline_mode=one),
            pl.BlockSpec((rows, width), whole, pipeline_mode=one),
            pl.BlockSpec((rows, width), whole, pipeline_mode=one),
            pl.BlockSpec((1, width), whole),
            pl.BlockSpec((1, width), lambda j: (0, j)),
            pl.BlockSpec((groups, each, width), lambda j: (0, fold + j, 0)),
            pl.BlockSpec((groups // fold, fold * each, width), lambda j: (j, 0, 0)),
        ],
        out_specs=[
            pl.BlockSpec((rows, width), whole),
            pl.BlockSpec((rows, width), whole),
            pl.BlockSpec((1, width), lambda j: (0, j)),
            pl.BlockSpec(memory_space=pl.ANY),
        ],
        out_shape=[
            jax.ShapeDtypeStruct((rows, width), f32),
            jax.ShapeDtypeStruct((rows, width), f32),
            jax.ShapeDtypeStruct((1, ff), f32),
            jax.ShapeDtypeStruct((groups, sum_rows, width), bf16),
        ],
        scratch_shapes=[
            pltpu.VMEM((rows, width), bf16),
            pltpu.VMEM((rows, width), bf16),
            pltpu.VMEM((groups // fold, fold * each, width), bf16),
            pltpu.VMEM((groups, each, width), bf16),
            pltpu.SemaphoreType.DMA((2,)),
        ],
        compiler_params=pltpu.CompilerParams(vmem_limit_bytes=58 << 20),
        cost_estimate=cost(12 * rows * width * ff),
        name="mlp",
    )(normed, branch_grad, middle, bias_reduce, bias_expand, packed, packed)


def middle_back_kernel(
    me_ref, da_ref, x_ref, og_ref, gain_ref, mixed_ref, wo_ref,
    grad_ref, mg_ref, keep_ref, send_ref, sums_ref, ag_ref,
):
    i = pl.program_id(0)
    tile, width = da_ref.shape
    steps = pl.num_programs(0) // 2
    half, each, _ = keep_ref.shape

    @pl.when(i == 0)
    def _():
        sums_ref[...] = jnp.zeros_like(sums_ref)

    @pl.when(i < steps)
    def _():
        normal, inv_std = norm_stats(x_ref[...])
        da = da_ref[...]
        grad = og_ref[...] + norm_back(da, gain_ref[...], normal, inv_std)
        grad_ref[...] = grad
        low = grad.astype(bf16)
        ag_ref[pl.ds(pl.multiple_of(i * tile, tile), tile), :] = low
        mg_ref[...] = dot(low, wo_ref[...].reshape(width, width), NT).astype(bf16)
        sums_ref[0:1, :] += jnp.sum(low.astype(f32), axis=0, keepdims=True)
        sums_ref[1:2, :] += jnp.sum(da * normal, axis=0, keepdims=True)
        sums_ref[2:3, :] += jnp.sum(da, axis=0, keepdims=True)

    @pl.when(i >= steps)
    def _():
        t = i - steps
        size = width // steps
        at = pl.ds(pl.multiple_of(t * size, size), size)
        out = dot(mixed_ref[:, at], ag_ref[...], TN).astype(bf16)
        n = size // each
        for k in range(n):
            spot = spot_of((t * n + k) ^ me_ref[0], half)
            block = out[k * each : (k + 1) * each]

            @pl.when(spot < half)
            def _():
                keep_ref[spot] = block

            @pl.when(spot >= half)
            def _():
                send_ref[spot - half] = block


def middle_back(normed_grad, middle, out_grad, gain, mixed, packed, last, place):
    rows, width = middle.shape
    groups = packed.shape[0]
    each = width // groups
    tile = rows // 4
    whole = lambda i, *_: (0, 0)
    by_rows = pl.BlockSpec((tile, width), lambda i, *_: (jnp.minimum(i, 3), 0))
    side = pl.BlockSpec((groups // 2, each, width), lambda i, *_: (0, 0, 0))
    half = jax.ShapeDtypeStruct((groups // 2, each, width), bf16)
    return pl.pallas_call(
        middle_back_kernel,
        grid_spec=pltpu.PrefetchScalarGridSpec(
            num_scalar_prefetch=1,
            grid=(8,),
            in_specs=[
                by_rows,
                by_rows,
                by_rows,
                pl.BlockSpec((1, width), whole),
                pl.BlockSpec((rows, width), whole),
                pl.BlockSpec((groups, each, width), lambda i, *_: (0, last, 0)),
            ],
            out_specs=[by_rows, by_rows, side, side, pl.BlockSpec((3, width), whole)],
            scratch_shapes=[pltpu.VMEM((rows, width), bf16)],
        ),
        out_shape=[
            jax.ShapeDtypeStruct((rows, width), f32),
            jax.ShapeDtypeStruct((rows, width), bf16),
            half,
            half,
            jax.ShapeDtypeStruct((3, width), f32),
        ],
        compiler_params=pltpu.CompilerParams(vmem_limit_bytes=56 << 20),
        cost_estimate=cost(4 * rows * width * width),
        name="middle_back",
    )(place, normed_grad, middle, out_grad, gain, mixed, packed)


def middle_kernel(mixed_ref, wo_ref, x_ref, bo_ref, gain_ref, bias_ref, out_ref, low_ref):
    width = x_ref.shape[1]
    middle = x_ref[...] + dot(mixed_ref[...], wo_ref[...].reshape(width, width), NN) + bo_ref[...]
    out_ref[...] = middle
    low_ref[...] = (norm_stats(middle)[0] * gain_ref[...] + bias_ref[...]).astype(bf16)


def middle_forward(mixed, packed, tokens, bias_output, gain, bias, last):
    rows, width = tokens.shape
    groups = packed.shape[0]
    by_rows = pl.BlockSpec((rows // 4, width), lambda i: (i, 0))
    vector = pl.BlockSpec((1, width), lambda i: (0, 0))
    return pl.pallas_call(
        middle_kernel,
        grid=(4,),
        in_specs=[
            by_rows,
            pl.BlockSpec((groups, width // groups, width), lambda i: (0, last, 0)),
            by_rows,
            vector,
            vector,
            vector,
        ],
        out_specs=[by_rows, by_rows],
        out_shape=[jax.ShapeDtypeStruct((rows, width), f32), jax.ShapeDtypeStruct((rows, width), bf16)],
        compiler_params=pltpu.CompilerParams(vmem_limit_bytes=56 << 20),
        cost_estimate=cost(2 * rows * width * width),
        name="middle",
    )(mixed, packed, tokens, bias_output, gain, bias)


def assemble(me, parts, w_ref):
    each, half = parts[0].shape[1:]
    for core, (left, right) in enumerate(((parts[0], parts[2]), (parts[1], parts[3]))):
        for spot in range(16):
            high, low, z8, z16 = spot >> 3 & 1, spot >> 2 & 1, spot >> 1 & 1, spot & 1
            z = z8 * 8 + z16 * 16 + core
            for ref, owner, lanes in (
                (left, z + high * 4 + low * 2, slice(0, half)),
                (right, z + high * 2 + low * 4, slice(half, 2 * half)),
            ):
                w_ref[pl.ds(pl.multiple_of((owner ^ me) * each, each), each), lanes] = ref[spot]


def part_specs(width):
    each = width // 32
    return [pl.BlockSpec((16, each, width // 2), lambda j, *_: (0, j, 0)) for _ in range(4)]


def qkv_kernel(me_ref, a_ref, p0, p1, p2, p3, bias_ref, q_ref, kv_ref, w_ref):
    j = pl.program_id(0)
    assemble(me_ref[0], (p0, p1, p2, p3), w_ref)
    near, width = a_ref.shape
    rows = q_ref.shape[0]
    rim = (near - rows) // 2

    @pl.when(j == 0)
    def _():
        def step(t, carry):
            source = pl.ds(pl.multiple_of(rim + t * 256, 8), 256)
            w = w_ref[...]
            q_ref[pl.ds(pl.multiple_of(t * 256, 256), 256), :] = (
                dot(a_ref[source, :], w, NN) + bias_ref[...]
            ).astype(bf16)
            return carry

        lax.fori_loop(0, rows // 256, step, 0)

    @pl.when(j > 0)
    def _():
        size = near // 8

        def step(t, carry):
            at = pl.ds(pl.multiple_of(t * size, 16), size)
            w = w_ref[...]
            kv_ref[at, :] = (dot(a_ref[at, :], w, NN) + bias_ref[...]).astype(bf16)
            return carry

        lax.fori_loop(0, near // size, step, 0)


def project(normed_near, parts, biases, rows, place):
    near, width = normed_near.shape
    return pl.pallas_call(
        qkv_kernel,
        grid_spec=pltpu.PrefetchScalarGridSpec(
            num_scalar_prefetch=1,
            grid=(3,),
            in_specs=[pl.BlockSpec((near, width), lambda j, *_: (0, 0))]
            + part_specs(width)
            + [pl.BlockSpec((1, width), lambda j, *_: (0, j))],
            out_specs=[
                pl.BlockSpec((rows, width), lambda j, *_: (0, 0)),
                pl.BlockSpec((near, width), lambda j, *_: (0, jnp.maximum(j - 1, 0))),
            ],
            scratch_shapes=[pltpu.VMEM((width, width), bf16)],
        ),
        out_shape=[
            jax.ShapeDtypeStruct((rows, width), bf16),
            jax.ShapeDtypeStruct((near, 2 * width), bf16),
        ],
        compiler_params=pltpu.CompilerParams(vmem_limit_bytes=56 << 20),
        cost_estimate=cost(2 * width * width * (rows + 2 * near)),
        name="qkv",
    )(place, normed_near, *parts, biases)


def qkv_grads_kernel(me_ref, a_ref, dq_ref, dk_hbm, dv_hbm, keep_ref, send_ref, kv_ref, sems):
    j = pl.program_id(0)
    near, width = a_ref.shape
    rows = dq_ref.shape[0]
    rim = (near - rows) // 2
    tile = 256
    half, each, _ = keep_ref.shape
    n = tile // each

    def fill(grad_ref, source):
        def step(t, carry):
            at = pl.ds(pl.multiple_of(t * tile, tile), tile)
            out = dot(a_ref[source, at], grad_ref[...], TN).astype(bf16)
            for i in range(n):
                spot = spot_of((t * n + i) ^ me_ref[0], half)
                block = out[i * each : (i + 1) * each]

                @pl.when(spot < half)
                def _():
                    keep_ref[spot] = block

                @pl.when(spot >= half)
                def _():
                    send_ref[spot - half] = block

            return carry

        lax.fori_loop(0, width // tile, step, 0)

    loads = [pltpu.make_async_copy(ref, kv_ref.at[i], sems.at[i]) for i, ref in enumerate((dk_hbm, dv_hbm))]

    @pl.when(j == 0)
    def _():
        for load in loads:
            load.start()
        fill(dq_ref, slice(rim, rim + rows))

    @pl.when(j == 1)
    def _():
        loads[0].wait()

    @pl.when(j == 2)
    def _():
        loads[1].wait()

    @pl.when(j > 0)
    def _():
        fill(kv_ref.at[j - 1], slice(0, near))


def qkv_grads(normed_near, query_grad, key_near, value_near, groups, place):
    near, width = normed_near.shape
    rows = query_grad.shape[0]
    each = width // groups
    whole = lambda j, *_: (0, 0)
    half = jax.ShapeDtypeStruct((groups // 2, 3 * each, width), bf16)
    out = pl.BlockSpec((groups // 2, each, width), lambda j, *_: (0, j, 0))
    return pl.pallas_call(
        qkv_grads_kernel,
        grid_spec=pltpu.PrefetchScalarGridSpec(
            num_scalar_prefetch=1,
            grid=(3,),
            in_specs=[
                pl.BlockSpec((near, width), whole),
                pl.BlockSpec((rows, width), whole),
                pl.BlockSpec(memory_space=pl.ANY),
                pl.BlockSpec(memory_space=pl.ANY),
            ],
            out_specs=[out, out],
            scratch_shapes=[
                pltpu.VMEM((2, near, width), bf16),
                pltpu.SemaphoreType.DMA((2,)),
            ],
        ),
        out_shape=[half, half],
        compiler_params=pltpu.CompilerParams(vmem_limit_bytes=56 << 20),
        cost_estimate=cost(2 * width * width * (rows + 2 * near)),
        name="qkv_grads",
    )(place, normed_near, query_grad, key_near, value_near)


def plus(a, b):
    return (a.astype(f32) + b.astype(f32)).astype(bf16)


def swap(value, bit):
    peers = lax.axis_size("dev")
    return lax.ppermute(value, "dev", [(i, i ^ bit) for i in range(peers)])


def merge(totals, bits, *beside):
    others = [swap(totals, bit) for bit in bits]
    out = lax.optimization_barrier((*beside, *others))
    beside, others = out[: len(beside)], out[len(beside) :]
    for other in others:
        totals = jnp.concatenate([totals[:-1] + other[:-1], jnp.maximum(totals[-1:], other[-1:])], axis=0)
    return totals, *beside


class Halving:
    def __init__(self, first, second):
        def split(pair):
            return [v.reshape((2, 2, 4) + v.shape[1:]) for v in pair]

        (keep, other), (keep_o, other_o) = split(first), split(second)
        half = (keep.shape[3] + keep_o.shape[3]) // 2

        def side_a(at):
            return plus(keep[at][..., :half, :], other[at][..., :half, :])

        def side_b(at):
            return jnp.concatenate(
                [plus(keep[at][..., half:, :], other[at][..., half:, :]), plus(keep_o[at], other_o[at])], axis=-2
            )

        self.sides = side_a(1), side_b((slice(None), 1))
        self.keeps = lambda: (side_a(0), side_b((slice(None), 0)))

    def start(self, *after):
        to_x, to_y, *after = lax.optimization_barrier((*self.sides, *after))
        self.others = swap(to_x, 2), swap(to_y, 4)
        return after

    def finish(self, totals, *beside):
        (from_x, from_y), (keep_x, keep_y) = self.others, self.keeps()
        to_y, to_x = plus(keep_x[1], from_x[1]), plus(keep_y[1], from_y[1])
        to_x, to_y, totals = lax.optimization_barrier((to_x, to_y, totals))
        second_y, second_x = swap(to_y, 4), swap(to_x, 2)
        totals, second_y, second_x = merge(totals, (1, 2, 3), second_y, second_x)
        keep_x = plus(keep_x[0], from_x[0])
        keep_y = plus(keep_y[0], from_y[0])
        send = jnp.concatenate([plus(keep_x[2:], second_y[2:]), plus(keep_y[2:], second_x[2:])], axis=1)
        send, totals = lax.optimization_barrier((send, totals))
        low = swap(send, 8)
        totals, low, *beside = merge(totals, (4, 8, 12), low, *beside)
        keep = jnp.concatenate([plus(keep_x[:2], second_y[:2]), plus(keep_y[:2], second_x[:2])], axis=1)
        send, totals = lax.optimization_barrier((plus(keep[1], low[1]), totals))
        last = swap(send, 16)
        totals, last = merge(totals, (16,), last)
        return plus(keep[0], low[0]).astype(f32) + last.astype(f32), totals, *beside


def plain(pairs, part):
    groups = 2 * pairs[0][0].shape[0]
    order = [int(f"{i:05b}"[::-1], 2) for i in range(groups)]
    joined = jnp.concatenate([jnp.concatenate(pair, axis=0) for pair in pairs], axis=1)
    joined = jnp.stack([joined[i] for i in order])
    return scatter(joined, [part] * (joined.shape[1] * groups // joined.shape[2])).astype(f32)


def normed_grad_kernel(
    me_ref, dq_ref, dk_hbm, dv_hbm, p0, p1, p2, p3, normal_hbm, nb_hbm, na_hbm,
    own_ref, before_ref, after_ref, sums_ref,
    acc_ref, kv_ref, normal_ref, nb_ref, na_ref, sems, w_ref,
):
    j = pl.program_id(0)
    assemble(me_ref[0], (p0, p1, p2, p3), w_ref)
    rows, width = own_ref.shape
    rim = before_ref.shape[0]
    near = 2 * rim + rows
    pairs = (
        (dk_hbm, kv_ref.at[0]),
        (dv_hbm, kv_ref.at[1]),
        (normal_hbm, normal_ref),
        (nb_hbm.at[pl.ds(0, rim)], nb_ref),
        (na_hbm.at[pl.ds(0, rim)], na_ref),
    )
    loads = [pltpu.make_async_copy(source, target, sems.at[i]) for i, (source, target) in enumerate(pairs)]

    @pl.when(j == 0)
    def _():
        for load in loads:
            load.start()
        acc_ref[:rim, :] = jnp.zeros((rim, width), f32)
        acc_ref[rim + rows :, :] = jnp.zeros((rim, width), f32)

        def step(t, carry):
            grads = dq_ref[pl.ds(pl.multiple_of(t * 256, 256), 256), :]
            acc_ref[pl.ds(pl.multiple_of(rim + t * 256, 8), 256), :] = dot(grads, w_ref[...], NT)
            return carry

        lax.fori_loop(0, rows // 256, step, 0)

    @pl.when(j == 1)
    def _():
        loads[0].wait()

    @pl.when(j == 2)
    def _():
        for load in loads[1:]:
            load.wait()

    @pl.when(j > 0)
    def _():
        size = near // 8

        def step(t, carry):
            at = pl.ds(pl.multiple_of(t * size, 8), size)
            acc_ref[at, :] += dot(kv_ref[j - 1, at, :], w_ref[...], NT)
            return carry

        lax.fori_loop(0, near // size, step, 0)

    @pl.when(j == 2)
    def _():
        def finish(base, normal, out, carry):
            def step(t, carry):
                gain_sum, bias_sum = carry
                at = pl.multiple_of(t * 16, 16)
                value = acc_ref[pl.ds(pl.multiple_of(base + at, 8), 16), :]
                product = value * normal[pl.ds(at, 16), :].astype(f32)
                out[pl.ds(at, 16), :] = value.astype(out.dtype)
                return gain_sum + product[:8] + product[8:], bias_sum + value[:8] + value[8:]

            return lax.fori_loop(0, out.shape[0] // 16, step, carry)

        carry = (jnp.zeros((8, width), f32), jnp.zeros((8, width), f32))
        carry = finish(0, nb_ref, before_ref, carry)
        carry = finish(rim + rows, na_ref, after_ref, carry)
        gain_sum, bias_sum = finish(rim, normal_ref, own_ref, carry)
        sums_ref[0:1, :] = jnp.sum(gain_sum, axis=0, keepdims=True)
        sums_ref[1:2, :] = jnp.sum(bias_sum, axis=0, keepdims=True)


def project_back(query_grad, key_near, value_near, parts, normal, before, after, place):
    rows, width = query_grad.shape
    near = key_near.shape[0]
    rim = (near - rows) // 2
    whole = lambda j, *_: (0, 0)
    anywhere = pl.BlockSpec(memory_space=pl.ANY)
    return pl.pallas_call(
        normed_grad_kernel,
        grid_spec=pltpu.PrefetchScalarGridSpec(
            num_scalar_prefetch=1,
            grid=(3,),
            in_specs=[pl.BlockSpec((rows, width), whole, pipeline_mode=pl.Buffered(1)), anywhere, anywhere]
            + part_specs(width)
            + [anywhere, anywhere, anywhere],
            out_specs=[
                pl.BlockSpec((rows, width), whole),
                pl.BlockSpec((rim, width), whole),
                pl.BlockSpec((rim, width), whole),
                pl.BlockSpec((2, width), whole),
            ],
            scratch_shapes=[
                pltpu.VMEM((near, width), f32),
                pltpu.VMEM((2, near, width), bf16),
                pltpu.VMEM((rows, width), f32),
                pltpu.VMEM((rim, width), bf16),
                pltpu.VMEM((rim, width), bf16),
                pltpu.SemaphoreType.DMA((5,)),
                pltpu.VMEM((width, width), bf16),
            ],
        ),
        out_shape=[
            jax.ShapeDtypeStruct((rows, width), f32),
            jax.ShapeDtypeStruct((rim, width), bf16),
            jax.ShapeDtypeStruct((rim, width), bf16),
            jax.ShapeDtypeStruct((2, width), f32),
        ],
        compiler_params=pltpu.CompilerParams(vmem_limit_bytes=58 << 20),
        cost_estimate=cost(2 * width * width * (rows + 2 * near)),
        name="normed_grad",
    )(place, query_grad, key_near, value_near, *parts, normal, before, after)


def gather(value, segments, groups):
    peers = lax.axis_size("dev")
    rows, width = value.shape
    whole = lax.all_gather(value, "dev", axis=0, tiled=True)
    sub = peers // groups
    if sub == 1:
        return whole.reshape(groups, rows, width)
    whole = whole.reshape(groups, sub, rows, width)
    parts, at = [], 0
    for size in segments:
        parts.append(whole[:, :, at : at + size].reshape(groups, sub * size, width))
        at += size
    return jnp.concatenate(parts, axis=1)


def scatter(value, segments):
    peers = lax.axis_size("dev")
    groups, rows, width = value.shape
    sub = peers // groups
    if sub > 1:
        parts, at = [], 0
        for size in segments:
            cut = value[:, at : at + sub * size]
            parts.append(cut.reshape(groups, sub, size, width))
            at += sub * size
        value = jnp.concatenate(parts, axis=2)
    value = value.reshape(peers * sum(segments), width)
    return lax.psum_scatter(value, "dev", scatter_dimension=0, tiled=True)


def pack_kernel(me_ref, q_ref, k_ref, v_ref, small_ref, r_ref, e_ref, o_ref, eb_ref, one_ref, two_ref):
    part, width = q_ref.shape
    for i, ref in enumerate((q_ref, k_ref, v_ref)):
        one_ref[i * part : (i + 1) * part, :] = ref[...].astype(bf16)

    def place(value, size):
        index = lax.broadcasted_iota(jnp.int32, value.shape, 0) * width
        index = index + lax.broadcasted_iota(jnp.int32, value.shape, 1)
        return jnp.where(index // size == me_ref[0], value, jnp.zeros_like(value))

    row = lax.broadcasted_iota(jnp.int32, (part, width), 0)
    column = lax.broadcasted_iota(jnp.int32, (part, width), 1)
    pick = jnp.where(column - me_ref[0] * part == row, 1.0, 0.0).astype(bf16)
    one_ref[3 * part :, :] = dot(small_ref[...].astype(bf16), pick, NN).astype(bf16)
    rows = r_ref.shape[0]
    fold = rows // part
    two_ref[:rows, :] = r_ref[...].astype(bf16)
    for i in range(fold):
        at = rows + i * part
        two_ref[at : at + part, :] = e_ref[:, i * width : (i + 1) * width].astype(bf16)
    at = rows + fold * part
    two_ref[at : at + part, :] = o_ref[...].astype(bf16)
    bias = jnp.concatenate([eb_ref[...]] * (width // eb_ref.shape[1]), axis=1)
    two_ref[at + part :, :] = place(jnp.broadcast_to(bias, (8, width)), fold * part).astype(bf16)


def pack(me, mats, smalls, reduce_mat, expand_mat, output_mat, expand_bias):
    part, width = output_mat.shape
    tiled = jnp.stack(smalls)
    bias = expand_bias[None]
    rows = reduce_mat.shape[0]
    return pl.pallas_call(
        pack_kernel,
        grid_spec=pltpu.PrefetchScalarGridSpec(
            num_scalar_prefetch=1,
            grid=(1,),
            in_specs=[
                pl.BlockSpec(v.shape, lambda i, *_: (0, 0))
                for v in (*mats, tiled, reduce_mat, expand_mat, output_mat, bias)
            ],
            out_specs=[
                pl.BlockSpec((3 * part + 8, width), lambda i, *_: (0, 0)),
                pl.BlockSpec((2 * rows + part + 8, width), lambda i, *_: (0, 0)),
            ],
        ),
        out_shape=[
            jax.ShapeDtypeStruct((3 * part + 8, width), bf16),
            jax.ShapeDtypeStruct((2 * rows + part + 8, width), bf16),
        ],
        name="pack",
    )(jnp.full((1,), me, jnp.int32), *mats, tiled, reduce_mat, expand_mat, output_mat, bias)


def doubling(value, tokens, packed, exchange, prepare):
    rows, width = value.shape
    half = width // 2
    grown = value[None]
    grown = jnp.concatenate([grown, swap(grown, 16)])
    grown, tokens = lax.optimization_barrier((grown, tokens))
    other = swap(grown, 8)
    near = exchange(tokens)
    grown, other, packed, *near = lax.optimization_barrier((grown, other, packed, *near))
    a = jnp.concatenate([grown[..., :half], other[..., :half]])
    b = jnp.concatenate([grown[..., half:], other[..., half:]])
    from_x, from_y = swap(a, 2), swap(b, 4)
    a, b = jnp.concatenate([a, from_x]), jnp.concatenate([b, from_y])
    from_y, from_x = swap(a, 4), swap(b, 2)
    prepared = prepare(*near)
    a, b = jnp.concatenate([a, from_y]), jnp.concatenate([b, from_x])
    a, b, *prepared = lax.optimization_barrier((a, b, *prepared))
    return (a, swap(a, 1), b, swap(b, 1)), prepared, packed


def fold_smalls(natural, sub):
    at = natural.shape[1] - 8 * sub
    tail = natural[:, at:].reshape(natural.shape[0], sub, 8, natural.shape[2])
    tail = jnp.sum(tail.astype(f32), axis=1).astype(natural.dtype)
    return jnp.concatenate([natural[:, :at], tail], axis=1)


def as_doubled(natural):
    half = natural.shape[2] // 2
    out = []
    for cut, orders in ((slice(0, half), (4, 2)), (slice(half, None), (2, 4))):
        for core in (0, 1):
            picks = []
            for spot in range(16):
                high, low, z8, z16 = spot >> 3 & 1, spot >> 2 & 1, spot >> 1 & 1, spot & 1
                picks.append(natural[z8 * 8 + z16 * 16 + core + high * orders[0] + low * orders[1], :, cut])
            out.append(jnp.stack(picks))
    return tuple(out)


def spread(vector, width):
    peers, me = lax.axis_size("dev"), lax.axis_index("dev")
    size = vector.shape[0]
    place = jnp.arange(peers * size, dtype=jnp.int32) // size
    full = jnp.where(place == me, jnp.tile(vector, peers), jnp.zeros((), vector.dtype))
    return full.reshape(-1, width)


def local(
    tokens_in,
    attn_gain,
    attn_bias,
    query_mat,
    query_bias,
    key_mat,
    value_mat,
    value_bias,
    output_mat,
    output_bias,
    mlp_gain,
    mlp_bias,
    expand_mat,
    expand_bias,
    reduce_mat,
    reduce_bias,
    image_ids,
    clip_flags,
    out_grad,
):
    peers, me = lax.axis_size("dev"), lax.axis_index("dev")
    rows, width = tokens_in.shape
    part = query_mat.shape[0]
    ff = expand_mat.shape[1]
    fold = ff // width
    groups = min(peers, 32)
    sub = peers // groups

    paired = peers == 32
    up = [(i, i + 1) for i in range(peers - 1)]
    down = [(i + 1, i) for i in range(peers - 1)]
    own_ids = image_ids + 1
    smalls = (attn_gain, attn_bias, query_bias, value_bias, output_bias, mlp_gain, mlp_bias, reduce_bias)

    def ids_of(halo):
        return (halo[RIM, :RIM].astype(f32) * 32 + halo[RIM + 1, :RIM].astype(f32)).astype(jnp.int32)

    def exchange(tokens):
        normal_one, inv_one = norm_stats(tokens)
        normal_low = normal_one.astype(bf16)

        def with_ids(at):
            ids = jnp.pad(own_ids[at], (0, width - RIM))
            ids = [(ids // 32).astype(bf16)[None], (ids % 32).astype(bf16)[None]]
            return jnp.concatenate([normal_low[at], *ids, jnp.zeros((6, width), bf16)])

        before = lax.ppermute(with_ids(slice(rows - RIM, rows)), "dev", up)
        after = lax.ppermute(with_ids(slice(0, RIM)), "dev", down)
        return before, after, normal_one, inv_one

    def prepare(before, after, normal_one, inv_one):
        near_ids = jnp.concatenate([ids_of(before), own_ids, ids_of(after)])
        ranges = key_ranges(own_ids, near_ids, rows // QB)
        return before, after, near_ids, near_ids[:, None], own_ids[None, :], *ranges, normal_one, inv_one

    if paired:
        packed_one, packed_two = pack(
            me, (query_mat, key_mat, value_mat), smalls, reduce_mat, expand_mat, output_mat, expand_bias
        )
        first, prepared, packed_two = doubling(packed_one, tokens_in, packed_two, exchange, prepare)
        second = gather(packed_two, (), groups)
    else:
        low = [v.astype(bf16) for v in (query_mat, key_mat, value_mat)]
        packed_one = jnp.concatenate(low + [spread(v.astype(bf16), width) for v in smalls])
        first = as_doubled(fold_smalls(gather(packed_one, [part] * 3 + [8], groups), sub))
        prepared = prepare(*exchange(tokens_in))
        expand_low = expand_mat.astype(bf16)
        packed_two = jnp.concatenate(
            [reduce_mat.astype(bf16)]
            + [expand_low[:, i * width : (i + 1) * width] for i in range(fold)]
            + [output_mat.astype(bf16), spread(expand_bias.astype(bf16), width), jnp.zeros((8 - fold, width), bf16)]
        )
        second = gather(packed_two, [fold * part] + [part] * (fold + 1) + [8], groups)

    before, after, near_ids, key_ids, query_ids, *ranges, normal_one, inv_one = prepared
    vectors = jnp.concatenate(
        [
            sum(jnp.sum(v[:, 3 * width // groups :].astype(f32), axis=0) for v in first[i : i + 2])
            for i in (0, 2)
        ],
        axis=1,
    )
    (gain_one, bias_one, bias_query, bias_value, bias_output, gain_two, bias_two, bias_reduce) = [
        vectors[i : i + 1] for i in range(8)
    ]

    normed_near = jnp.concatenate(
        [(v.astype(f32) * gain_one + bias_one).astype(bf16) for v in (before[:RIM], normal_one, after[:RIM])],
        axis=0,
    )
    bias_qkv = jnp.concatenate([bias_query, jnp.zeros_like(bias_value), bias_value], axis=1)
    place = jnp.full((1,), me if paired else 0, jnp.int32)
    queries, near_kv = project(normed_near, first, bias_qkv, rows, place)
    mixed, mixed_wide, log_sums, tops = attend(ranges, key_ids, query_ids, queries, near_kv)
    head_top = jnp.max(tops.reshape(H, QB), axis=1)

    tail = second[:, (2 * fold + 1) * part * sub :].reshape(groups * sub, 8, width)
    bias_expand = jnp.sum(tail.astype(f32), axis=0)[:fold].reshape(1, ff)
    middle, normed_two = middle_forward(mixed, second, tokens_in, bias_output, gain_two, bias_two, 2 * fold)
    branch_grad = out_grad.astype(bf16)
    block_out, normed_two_grad, expand_bias_grad, sums = mlp(
        normed_two, branch_grad, middle, bias_reduce, bias_expand, second, 2 * fold * width // groups + 8
    )
    reduce_bias_grad = column_sums(branch_grad)
    first_sum = scatter(sums, [fold * part] + [part] * fold + [8 // sub])
    middle_grad, mixed_grad, *out_halves, middle_sums = middle_back(
        normed_two_grad, middle, out_grad, gain_two, mixed, second, 2 * fold, place
    )
    out_other = swap(out_halves[1], 1) if peers == 32 else None
    rest = jnp.concatenate(
        [
            middle_sums,
            reduce_bias_grad[None],
            expand_bias_grad.reshape(fold, width),
            jnp.pad(head_top, (0, width - H))[None],
        ]
    )
    mixed_grad, rest = lax.optimization_barrier((mixed_grad, rest))
    query_grad, key_near, value_near, bias_sums = attend_back(
        ranges, key_ids, query_ids, queries, near_kv, mixed_grad, mixed_wide, log_sums
    )
    halves = qkv_grads(normed_near, query_grad, key_near, value_near, groups, place)
    if paired:
        late = Halving((halves[0], swap(halves[1], 1)), (out_halves[0], out_other))
        query_grad, key_near, value_near = late.start(query_grad, key_near, value_near)
    normed_grad, to_prev, to_next, norm_sums = project_back(
        query_grad, key_near, value_near, first, normal_one, before, after, place
    )
    from_next = lax.ppermute(to_prev, "dev", down)
    from_prev = lax.ppermute(to_next, "dev", up)
    totals = jnp.concatenate([norm_sums, bias_sums, rest])
    if paired:
        second_sum, totals, from_next, from_prev = late.finish(totals, from_next, from_prev)
    else:
        second_sum = plain((halves, out_halves), part)
        bit = 1
        while bit < peers:
            (totals,) = merge(totals, (bit,))
            bit *= 2
    normed_grad = normed_grad + jnp.pad(from_prev.astype(f32), ((0, rows - RIM), (0, 0)))
    normed_grad = normed_grad + jnp.pad(from_next.astype(f32), ((rows - RIM, 0), (0, 0)))
    tokens_grad = middle_grad + norm_back(normed_grad, gain_one, normal_one, inv_one)
    mine = lax.dynamic_slice_in_dim(totals[:8], me * part, part, 1)
    expand_mine = lax.dynamic_slice_in_dim(totals[8 : 8 + fold].reshape(-1), me * part * fold, part * fold, 0)
    global_top = totals[-1, :H]

    first_sum = first_sum.astype(f32)
    expand_out = jnp.concatenate(
        [first_sum[(fold + i) * part : (fold + i + 1) * part] for i in range(fold)], axis=1
    )
    ratio = CLIP_TAU / jnp.maximum(global_top, CLIP_TAU)
    factor = jnp.where(clip_flags == 1, jnp.sqrt(ratio), 1.0)
    by_column = jnp.repeat(factor, HD)
    return (
        block_out,
        tokens_grad,
        query_mat * by_column[None, :],
        key_mat * by_column[None, :],
        mine[0],
        mine[1],
        second_sum[:part],
        mine[2],
        second_sum[part : 2 * part],
        second_sum[2 * part : 3 * part],
        mine[3],
        second_sum[3 * part :],
        mine[4],
        mine[5],
        mine[6],
        expand_out,
        expand_mine,
        first_sum[: fold * part],
        mine[7],
    )


def solution(mesh):
    split, both = P("dev"), P("dev", None)
    mat = both
    in_specs = (
        mat, split, split, mat, split, mat, mat, split, mat, split, split, split, mat, split, mat, split,
        split, P(), mat,
    )
    out_specs = (
        mat, mat, mat, mat, split, split, mat, split, mat, mat, split, mat, split, split, split, mat,
        split, mat, split,
    )
    return jax.shard_map(local, mesh=mesh, in_specs=in_specs, out_specs=out_specs, check_vma=False)
```

```python
import functools

import jax
import jax.numpy as jnp
from jax import lax
from jax.experimental import pallas as pl
from jax.experimental.pallas import tpu as pltpu
from jax.sharding import PartitionSpec as P

H = 16
HD = 64
LEN = 577
RIM = LEN - 1
HEADS = 4
QB = 256
KB = 256

NORM_EPS = 1e-05
CLIP_TAU = 3.0
GELU_COEF = 1.702
NEG_FILL = -1e30
SCALE = HD ** (-0.5)

bf16 = jnp.bfloat16
f32 = jnp.float32
NN = (((1,), (0,)), ((), ()))
NT = (((1,), (1,)), ((), ()))
TN = (((0,), (0,)), ((), ()))


def dot(lhs, rhs, dims):
    return lax.dot_general(lhs, rhs, dims, preferred_element_type=f32)


def norm_stats(values):
    centre = values - jnp.mean(values, axis=1, keepdims=True)
    inv_std = lax.rsqrt(jnp.mean(centre * centre, axis=1, keepdims=True) + NORM_EPS)
    return centre * inv_std, inv_std


def norm_back(grad_out, gain, normal, inv_std):
    scaled = grad_out * gain
    return inv_std * (
        scaled
        - jnp.mean(scaled, axis=1, keepdims=True)
        - normal * jnp.mean(scaled * normal, axis=1, keepdims=True)
    )


def column_sums(values):
    return jnp.sum(values.astype(f32), axis=0)


def cost(flops):
    return pl.CostEstimate(flops=flops, transcendentals=0, bytes_accessed=flops // 500)


def by_head(block):
    lane = lax.broadcasted_iota(jnp.int32, block.shape, 1) // HD
    zero = jnp.zeros_like(block)
    return jnp.concatenate([jnp.where(lane == i, block, zero) for i in range(HEADS)], axis=0)


def pair_slices(p):
    return slice(p * 2 * HD, (p + 1) * 2 * HD), slice(p * 2 * QB, (p + 1) * 2 * QB)


def untangle(parts):
    joined = []
    for part in parts:
        joined.append(jnp.concatenate([part[:HD, :QB], part[HD:, QB:]], axis=0).T)
    return jnp.concatenate(joined, axis=1)


def by_twos(count, step, start):
    two = lambda i, carry: step(2 * i + 1, step(2 * i, carry))
    return lax.fori_loop(count // 2 * 2, count, step, lax.fori_loop(0, count // 2, two, start))


def widen(bias):
    return jnp.concatenate([bias] * HEADS, axis=1)


def fill_bias(bias_ref, key_ids_ref, query_ids_ref, block, low, count):
    def one(c, carry):
        start = pl.multiple_of(low + c * KB, 128)
        keys = key_ids_ref[pl.ds(start, KB), :]
        same = keys == query_ids_ref[...]
        bias_ref[block, pl.ds(pl.multiple_of(c * KB, KB), KB), :] = jnp.where(same, 0.0, NEG_FILL)
        return carry

    lax.fori_loop(0, count, one, 0)


def attend_kernel(
    low_ref, count_ref, key_ids_ref, query_ids_ref, q_ref, k_ref, v_ref,
    o_ref, wide_ref, lse_ref, top_ref, bias_ref, score_ref,
):
    group, block = pl.program_id(0), pl.program_id(1)
    low, count = low_ref[block], count_ref[block]

    @pl.when(group == 0)
    def _():
        fill_bias(bias_ref, key_ids_ref, query_ids_ref, block, low, count)

    queries = by_head(q_ref[...] * jnp.asarray(SCALE, bf16))
    width = queries.shape[0]
    pairs = HEADS // 2

    def score(c):
        start = pl.multiple_of(low + c * KB, 128)
        return dot(k_ref[pl.ds(start, KB), :], queries, NT)

    def fold(op, tile):
        return op(tile.reshape(KB // 8, 8, width), axis=0)

    def first(c, top):
        at = pl.ds(pl.multiple_of(c * KB, KB), KB)
        scores = score(c) + widen(bias_ref[block, at, :])
        score_ref[at, :] = scores
        return jnp.maximum(top, fold(jnp.max, scores))

    top = by_twos(count, first, jnp.full((8, width), NEG_FILL, f32))
    top = jnp.max(top, axis=0, keepdims=True)

    def second(c, carry):
        total, accs = carry
        start = pl.multiple_of(low + c * KB, 128)
        weights = jnp.exp(score_ref[pl.ds(pl.multiple_of(c * KB, KB), KB), :] - top)
        total = total + fold(jnp.sum, weights)
        low_weights = weights.astype(bf16)
        values = v_ref[pl.ds(start, KB), :]
        new_accs = []
        for p, acc in enumerate(accs):
            lanes, place = pair_slices(p)
            new_accs.append(acc + dot(values[:, lanes], low_weights[:, place], TN))
        return total, tuple(new_accs)

    zeros = tuple(jnp.zeros((2 * HD, 2 * QB), f32) for _ in range(pairs))
    total, accs = by_twos(count, second, (jnp.zeros((8, width), f32), zeros))
    total = jnp.sum(total, axis=0, keepdims=True)
    mixed = untangle([acc / total[:, pair_slices(p)[1]] for p, acc in enumerate(accs)])
    wide_ref[...] = mixed
    o_ref[...] = mixed.astype(bf16)
    lse_ref[0] = top + jnp.log(total)

    @pl.when(block == 0)
    def _():
        top_ref[0] = top

    @pl.when(block != 0)
    def _():
        top_ref[0] = jnp.maximum(top_ref[0], top)


def attend_back_kernel(
    low_ref,
    count_ref,
    key_ids_ref,
    query_ids_ref,
    q_ref,
    k_ref,
    v_ref,
    do_ref,
    o_ref,
    lse_ref,
    dq_ref,
    dk_ref,
    dv_ref,
    sums_ref,
    bias_ref,
    dk_acc,
    dv_acc,
):
    pair, block = pl.program_id(0), pl.program_id(1)
    low, count = low_ref[block], count_ref[block]

    @pl.when(pair == 0)
    def _():
        fill_bias(bias_ref, key_ids_ref, query_ids_ref, block, low, count)

    @pl.when(block == 0)
    def _():
        dk_acc[...] = jnp.zeros_like(dk_acc)
        dv_acc[...] = jnp.zeros_like(dv_acc)

    queries = by_head(q_ref[...] * jnp.asarray(SCALE, bf16))
    grads = by_head(do_ref[...])
    product = (do_ref[...].astype(f32) * o_ref[...]).T
    inner = jnp.concatenate(
        [jnp.sum(product[i * HD : (i + 1) * HD], axis=0, keepdims=True) for i in range(HEADS)], axis=1
    )
    log_sum = lse_ref[0]
    pairs = HEADS // 2

    def step(c, accs):
        start = pl.multiple_of(low + c * KB, 128)
        keys = k_ref[pl.ds(start, KB), :]
        bias = bias_ref[block, pl.ds(pl.multiple_of(c * KB, KB), KB), :]
        scores = dot(keys, queries, NT) + widen(bias)
        probs = jnp.exp(scores - log_sum)
        prob_grad = dot(v_ref[pl.ds(start, KB), :], grads, NT)
        score_grad = (probs * (prob_grad - inner)).astype(bf16)
        dv_acc[pl.ds(start, KB), :] += dot(probs.astype(bf16), grads, NN)
        dk_acc[pl.ds(start, KB), :] += dot(score_grad, queries, NN)
        new_accs = []
        for p, acc in enumerate(accs):
            lanes, place = pair_slices(p)
            new_accs.append(acc + dot(keys[:, lanes], score_grad[:, place], TN))
        return tuple(new_accs)

    zeros = tuple(jnp.zeros((2 * HD, 2 * QB), f32) for _ in range(pairs))
    dq = (untangle(lax.fori_loop(0, count, step, zeros)) * SCALE).astype(bf16)
    dq_ref[...] = dq
    dq_sum = jnp.sum(dq.astype(f32), axis=0, keepdims=True)

    @pl.when(block == 0)
    def _():
        sums_ref[0:1, :] = dq_sum

    @pl.when(block != 0)
    def _():
        sums_ref[0:1, :] += dq_sum

    @pl.when(block == pl.num_programs(1) - 1)
    def _():
        dk_ref[...] = dk_acc[...].astype(bf16)
        dv = dv_acc[...].astype(bf16)
        dv_ref[...] = dv
        sums_ref[1:2, :] = jnp.sum(dv.astype(f32), axis=0, keepdims=True)


def key_ranges(own_ids, near_ids, blocks):
    rows, near = own_ids.shape[0], near_ids.shape[0]
    size = rows // blocks
    place = jnp.arange(near, dtype=jnp.int32)[None, :]
    first = own_ids[0::size][:, None]
    last = own_ids[size - 1 :: size][:, None]
    low = jnp.min(jnp.where(near_ids[None, :] == first, place, near), axis=1)
    high = jnp.max(jnp.where(near_ids[None, :] == last, place, -1), axis=1) + 1
    low = low // 128 * 128
    count = (high - low + KB - 1) // KB
    low = jnp.minimum(low, near - count * KB)
    return low.astype(jnp.int32), count.astype(jnp.int32)


def attention_specs(rows, near, blocks):
    groups = H // HEADS
    span = HEADS * HD
    most = -(-(QB + 2 * RIM + 127) // KB) * KB
    assert most <= near and rows % QB == 0 and near % 128 == 0
    own = pl.BlockSpec((QB, span), lambda p, b, *_: (b, p))
    base = [
        pl.BlockSpec((near, 1), lambda p, b, *_: (0, 0)),
        pl.BlockSpec((1, QB), lambda p, b, *_: (0, b)),
        own,
        pl.BlockSpec((near, span), lambda p, b, *_: (0, p)),
        pl.BlockSpec((near, span), lambda p, b, *_: (0, p + groups)),
    ]
    row = pl.BlockSpec((1, 1, HEADS * QB), lambda p, b, *_: (p, 0, b))
    bias = pltpu.VMEM((blocks, most, QB), f32)
    return groups, own, base, row, bias


def attend(ranges, key_ids, query_ids, queries, near_kv):
    rows, near = queries.shape[0], near_kv.shape[0]
    blocks = rows // QB
    groups, own, base, row, bias = attention_specs(rows, near, blocks)
    top = pl.BlockSpec((1, 1, HEADS * QB), lambda p, b, *_: (p, 0, 0))
    return pl.pallas_call(
        attend_kernel,
        grid_spec=pltpu.PrefetchScalarGridSpec(
            num_scalar_prefetch=2,
            grid=(groups, blocks),
            in_specs=base,
            out_specs=[own, own, row, top],
            scratch_shapes=[bias, pltpu.VMEM((bias.shape[1], HEADS * QB), f32)],
        ),
        out_shape=[
            jax.ShapeDtypeStruct(queries.shape, bf16),
            jax.ShapeDtypeStruct(queries.shape, f32),
            jax.ShapeDtypeStruct((groups, 1, HEADS * rows), f32),
            jax.ShapeDtypeStruct((groups, 1, HEADS * QB), f32),
        ],
        compiler_params=pltpu.CompilerParams(vmem_limit_bytes=56 << 20),
        cost_estimate=cost(rows * H * HD * 850 * 16),
        name="attend",
    )(*ranges, key_ids, query_ids, queries, near_kv, near_kv)


def attend_back(ranges, key_ids, query_ids, queries, near_kv, mixed_grad, mixed, log_sums):
    rows, near = queries.shape[0], near_kv.shape[0]
    blocks = rows // QB
    groups, own, base, row, bias = attention_specs(rows, near, blocks)
    wide = pl.BlockSpec((near, HEADS * HD), lambda p, b, *_: (0, p))
    return pl.pallas_call(
        attend_back_kernel,
        grid_spec=pltpu.PrefetchScalarGridSpec(
            num_scalar_prefetch=2,
            grid=(groups, blocks),
            in_specs=base + [own, own, row],
            out_specs=[own, wide, wide, pl.BlockSpec((2, HEADS * HD), lambda p, b, *_: (0, p))],
            scratch_shapes=[bias, pltpu.VMEM((near, HEADS * HD), f32), pltpu.VMEM((near, HEADS * HD), f32)],
        ),
        out_shape=[
            jax.ShapeDtypeStruct(queries.shape, bf16),
            jax.ShapeDtypeStruct((near, queries.shape[1]), bf16),
            jax.ShapeDtypeStruct((near, queries.shape[1]), bf16),
            jax.ShapeDtypeStruct((2, queries.shape[1]), f32),
        ],
        compiler_params=pltpu.CompilerParams(vmem_limit_bytes=56 << 20),
        cost_estimate=cost(rows * H * HD * 850 * 32),
        name="attend_back",
    )(*ranges, key_ids, query_ids, queries, near_kv, near_kv, mixed_grad, mixed, log_sums)


def spot_of(place, half):
    spot, bit = 0, half
    while bit:
        spot = spot + (place & 1) * bit
        place, bit = place >> 1, bit >> 1
    return spot


def mlp_kernel(
    a_ref, dz_ref, x_ref, rb_ref, eb_ref, we_ref, wr_ref,
    y_ref, da_ref, ebg_ref, sum_ref,
    act_ref, du_ref, rg_ref, eg_ref, sems,
):
    j = pl.program_id(0)
    rows, width = a_ref.shape
    tile = 256

    def copies(step):
        d, r, _ = rg_ref.shape
        g, e, _ = eg_ref.shape
        fold = pl.num_programs(0)
        return (
            pltpu.make_async_copy(rg_ref, sum_ref.at[pl.ds(step * d, d), pl.ds(0, r), :], sems.at[0]),
            pltpu.make_async_copy(eg_ref, sum_ref.at[:, pl.ds(r + step * e, e), :], sems.at[1]),
        )

    @pl.when(j == 0)
    def _():
        y_ref[...] = x_ref[...] + rb_ref[...]
        da_ref[...] = jnp.zeros_like(da_ref)

    ebg_ref[...] = jnp.zeros_like(ebg_ref)

    def by_rows(r, carry):
        at = pl.ds(pl.multiple_of(r * tile, tile), tile)
        we = we_ref[...].reshape(width, width)
        wr = wr_ref[...].reshape(width, width)
        hidden = dot(a_ref[at, :], we, NN) + eb_ref[...]
        back = dot(dz_ref[at, :], wr, NT)
        sigma = jax.nn.sigmoid(GELU_COEF * hidden)
        act = (hidden * sigma).astype(bf16)
        act_ref[at, :] = act
        du = (back * (sigma + GELU_COEF * hidden * sigma * (1.0 - sigma))).astype(bf16)
        du_ref[at, :] = du
        ebg_ref[...] += jnp.sum(du.astype(f32), axis=0, keepdims=True)
        y_ref[at, :] += dot(act, wr, NN)
        da_ref[at, :] += dot(du, we, NT)
        return carry

    lax.fori_loop(0, rows // tile, by_rows, 0)

    @pl.when(j > 0)
    def _():
        for copy in copies(j - 1):
            copy.wait()

    def by_columns(t, carry):
        at = pl.ds(pl.multiple_of(t * tile, tile), tile)
        rg = dot(act_ref[:, at], dz_ref[...], TN).astype(bf16)
        n = tile // rg_ref.shape[1]
        rg_ref[pl.ds(t * n, n)] = rg.reshape(n, rg_ref.shape[1], width)
        eg = dot(a_ref[:, at], du_ref[...], TN).astype(bf16)
        n = tile // eg_ref.shape[1]
        eg_ref[pl.ds(t * n, n)] = eg.reshape(n, eg_ref.shape[1], width)
        return carry

    lax.fori_loop(0, width // tile, by_columns, 0)
    for copy in copies(j):
        copy.start()

    @pl.when(j == pl.num_programs(0) - 1)
    def _():
        for copy in copies(j):
            copy.wait()


def mlp(normed, branch_grad, middle, bias_reduce, bias_expand, packed, sum_rows):
    rows, width = normed.shape
    ff = bias_expand.shape[1]
    fold = ff // width
    groups = packed.shape[0]
    each = width // groups
    whole = lambda j: (0, 0)
    one = pl.Buffered(1)
    return pl.pallas_call(
        mlp_kernel,
        grid=(fold,),
        in_specs=[
            pl.BlockSpec((rows, width), whole, pipeline_mode=one),
            pl.BlockSpec((rows, width), whole, pipeline_mode=one),
            pl.BlockSpec((rows, width), whole, pipeline_mode=one),
            pl.BlockSpec((1, width), whole),
            pl.BlockSpec((1, width), lambda j: (0, j)),
            pl.BlockSpec((groups, each, width), lambda j: (0, fold + j, 0)),
            pl.BlockSpec((groups // fold, fold * each, width), lambda j: (j, 0, 0)),
        ],
        out_specs=[
            pl.BlockSpec((rows, width), whole),
            pl.BlockSpec((rows, width), whole),
            pl.BlockSpec((1, width), lambda j: (0, j)),
            pl.BlockSpec(memory_space=pl.ANY),
        ],
        out_shape=[
            jax.ShapeDtypeStruct((rows, width), f32),
            jax.ShapeDtypeStruct((rows, width), f32),
            jax.ShapeDtypeStruct((1, ff), f32),
            jax.ShapeDtypeStruct((groups, sum_rows, width), bf16),
        ],
        scratch_shapes=[
            pltpu.VMEM((rows, width), bf16),
            pltpu.VMEM((rows, width), bf16),
            pltpu.VMEM((groups // fold, fold * each, width), bf16),
            pltpu.VMEM((groups, each, width), bf16),
            pltpu.SemaphoreType.DMA((2,)),
        ],
        compiler_params=pltpu.CompilerParams(vmem_limit_bytes=58 << 20),
        cost_estimate=cost(12 * rows * width * ff),
        name="mlp",
    )(normed, branch_grad, middle, bias_reduce, bias_expand, packed, packed)


def middle_back_kernel(
    me_ref, da_ref, x_ref, og_ref, gain_ref, mixed_ref, wo_ref,
    grad_ref, mg_ref, keep_ref, send_ref, sums_ref, ag_ref,
):
    i = pl.program_id(0)
    tile, width = da_ref.shape
    steps = pl.num_programs(0) // 2
    half, each, _ = keep_ref.shape

    @pl.when(i == 0)
    def _():
        sums_ref[...] = jnp.zeros_like(sums_ref)

    @pl.when(i < steps)
    def _():
        normal, inv_std = norm_stats(x_ref[...])
        da = da_ref[...]
        grad = og_ref[...] + norm_back(da, gain_ref[...], normal, inv_std)
        grad_ref[...] = grad
        low = grad.astype(bf16)
        ag_ref[pl.ds(pl.multiple_of(i * tile, tile), tile), :] = low
        mg_ref[...] = dot(low, wo_ref[...].reshape(width, width), NT).astype(bf16)
        sums_ref[0:1, :] += jnp.sum(low.astype(f32), axis=0, keepdims=True)
        sums_ref[1:2, :] += jnp.sum(da * normal, axis=0, keepdims=True)
        sums_ref[2:3, :] += jnp.sum(da, axis=0, keepdims=True)

    @pl.when(i >= steps)
    def _():
        t = i - steps
        size = width // steps
        at = pl.ds(pl.multiple_of(t * size, size), size)
        out = dot(mixed_ref[:, at], ag_ref[...], TN).astype(bf16)
        n = size // each
        for k in range(n):
            spot = spot_of((t * n + k) ^ me_ref[0], half)
            block = out[k * each : (k + 1) * each]

            @pl.when(spot < half)
            def _():
                keep_ref[spot] = block

            @pl.when(spot >= half)
            def _():
                send_ref[spot - half] = block


def middle_back(normed_grad, middle, out_grad, gain, mixed, packed, last, place):
    rows, width = middle.shape
    groups = packed.shape[0]
    each = width // groups
    tile = rows // 4
    whole = lambda i, *_: (0, 0)
    by_rows = pl.BlockSpec((tile, width), lambda i, *_: (jnp.minimum(i, 3), 0))
    side = pl.BlockSpec((groups // 2, each, width), lambda i, *_: (0, 0, 0))
    half = jax.ShapeDtypeStruct((groups // 2, each, width), bf16)
    return pl.pallas_call(
        middle_back_kernel,
        grid_spec=pltpu.PrefetchScalarGridSpec(
            num_scalar_prefetch=1,
            grid=(8,),
            in_specs=[
                by_rows,
                by_rows,
                by_rows,
                pl.BlockSpec((1, width), whole),
                pl.BlockSpec((rows, width), whole),
                pl.BlockSpec((groups, each, width), lambda i, *_: (0, last, 0)),
            ],
            out_specs=[by_rows, by_rows, side, side, pl.BlockSpec((3, width), whole)],
            scratch_shapes=[pltpu.VMEM((rows, width), bf16)],
        ),
        out_shape=[
            jax.ShapeDtypeStruct((rows, width), f32),
            jax.ShapeDtypeStruct((rows, width), bf16),
            half,
            half,
            jax.ShapeDtypeStruct((3, width), f32),
        ],
        compiler_params=pltpu.CompilerParams(vmem_limit_bytes=56 << 20),
        cost_estimate=cost(4 * rows * width * width),
        name="middle_back",
    )(place, normed_grad, middle, out_grad, gain, mixed, packed)


def middle_kernel(mixed_ref, wo_ref, x_ref, bo_ref, gain_ref, bias_ref, out_ref, low_ref):
    width = x_ref.shape[1]
    middle = x_ref[...] + dot(mixed_ref[...], wo_ref[...].reshape(width, width), NN) + bo_ref[...]
    out_ref[...] = middle
    low_ref[...] = (norm_stats(middle)[0] * gain_ref[...] + bias_ref[...]).astype(bf16)


def middle_forward(mixed, packed, tokens, bias_output, gain, bias, last):
    rows, width = tokens.shape
    groups = packed.shape[0]
    by_rows = pl.BlockSpec((rows // 4, width), lambda i: (i, 0))
    vector = pl.BlockSpec((1, width), lambda i: (0, 0))
    return pl.pallas_call(
        middle_kernel,
        grid=(4,),
        in_specs=[
            by_rows,
            pl.BlockSpec((groups, width // groups, width), lambda i: (0, last, 0)),
            by_rows,
            vector,
            vector,
            vector,
        ],
        out_specs=[by_rows, by_rows],
        out_shape=[jax.ShapeDtypeStruct((rows, width), f32), jax.ShapeDtypeStruct((rows, width), bf16)],
        compiler_params=pltpu.CompilerParams(vmem_limit_bytes=56 << 20),
        cost_estimate=cost(2 * rows * width * width),
        name="middle",
    )(mixed, packed, tokens, bias_output, gain, bias)


def assemble(me, parts, w_ref):
    each, half = parts[0].shape[1:]
    for core, (left, right) in enumerate(((parts[0], parts[2]), (parts[1], parts[3]))):
        for spot in range(16):
            high, low, z8, z16 = spot >> 3 & 1, spot >> 2 & 1, spot >> 1 & 1, spot & 1
            z = z8 * 8 + z16 * 16 + core
            for ref, owner, lanes in (
                (left, z + high * 4 + low * 2, slice(0, half)),
                (right, z + high * 2 + low * 4, slice(half, 2 * half)),
            ):
                w_ref[pl.ds(pl.multiple_of((owner ^ me) * each, each), each), lanes] = ref[spot]


def part_specs(width):
    each = width // 32
    return [pl.BlockSpec((16, each, width // 2), lambda j, *_: (0, j, 0)) for _ in range(4)]


def qkv_kernel(me_ref, a_ref, p0, p1, p2, p3, bias_ref, q_ref, kv_ref, w_ref):
    j = pl.program_id(0)
    assemble(me_ref[0], (p0, p1, p2, p3), w_ref)
    near, width = a_ref.shape
    rows = q_ref.shape[0]
    rim = (near - rows) // 2

    @pl.when(j == 0)
    def _():
        def step(t, carry):
            source = pl.ds(pl.multiple_of(rim + t * 256, 8), 256)
            w = w_ref[...]
            q_ref[pl.ds(pl.multiple_of(t * 256, 256), 256), :] = (
                dot(a_ref[source, :], w, NN) + bias_ref[...]
            ).astype(bf16)
            return carry

        lax.fori_loop(0, rows // 256, step, 0)

    @pl.when(j > 0)
    def _():
        size = near // 8

        def step(t, carry):
            at = pl.ds(pl.multiple_of(t * size, 16), size)
            w = w_ref[...]
            kv_ref[at, :] = (dot(a_ref[at, :], w, NN) + bias_ref[...]).astype(bf16)
            return carry

        lax.fori_loop(0, near // size, step, 0)


def project(normed_near, parts, biases, rows, place):
    near, width = normed_near.shape
    return pl.pallas_call(
        qkv_kernel,
        grid_spec=pltpu.PrefetchScalarGridSpec(
            num_scalar_prefetch=1,
            grid=(3,),
            in_specs=[pl.BlockSpec((near, width), lambda j, *_: (0, 0))]
            + part_specs(width)
            + [pl.BlockSpec((1, width), lambda j, *_: (0, j))],
            out_specs=[
                pl.BlockSpec((rows, width), lambda j, *_: (0, 0)),
                pl.BlockSpec((near, width), lambda j, *_: (0, jnp.maximum(j - 1, 0))),
            ],
            scratch_shapes=[pltpu.VMEM((width, width), bf16)],
        ),
        out_shape=[
            jax.ShapeDtypeStruct((rows, width), bf16),
            jax.ShapeDtypeStruct((near, 2 * width), bf16),
        ],
        compiler_params=pltpu.CompilerParams(vmem_limit_bytes=56 << 20),
        cost_estimate=cost(2 * width * width * (rows + 2 * near)),
        name="qkv",
    )(place, normed_near, *parts, biases)


def qkv_grads_kernel(me_ref, a_ref, dq_ref, dk_hbm, dv_hbm, keep_ref, send_ref, kv_ref, sems):
    j = pl.program_id(0)
    near, width = a_ref.shape
    rows = dq_ref.shape[0]
    rim = (near - rows) // 2
    tile = 256
    half, each, _ = keep_ref.shape
    n = tile // each

    def fill(grad_ref, source):
        def step(t, carry):
            at = pl.ds(pl.multiple_of(t * tile, tile), tile)
            out = dot(a_ref[source, at], grad_ref[...], TN).astype(bf16)
            for i in range(n):
                spot = spot_of((t * n + i) ^ me_ref[0], half)
                block = out[i * each : (i + 1) * each]

                @pl.when(spot < half)
                def _():
                    keep_ref[spot] = block

                @pl.when(spot >= half)
                def _():
                    send_ref[spot - half] = block

            return carry

        lax.fori_loop(0, width // tile, step, 0)

    loads = [pltpu.make_async_copy(ref, kv_ref.at[i], sems.at[i]) for i, ref in enumerate((dk_hbm, dv_hbm))]

    @pl.when(j == 0)
    def _():
        for load in loads:
            load.start()
        fill(dq_ref, slice(rim, rim + rows))

    @pl.when(j == 1)
    def _():
        loads[0].wait()

    @pl.when(j == 2)
    def _():
        loads[1].wait()

    @pl.when(j > 0)
    def _():
        fill(kv_ref.at[j - 1], slice(0, near))


def qkv_grads(normed_near, query_grad, key_near, value_near, groups, place):
    near, width = normed_near.shape
    rows = query_grad.shape[0]
    each = width // groups
    whole = lambda j, *_: (0, 0)
    half = jax.ShapeDtypeStruct((groups // 2, 3 * each, width), bf16)
    out = pl.BlockSpec((groups // 2, each, width), lambda j, *_: (0, j, 0))
    return pl.pallas_call(
        qkv_grads_kernel,
        grid_spec=pltpu.PrefetchScalarGridSpec(
            num_scalar_prefetch=1,
            grid=(3,),
            in_specs=[
                pl.BlockSpec((near, width), whole),
                pl.BlockSpec((rows, width), whole),
                pl.BlockSpec(memory_space=pl.ANY),
                pl.BlockSpec(memory_space=pl.ANY),
            ],
            out_specs=[out, out],
            scratch_shapes=[
                pltpu.VMEM((2, near, width), bf16),
                pltpu.SemaphoreType.DMA((2,)),
            ],
        ),
        out_shape=[half, half],
        compiler_params=pltpu.CompilerParams(vmem_limit_bytes=56 << 20),
        cost_estimate=cost(2 * width * width * (rows + 2 * near)),
        name="qkv_grads",
    )(place, normed_near, query_grad, key_near, value_near)


def plus(a, b):
    return (a.astype(f32) + b.astype(f32)).astype(bf16)


def swap(value, bit):
    peers = lax.axis_size("dev")
    return lax.ppermute(value, "dev", [(i, i ^ bit) for i in range(peers)])


def merge(totals, bits, *beside):
    others = [swap(totals, bit) for bit in bits]
    out = lax.optimization_barrier((*beside, *others))
    beside, others = out[: len(beside)], out[len(beside) :]
    for other in others:
        totals = jnp.concatenate([totals[:-1] + other[:-1], jnp.maximum(totals[-1:], other[-1:])], axis=0)
    return totals, *beside


class Halving:
    def __init__(self, first, second):
        def split(pair):
            return [v.reshape((2, 2, 4) + v.shape[1:]) for v in pair]

        (keep, other), (keep_o, other_o) = split(first), split(second)
        half = (keep.shape[3] + keep_o.shape[3]) // 2

        def side_a(at):
            return plus(keep[at][..., :half, :], other[at][..., :half, :])

        def side_b(at):
            return jnp.concatenate(
                [plus(keep[at][..., half:, :], other[at][..., half:, :]), plus(keep_o[at], other_o[at])], axis=-2
            )

        self.sides = side_a(1), side_b((slice(None), 1))
        self.keeps = lambda: (side_a(0), side_b((slice(None), 0)))

    def start(self, *after):
        to_x, to_y, *after = lax.optimization_barrier((*self.sides, *after))
        self.others = swap(to_x, 2), swap(to_y, 4)
        return after

    def finish(self, totals, *beside):
        (from_x, from_y), (keep_x, keep_y) = self.others, self.keeps()
        to_y, to_x = plus(keep_x[1], from_x[1]), plus(keep_y[1], from_y[1])
        to_x, to_y, totals = lax.optimization_barrier((to_x, to_y, totals))
        second_y, second_x = swap(to_y, 4), swap(to_x, 2)
        totals, second_y, second_x = merge(totals, (1,), second_y, second_x)
        keep_x = plus(keep_x[0], from_x[0])
        keep_y = plus(keep_y[0], from_y[0])
        send = jnp.concatenate([plus(keep_x[2:], second_y[2:]), plus(keep_y[2:], second_x[2:])], axis=1)
        send, totals = lax.optimization_barrier((send, totals))
        low = swap(send, 8)
        totals, low, *beside = merge(totals, (2, 4, 6), low, *beside)
        keep = jnp.concatenate([plus(keep_x[:2], second_y[:2]), plus(keep_y[:2], second_x[:2])], axis=1)
        send, totals = lax.optimization_barrier((plus(keep[1], low[1]), totals))
        last = swap(send, 16)
        totals, last = merge(totals, (8, 16, 24), last)
        return plus(keep[0], low[0]).astype(f32) + last.astype(f32), totals, *beside


def plain(pairs, part):
    groups = 2 * pairs[0][0].shape[0]
    order = [int(f"{i:05b}"[::-1], 2) for i in range(groups)]
    joined = jnp.concatenate([jnp.concatenate(pair, axis=0) for pair in pairs], axis=1)
    joined = jnp.stack([joined[i] for i in order])
    return scatter(joined, [part] * (joined.shape[1] * groups // joined.shape[2])).astype(f32)


def normed_grad_kernel(
    me_ref, dq_ref, dk_hbm, dv_hbm, p0, p1, p2, p3, normal_hbm, nb_hbm, na_hbm,
    own_ref, before_ref, after_ref, sums_ref,
    acc_ref, kv_ref, normal_ref, nb_ref, na_ref, sems, w_ref,
):
    j = pl.program_id(0)
    assemble(me_ref[0], (p0, p1, p2, p3), w_ref)
    rows, width = own_ref.shape
    rim = before_ref.shape[0]
    near = 2 * rim + rows
    pairs = (
        (dk_hbm, kv_ref.at[0]),
        (dv_hbm, kv_ref.at[1]),
        (normal_hbm, normal_ref),
        (nb_hbm.at[pl.ds(0, rim)], nb_ref),
        (na_hbm.at[pl.ds(0, rim)], na_ref),
    )
    loads = [pltpu.make_async_copy(source, target, sems.at[i]) for i, (source, target) in enumerate(pairs)]

    @pl.when(j == 0)
    def _():
        for load in loads:
            load.start()
        acc_ref[:rim, :] = jnp.zeros((rim, width), f32)
        acc_ref[rim + rows :, :] = jnp.zeros((rim, width), f32)

        def step(t, carry):
            grads = dq_ref[pl.ds(pl.multiple_of(t * 256, 256), 256), :]
            acc_ref[pl.ds(pl.multiple_of(rim + t * 256, 8), 256), :] = dot(grads, w_ref[...], NT)
            return carry

        lax.fori_loop(0, rows // 256, step, 0)

    @pl.when(j == 1)
    def _():
        loads[0].wait()

    @pl.when(j == 2)
    def _():
        for load in loads[1:]:
            load.wait()

    @pl.when(j > 0)
    def _():
        size = near // 8

        def step(t, carry):
            at = pl.ds(pl.multiple_of(t * size, 8), size)
            acc_ref[at, :] += dot(kv_ref[j - 1, at, :], w_ref[...], NT)
            return carry

        lax.fori_loop(0, near // size, step, 0)

    @pl.when(j == 2)
    def _():
        def finish(base, normal, out, carry):
            def step(t, carry):
                gain_sum, bias_sum = carry
                at = pl.multiple_of(t * 16, 16)
                value = acc_ref[pl.ds(pl.multiple_of(base + at, 8), 16), :]
                product = value * normal[pl.ds(at, 16), :].astype(f32)
                out[pl.ds(at, 16), :] = value.astype(out.dtype)
                return gain_sum + product[:8] + product[8:], bias_sum + value[:8] + value[8:]

            return lax.fori_loop(0, out.shape[0] // 16, step, carry)

        carry = (jnp.zeros((8, width), f32), jnp.zeros((8, width), f32))
        carry = finish(0, nb_ref, before_ref, carry)
        carry = finish(rim + rows, na_ref, after_ref, carry)
        gain_sum, bias_sum = finish(rim, normal_ref, own_ref, carry)
        sums_ref[0:1, :] = jnp.sum(gain_sum, axis=0, keepdims=True)
        sums_ref[1:2, :] = jnp.sum(bias_sum, axis=0, keepdims=True)


def project_back(query_grad, key_near, value_near, parts, normal, before, after, place):
    rows, width = query_grad.shape
    near = key_near.shape[0]
    rim = (near - rows) // 2
    whole = lambda j, *_: (0, 0)
    anywhere = pl.BlockSpec(memory_space=pl.ANY)
    return pl.pallas_call(
        normed_grad_kernel,
        grid_spec=pltpu.PrefetchScalarGridSpec(
            num_scalar_prefetch=1,
            grid=(3,),
            in_specs=[pl.BlockSpec((rows, width), whole, pipeline_mode=pl.Buffered(1)), anywhere, anywhere]
            + part_specs(width)
            + [anywhere, anywhere, anywhere],
            out_specs=[
                pl.BlockSpec((rows, width), whole),
                pl.BlockSpec((rim, width), whole),
                pl.BlockSpec((rim, width), whole),
                pl.BlockSpec((2, width), whole),
            ],
            scratch_shapes=[
                pltpu.VMEM((near, width), f32),
                pltpu.VMEM((2, near, width), bf16),
                pltpu.VMEM((rows, width), f32),
                pltpu.VMEM((rim, width), bf16),
                pltpu.VMEM((rim, width), bf16),
                pltpu.SemaphoreType.DMA((5,)),
                pltpu.VMEM((width, width), bf16),
            ],
        ),
        out_shape=[
            jax.ShapeDtypeStruct((rows, width), f32),
            jax.ShapeDtypeStruct((rim, width), bf16),
            jax.ShapeDtypeStruct((rim, width), bf16),
            jax.ShapeDtypeStruct((2, width), f32),
        ],
        compiler_params=pltpu.CompilerParams(vmem_limit_bytes=58 << 20),
        cost_estimate=cost(2 * width * width * (rows + 2 * near)),
        name="normed_grad",
    )(place, query_grad, key_near, value_near, *parts, normal, before, after)


def gather(value, segments, groups):
    peers = lax.axis_size("dev")
    rows, width = value.shape
    whole = lax.all_gather(value, "dev", axis=0, tiled=True)
    sub = peers // groups
    if sub == 1:
        return whole.reshape(groups, rows, width)
    whole = whole.reshape(groups, sub, rows, width)
    parts, at = [], 0
    for size in segments:
        parts.append(whole[:, :, at : at + size].reshape(groups, sub * size, width))
        at += size
    return jnp.concatenate(parts, axis=1)


def scatter(value, segments):
    peers = lax.axis_size("dev")
    groups, rows, width = value.shape
    sub = peers // groups
    if sub > 1:
        parts, at = [], 0
        for size in segments:
            cut = value[:, at : at + sub * size]
            parts.append(cut.reshape(groups, sub, size, width))
            at += sub * size
        value = jnp.concatenate(parts, axis=2)
    value = value.reshape(peers * sum(segments), width)
    return lax.psum_scatter(value, "dev", scatter_dimension=0, tiled=True)


def pack_kernel(me_ref, q_ref, k_ref, v_ref, small_ref, r_ref, e_ref, o_ref, eb_ref, one_ref, two_ref):
    part, width = q_ref.shape
    for i, ref in enumerate((q_ref, k_ref, v_ref)):
        one_ref[i * part : (i + 1) * part, :] = ref[...].astype(bf16)

    def place(value, size):
        index = lax.broadcasted_iota(jnp.int32, value.shape, 0) * width
        index = index + lax.broadcasted_iota(jnp.int32, value.shape, 1)
        return jnp.where(index // size == me_ref[0], value, jnp.zeros_like(value))

    row = lax.broadcasted_iota(jnp.int32, (part, width), 0)
    column = lax.broadcasted_iota(jnp.int32, (part, width), 1)
    pick = jnp.where(column - me_ref[0] * part == row, 1.0, 0.0).astype(bf16)
    one_ref[3 * part :, :] = dot(small_ref[...].astype(bf16), pick, NN).astype(bf16)
    rows = r_ref.shape[0]
    fold = rows // part
    two_ref[:rows, :] = r_ref[...].astype(bf16)
    for i in range(fold):
        at = rows + i * part
        two_ref[at : at + part, :] = e_ref[:, i * width : (i + 1) * width].astype(bf16)
    at = rows + fold * part
    two_ref[at : at + part, :] = o_ref[...].astype(bf16)
    bias = jnp.concatenate([eb_ref[...]] * (width // eb_ref.shape[1]), axis=1)
    two_ref[at + part :, :] = place(jnp.broadcast_to(bias, (8, width)), fold * part).astype(bf16)


def pack(me, mats, smalls, reduce_mat, expand_mat, output_mat, expand_bias):
    part, width = output_mat.shape
    tiled = jnp.stack(smalls)
    bias = expand_bias[None]
    rows = reduce_mat.shape[0]
    return pl.pallas_call(
        pack_kernel,
        grid_spec=pltpu.PrefetchScalarGridSpec(
            num_scalar_prefetch=1,
            grid=(1,),
            in_specs=[
                pl.BlockSpec(v.shape, lambda i, *_: (0, 0))
                for v in (*mats, tiled, reduce_mat, expand_mat, output_mat, bias)
            ],
            out_specs=[
                pl.BlockSpec((3 * part + 8, width), lambda i, *_: (0, 0)),
                pl.BlockSpec((2 * rows + part + 8, width), lambda i, *_: (0, 0)),
            ],
        ),
        out_shape=[
            jax.ShapeDtypeStruct((3 * part + 8, width), bf16),
            jax.ShapeDtypeStruct((2 * rows + part + 8, width), bf16),
        ],
        name="pack",
    )(jnp.full((1,), me, jnp.int32), *mats, tiled, reduce_mat, expand_mat, output_mat, bias)


def doubling(value, tokens, packed, exchange, prepare):
    rows, width = value.shape
    half = width // 2
    grown = value[None]
    grown = jnp.concatenate([grown, swap(grown, 16)])
    grown, tokens = lax.optimization_barrier((grown, tokens))
    other = swap(grown, 8)
    near = exchange(tokens)
    grown, other, packed, *near = lax.optimization_barrier((grown, other, packed, *near))
    a = jnp.concatenate([grown[..., :half], other[..., :half]])
    b = jnp.concatenate([grown[..., half:], other[..., half:]])
    from_x, from_y = swap(a, 2), swap(b, 4)
    a, b = jnp.concatenate([a, from_x]), jnp.concatenate([b, from_y])
    from_y, from_x = swap(a, 4), swap(b, 2)
    prepared = prepare(*near)
    a, b = jnp.concatenate([a, from_y]), jnp.concatenate([b, from_x])
    a, b, *prepared = lax.optimization_barrier((a, b, *prepared))
    return (a, swap(a, 1), b, swap(b, 1)), prepared, packed


def fold_smalls(natural, sub):
    at = natural.shape[1] - 8 * sub
    tail = natural[:, at:].reshape(natural.shape[0], sub, 8, natural.shape[2])
    tail = jnp.sum(tail.astype(f32), axis=1).astype(natural.dtype)
    return jnp.concatenate([natural[:, :at], tail], axis=1)


def as_doubled(natural):
    half = natural.shape[2] // 2
    out = []
    for cut, orders in ((slice(0, half), (4, 2)), (slice(half, None), (2, 4))):
        for core in (0, 1):
            picks = []
            for spot in range(16):
                high, low, z8, z16 = spot >> 3 & 1, spot >> 2 & 1, spot >> 1 & 1, spot & 1
                picks.append(natural[z8 * 8 + z16 * 16 + core + high * orders[0] + low * orders[1], :, cut])
            out.append(jnp.stack(picks))
    return tuple(out)


def spread(vector, width):
    peers, me = lax.axis_size("dev"), lax.axis_index("dev")
    size = vector.shape[0]
    place = jnp.arange(peers * size, dtype=jnp.int32) // size
    full = jnp.where(place == me, jnp.tile(vector, peers), jnp.zeros((), vector.dtype))
    return full.reshape(-1, width)


def local(
    tokens_in,
    attn_gain,
    attn_bias,
    query_mat,
    query_bias,
    key_mat,
    value_mat,
    value_bias,
    output_mat,
    output_bias,
    mlp_gain,
    mlp_bias,
    expand_mat,
    expand_bias,
    reduce_mat,
    reduce_bias,
    image_ids,
    clip_flags,
    out_grad,
):
    peers, me = lax.axis_size("dev"), lax.axis_index("dev")
    rows, width = tokens_in.shape
    part = query_mat.shape[0]
    ff = expand_mat.shape[1]
    fold = ff // width
    groups = min(peers, 32)
    sub = peers // groups

    paired = peers == 32
    up = [(i, i + 1) for i in range(peers - 1)]
    down = [(i + 1, i) for i in range(peers - 1)]
    own_ids = image_ids + 1
    smalls = (attn_gain, attn_bias, query_bias, value_bias, output_bias, mlp_gain, mlp_bias, reduce_bias)

    def ids_of(halo):
        return (halo[RIM, :RIM].astype(f32) * 32 + halo[RIM + 1, :RIM].astype(f32)).astype(jnp.int32)

    def exchange(tokens):
        normal_one, inv_one = norm_stats(tokens)
        normal_low = normal_one.astype(bf16)

        def with_ids(at):
            ids = jnp.pad(own_ids[at], (0, width - RIM))
            ids = [(ids // 32).astype(bf16)[None], (ids % 32).astype(bf16)[None]]
            return jnp.concatenate([normal_low[at], *ids, jnp.zeros((6, width), bf16)])

        before = lax.ppermute(with_ids(slice(rows - RIM, rows)), "dev", up)
        after = lax.ppermute(with_ids(slice(0, RIM)), "dev", down)
        return before, after, normal_one, inv_one

    def prepare(before, after, normal_one, inv_one):
        near_ids = jnp.concatenate([ids_of(before), own_ids, ids_of(after)])
        ranges = key_ranges(own_ids, near_ids, rows // QB)
        return before, after, near_ids, near_ids[:, None], own_ids[None, :], *ranges, normal_one, inv_one

    if paired:
        packed_one, packed_two = pack(
            me, (query_mat, key_mat, value_mat), smalls, reduce_mat, expand_mat, output_mat, expand_bias
        )
        first, prepared, packed_two = doubling(packed_one, tokens_in, packed_two, exchange, prepare)
        second = gather(packed_two, (), groups)
    else:
        low = [v.astype(bf16) for v in (query_mat, key_mat, value_mat)]
        packed_one = jnp.concatenate(low + [spread(v.astype(bf16), width) for v in smalls])
        first = as_doubled(fold_smalls(gather(packed_one, [part] * 3 + [8], groups), sub))
        prepared = prepare(*exchange(tokens_in))
        expand_low = expand_mat.astype(bf16)
        packed_two = jnp.concatenate(
            [reduce_mat.astype(bf16)]
            + [expand_low[:, i * width : (i + 1) * width] for i in range(fold)]
            + [output_mat.astype(bf16), spread(expand_bias.astype(bf16), width), jnp.zeros((8 - fold, width), bf16)]
        )
        second = gather(packed_two, [fold * part] + [part] * (fold + 1) + [8], groups)

    before, after, near_ids, key_ids, query_ids, *ranges, normal_one, inv_one = prepared
    vectors = jnp.concatenate(
        [
            sum(jnp.sum(v[:, 3 * width // groups :].astype(f32), axis=0) for v in first[i : i + 2])
            for i in (0, 2)
        ],
        axis=1,
    )
    (gain_one, bias_one, bias_query, bias_value, bias_output, gain_two, bias_two, bias_reduce) = [
        vectors[i : i + 1] for i in range(8)
    ]

    normed_near = jnp.concatenate(
        [(v.astype(f32) * gain_one + bias_one).astype(bf16) for v in (before[:RIM], normal_one, after[:RIM])],
        axis=0,
    )
    bias_qkv = jnp.concatenate([bias_query, jnp.zeros_like(bias_value), bias_value], axis=1)
    place = jnp.full((1,), me if paired else 0, jnp.int32)
    queries, near_kv = project(normed_near, first, bias_qkv, rows, place)
    mixed, mixed_wide, log_sums, tops = attend(ranges, key_ids, query_ids, queries, near_kv)
    head_top = jnp.max(tops.reshape(H, QB), axis=1)

    tail = second[:, (2 * fold + 1) * part * sub :].reshape(groups * sub, 8, width)
    bias_expand = jnp.sum(tail.astype(f32), axis=0)[:fold].reshape(1, ff)
    middle, normed_two = middle_forward(mixed, second, tokens_in, bias_output, gain_two, bias_two, 2 * fold)
    branch_grad = out_grad.astype(bf16)
    block_out, normed_two_grad, expand_bias_grad, sums = mlp(
        normed_two, branch_grad, middle, bias_reduce, bias_expand, second, 2 * fold * width // groups + 8
    )
    reduce_bias_grad = column_sums(branch_grad)
    first_sum = scatter(sums, [fold * part] + [part] * fold + [8 // sub])
    middle_grad, mixed_grad, *out_halves, middle_sums = middle_back(
        normed_two_grad, middle, out_grad, gain_two, mixed, second, 2 * fold, place
    )
    out_other = swap(out_halves[1], 1) if peers == 32 else None
    rest = jnp.concatenate(
        [
            middle_sums,
            reduce_bias_grad[None],
            expand_bias_grad.reshape(fold, width),
            jnp.pad(head_top, (0, width - H))[None],
        ]
    )
    mixed_grad, rest = lax.optimization_barrier((mixed_grad, rest))
    query_grad, key_near, value_near, bias_sums = attend_back(
        ranges, key_ids, query_ids, queries, near_kv, mixed_grad, mixed_wide, log_sums
    )
    halves = qkv_grads(normed_near, query_grad, key_near, value_near, groups, place)
    if paired:
        late = Halving((halves[0], swap(halves[1], 1)), (out_halves[0], out_other))
        query_grad, key_near, value_near = late.start(query_grad, key_near, value_near)
    normed_grad, to_prev, to_next, norm_sums = project_back(
        query_grad, key_near, value_near, first, normal_one, before, after, place
    )
    from_next = lax.ppermute(to_prev, "dev", down)
    from_prev = lax.ppermute(to_next, "dev", up)
    totals = jnp.concatenate([norm_sums, bias_sums, rest])
    if paired:
        second_sum, totals, from_next, from_prev = late.finish(totals, from_next, from_prev)
    else:
        second_sum = plain((halves, out_halves), part)
        bit = 1
        while bit < peers:
            (totals,) = merge(totals, (bit,))
            bit *= 2
    normed_grad = normed_grad + jnp.pad(from_prev.astype(f32), ((0, rows - RIM), (0, 0)))
    normed_grad = normed_grad + jnp.pad(from_next.astype(f32), ((rows - RIM, 0), (0, 0)))
    tokens_grad = middle_grad + norm_back(normed_grad, gain_one, normal_one, inv_one)
    mine = lax.dynamic_slice_in_dim(totals[:8], me * part, part, 1)
    expand_mine = lax.dynamic_slice_in_dim(totals[8 : 8 + fold].reshape(-1), me * part * fold, part * fold, 0)
    global_top = totals[-1, :H]

    first_sum = first_sum.astype(f32)
    expand_out = jnp.concatenate(
        [first_sum[(fold + i) * part : (fold + i + 1) * part] for i in range(fold)], axis=1
    )
    ratio = CLIP_TAU / jnp.maximum(global_top, CLIP_TAU)
    factor = jnp.where(clip_flags == 1, jnp.sqrt(ratio), 1.0)
    by_column = jnp.repeat(factor, HD)
    return (
        block_out,
        tokens_grad,
        query_mat * by_column[None, :],
        key_mat * by_column[None, :],
        mine[0],
        mine[1],
        second_sum[:part],
        mine[2],
        second_sum[part : 2 * part],
        second_sum[2 * part : 3 * part],
        mine[3],
        second_sum[3 * part :],
        mine[4],
        mine[5],
        mine[6],
        expand_out,
        expand_mine,
        first_sum[: fold * part],
        mine[7],
    )


def solution(mesh):
    split, both = P("dev"), P("dev", None)
    mat = both
    in_specs = (
        mat, split, split, mat, split, mat, mat, split, mat, split, split, split, mat, split, mat, split,
        split, P(), mat,
    )
    out_specs = (
        mat, mat, mat, mat, split, split, mat, split, mat, mat, split, mat, split, split, split, mat,
        split, mat, split,
    )
    return jax.shard_map(local, mesh=mesh, in_specs=in_specs, out_specs=out_specs, check_vma=False)
```
